256 devices in a mesh: dp: 8 (over y, core), seq: 32 (over x, z).
Axes of the slice: x: 4, y: 4, z: 8, core: 2. Of those that a mesh axis runs over, the one named last changes fastest.
Arguments:
- x_in: bfloat16 [8, 8192, 2048], P('dp', 'seq'), may hold values from -0.37 to 0.37
- b_in: bfloat16 [8, 8192, 128], P('dp', 'seq'), may hold values from -7.4 to 7.4
- c_in: bfloat16 [8, 8192, 128], P('dp', 'seq'), may hold values from -0.12988281 to 0.12988281
- dt: float32 [8, 32, 8192], P('dp', None, 'seq'), may hold values from 0.2 to 32768, as said below
- a_log: float32 [32], replicated, may hold values from -14 to -2, as said below
- skip: float32 [32], replicated, may hold values from 1 to 3
- cotangent: bfloat16 [8, 8192, 2048], P('dp', 'seq'), may hold values from -0.29882812 to 0.29882812
Outputs:
- y_out: bfloat16 [8, 8192, 2048], P('dp', 'seq')
- grad_x: bfloat16 [8, 8192, 2048], P('dp', 'seq')
- grad_b: bfloat16 [8, 8192, 128], P('dp', 'seq')
- grad_c: bfloat16 [8, 8192, 128], P('dp', 'seq')
- grad_dt: float32 [8, 32, 8192], P('dp', None, 'seq')
- grad_alog: float32 [32], replicated
- derivative_bypass: float32 [32], replicated
The draws below stay inside these ranges and needn't reach their ends.
Inputs may be any that keep to these rules, and one draw needn't show every extreme that they name: `dt`: positive step sizes. Each head's decay rate exp(a_log) is positive.
All inputs are finite; a program needn't handle non-finite values.
Results may differ from the reference program's by a relative error of at most 0.018.
Values sent between devices are 32-bit elements; how exact they have to be, the bound alone decides.
No kernel may reach another device: no remote copies, remote signals or barrier semaphores. Data moves between devices by JAX's collectives and lax.ppermute only.
A program may use at most 128 MiB of HBM per device.

```python
import jax
import jax.numpy as jnp
from jax import lax

H = 32
P_SIZE = 64
N = 128
GROUP = 256
TOK_DEV = 256
SEQLEN = 8192
BATCH = 8
HP = 2048


def decay_rates(key):
    base_key = jax.random.fold_in(key, 11)
    pick_key, slow_key, fast_key = jax.random.split(base_key, 3)
    slow_share = 0.5
    slow_mask = jax.random.uniform(pick_key, (H,), jnp.float32) < slow_share
    slow_rate = jax.random.uniform(slow_key, (H,), jnp.float32, 0.2, 0.8) / SEQLEN
    fast_rate = jnp.exp(jax.random.uniform(fast_key, (H,), jnp.float32, -1.204, 0.0)) / TOK_DEV
    return jnp.where(slow_mask, slow_rate, fast_rate)


def device_levels(key):
    level_key = jax.random.fold_in(key, 37)
    return jnp.exp(jax.random.uniform(level_key, (BATCH, SEQLEN // TOK_DEV, 1, 1), jnp.float32, -2.5, 0.2))


def loud_field(key, offset_number, width, spread):
    field_key = jax.random.fold_in(key, offset_number)
    field_shape = (BATCH, SEQLEN // TOK_DEV, TOK_DEV, width)
    entries = jax.random.truncated_normal(field_key, -6.0, 6.0, field_shape, jnp.float32)
    shaped = entries * spread * device_levels(key)
    return shaped.reshape(BATCH, SEQLEN, width).astype(jnp.bfloat16)


def draw_x_in(key, part):
    return loud_field(key, 41, HP, 0.05)


def draw_b_in(key, part):
    return loud_field(key, 43, N, 1.0)


def draw_a_log(key, part):
    return jnp.log(decay_rates(key))


def draw_dt(key, part):
    speed_numbers = decay_rates(key)
    step_key = jax.random.fold_in(key, 23)
    rough_key, plateau_key, spot_key, loss_key = jax.random.split(step_key, 4)
    roughness = jnp.exp(jax.random.uniform(rough_key, (BATCH, H, SEQLEN), jnp.float32, -0.693, 0.693))
    level_count = SEQLEN // TOK_DEV
    plateau = jnp.exp(jax.random.uniform(plateau_key, (BATCH, 1, level_count, 1), jnp.float32, -0.7, 0.7))
    plateau = jnp.broadcast_to(plateau, (BATCH, H, level_count, TOK_DEV)).reshape(BATCH, H, SEQLEN)
    point_offsets = jax.random.randint(spot_key, (BATCH, 2), 0, SEQLEN)
    objective_numbers = jax.random.uniform(loss_key, (BATCH, 2), jnp.float32, 0.22, 0.69)
    location_numbers = jnp.arange(SEQLEN)[None, :]
    segment_extent = jnp.where(location_numbers == point_offsets[:, 0:1], objective_numbers[:, 0:1], jnp.where(location_numbers == point_offsets[:, 1:2], objective_numbers[:, 1:2], 0.0))
    equilibrium_memory = roughness * plateau
    return jnp.where(segment_extent[:, None, :] > 0.0, segment_extent[:, None, :] / speed_numbers[None, :, None], equilibrium_memory)


def steps_of(own_key, extent, cuts, low, top_value):
    def one(position, blocks):
        heights = jax.random.uniform(jax.random.fold_in(jax.random.fold_in(own_key, 6), position), (blocks,), jnp.float32, low / len(cuts), top_value / len(cuts))
        return jnp.repeat(jnp.exp(heights), extent[position] // blocks).reshape((-1,) + (1,) * (len(extent) - position - 1))

    factor_of = one(*cuts[0])
    for cut in cuts[1:]:
        factor_of = factor_of * one(*cut)
    return factor_of


def noise(key, dims, deviation, limit, pieces=(), kind=jnp.bfloat16):
    level = steps_of(key, dims, pieces, -0.22, 0.18) if pieces else 1.0
    values = jax.random.normal(key, dims, jnp.float32) * deviation * level
    return jnp.minimum(jnp.maximum(values, -limit), limit).astype(kind)


def setup_inputs(seed: int = 0) -> dict:
    streams_of = jax.random.split(jax.random.key(seed), 8)
    return {
        "x_in": draw_x_in(jax.random.fold_in(streams_of[7], 71), 0),
        "b_in": draw_b_in(jax.random.fold_in(streams_of[7], 71), 0),
        "c_in": noise(streams_of[2], (BATCH, SEQLEN, N), 0.022, 0.12988281, ((0, 8), (1, 32))),
        "dt": draw_dt(jax.random.fold_in(streams_of[7], 71), 0),
        "a_log": draw_a_log(jax.random.fold_in(streams_of[7], 71), 0),
        "skip": jnp.clip(jax.random.uniform(streams_of[5], (H,), jnp.float32, 1.0, 3.0), 1.0, 3.0),
        "cotangent": noise(streams_of[6], (BATCH, SEQLEN, HP), 0.05, 0.29882812, ((0, 8), (1, 32))),
    }


def piece_state(x_block, b_block, log_decay):
    span = x_block.shape[0]
    head_count = log_decay.shape[0]
    feat_width = x_block.shape[1]
    head_size = feat_width // head_count
    cum_log = jnp.cumsum(log_decay, axis=1)
    to_end = jnp.exp(cum_log[:, -1:] - cum_log)
    scaled = (x_block.reshape(span, head_count, head_size).astype(jnp.float32) * to_end.T[:, :, None]).astype(jnp.bfloat16)
    block_state = lax.dot_general(scaled.reshape(span, feat_width), b_block, (((0,), (0,)), ((), ())), preferred_element_type=jnp.float32)
    return (jnp.exp(cum_log[:, -1]), block_state.reshape(head_count, head_size, b_block.shape[1]))

def piece_out(x_block, b_block, c_block, log_decay, skip_gain, state_in):
    span = x_block.shape[0]
    head_count = log_decay.shape[0]
    feat_width = x_block.shape[1]
    head_size = feat_width // head_count
    cum_log = jnp.cumsum(log_decay, axis=1)
    inner_cb = jnp.dot(c_block, b_block.T, preferred_element_type=jnp.float32)
    row_ids = lax.broadcasted_iota(jnp.int32, (span, span), 0)
    col_ids = lax.broadcasted_iota(jnp.int32, (span, span), 1)
    lower = (row_ids >= col_ids)[None]
    differ = jnp.where(lower, cum_log[:, :, None] - cum_log[:, None, :], 0.0)
    weights = jnp.where(lower, inner_cb[None] * jnp.exp(differ), 0.0).astype(jnp.bfloat16)
    x_heads = x_block.reshape(span, head_count, head_size)
    inner = jnp.einsum('htu,uhp->thp', weights.astype(jnp.float32), x_heads.astype(jnp.float32))
    state_low = state_in.astype(jnp.bfloat16)
    carried = jnp.einsum('tn,hpn->thp', c_block.astype(jnp.float32), state_low.astype(jnp.float32))
    carried = carried * jnp.exp(cum_log).T[:, :, None]
    result = inner + carried + skip_gain[None, :, None] * x_heads.astype(jnp.float32)
    return result.reshape(span, feat_width)

def reference(x_in, b_in, c_in, dt, a_log, skip, cotangent):
    block_count = SEQLEN // GROUP

    def forward(x_all, b_all, c_all, dt_all, a_param, skip_param):
        la_all = -jnp.exp(a_param)[None, :, None] * dt_all

        def one_sequence(fragments):
            x_seq, b_seq, c_seq, la_seq = fragments
            x_blocks = x_seq.reshape(block_count, GROUP, H * P_SIZE)
            b_blocks = b_seq.reshape(block_count, GROUP, N)
            c_blocks = c_seq.reshape(block_count, GROUP, N)
            la_blocks = la_seq.reshape(H, block_count, GROUP).transpose(1, 0, 2)

            def advance(state_now, piece):
                x_block, b_block, c_block, log_decay = piece
                y_block = piece_out(x_block, b_block, c_block, log_decay, skip_param, state_now)
                gain, block_state = piece_state(x_block, b_block, log_decay)
                return (gain[:, None, None] * state_now + block_state, y_block)
            start = jnp.zeros((H, P_SIZE, N), jnp.float32)
            _, outputs = lax.scan(jax.checkpoint(advance), start, (x_blocks, b_blocks, c_blocks, la_blocks))
            return outputs.reshape(SEQLEN, H * P_SIZE)
        return lax.map(one_sequence, (x_all, b_all, c_all, la_all))
    y_full, pull_back = jax.vjp(forward, x_in, b_in, c_in, dt, a_log, skip)
    grad_x, grad_b, grad_c, grad_dt, grad_alog, derivative_bypass = pull_back(cotangent.astype(jnp.float32))
    return (y_full.astype(jnp.bfloat16), grad_x, grad_b, grad_c, grad_dt, grad_alog, derivative_bypass)
```

```python
import jax
import jax.numpy as jnp
from jax import lax
from jax.experimental import pallas as pl
from jax.experimental.pallas import tpu as pltpu
from jax.sharding import PartitionSpec as P

GROUP = 256
HEADS = 32
SIZE = 64
STATE = 128
STEP = 8
WIDE = STEP * SIZE
GRID = HEADS // STEP
HALF = HEADS // 2
HALF_STEPS = GRID // 2
ROWS = SIZE + 8

F32 = jnp.float32
BF16 = jnp.bfloat16
EXACT = lax.Precision.HIGHEST
VMEM_LIMIT = 60 * 1024 * 1024


def dot(a, b, ca, cb, precision=None):
    return lax.dot_general(
        a, b, (((ca,), (cb,)), ((), ())), precision=precision, preferred_element_type=F32
    )


def iota(shape, dim):
    return lax.broadcasted_iota(jnp.int32, shape, dim)


def triangle():
    shape = (GROUP, GROUP)
    return jnp.where(iota(shape, 0) <= iota(shape, 1), 1.0, 0.0).astype(F32)


def column(row):
    shape = (HEADS, HEADS)
    eye = iota(shape, 0) == iota(shape, 1)
    return jnp.sum(jnp.where(eye, jnp.broadcast_to(row, shape), 0.0), axis=1, keepdims=True)


def as_row(col):
    shape = (HEADS, HEADS)
    eye = iota(shape, 0) == iota(shape, 1)
    return jnp.sum(jnp.where(eye, jnp.broadcast_to(col, shape), 0.0), axis=0, keepdims=True)


def spread(rows):
    return jnp.concatenate(
        [jnp.broadcast_to(rows[j : j + 1], (SIZE, GROUP)) for j in range(STEP)], axis=0
    )


def per_head(full):
    return jnp.concatenate(
        [
            jnp.sum(full[j * SIZE : (j + 1) * SIZE], axis=0, keepdims=True)
            for j in range(STEP)
        ],
        axis=0,
    )


def head_rows(step):
    return pl.ds(pl.multiple_of(step * STEP, STEP), STEP)


def keeps_adjoint(step):
    even = lax.rem(lax.axis_index("seq"), 2) == 0
    return even == (step < HALF_STEPS)


def unpaired(step):
    place = lax.axis_index("seq")
    edge = (place == 0) | (place == lax.axis_size("seq") - 1)
    return jnp.where(edge & (step >= HALF_STEPS), 0.0, 1.0).astype(F32)


def store_half(step, low_ref, high_ref, head, value):
    @pl.when(step < HALF_STEPS)
    def _():
        low_ref[head] = value

    @pl.when(step >= HALF_STEPS)
    def _():
        high_ref[head] = value


def states_kernel(
    x_ref, g_ref, b_ref, c_ref, dt_ref, alog_ref,
    low_ref, high_ref, keep_ref, xt_ref, gt_ref, cum_ref,
):
    step = pl.program_id(0)

    @pl.when(step == 0)
    def _():
        rate = jnp.exp(column(alog_ref[...]))
        cum_ref[...] = dot(-rate * dt_ref[...], triangle(), 1, 0, EXACT)

    cum = cum_ref[head_rows(step), :]
    last = cum[:, GROUP - 1 :]
    to_end = jnp.exp(last - cum)
    from_start = jnp.exp(cum)
    gain = jnp.exp(last)
    xt = x_ref[...].T
    gt = g_ref[...].T
    xt_ref[...] = xt
    gt_ref[...] = gt
    scaled = (xt.astype(F32) * spread(to_end)).astype(BF16)
    raised = (gt.astype(F32) * spread(from_start)).astype(BF16)
    state = dot(scaled, b_ref[...], 1, 0)
    adjoint = dot(raised, c_ref[...], 1, 0)
    first = keeps_adjoint(step)
    paired = unpaired(step)
    send = jnp.where(first, state, adjoint) * paired
    keep = jnp.where(first, adjoint, state)
    for j in range(STEP):
        store_half(step, low_ref, high_ref, j, send[j * SIZE : (j + 1) * SIZE])
        keep_ref[j, :SIZE, :] = keep[j * SIZE : (j + 1) * SIZE]
        keep_ref[j, SIZE:, :] = jnp.broadcast_to(gain[j : j + 1], (8, STATE))


def of_half(step, low_ref, high_ref, head):
    return jnp.where(step < HALF_STEPS, low_ref[head], high_ref[head])


def join_kernel(keep_ref, low_ref, high_ref, out_ref):
    step = pl.program_id(0)
    for j in range(STEP):
        other = of_half(step, low_ref, high_ref, j)
        out_ref[j, :SIZE, :] = keep_ref[j, :SIZE, :] + keep_ref[j, SIZE : SIZE + 1, :] * other
        out_ref[j, SIZE:, :] = keep_ref[j, SIZE:, :]


def scan_kernel(part_ref, out_ref):
    count = part_ref.shape[0]
    low = lax.axis_index("seq") < HALF

    def matrix(k):
        return part_ref[k, :SIZE, :]

    def gain(k):
        return part_ref[k, SIZE : SIZE + 1, :]

    def pair(first, second, carried, mine):
        return gain(first) * gain(second) * carried + matrix(mine)

    nothing = jnp.zeros((SIZE, STATE), F32)

    @pl.when(low)
    def _():
        state = nothing
        for k in range(0, count, 2):
            out_ref[k] = state
            state = pair(k, k + 1, state, k + 1)
        adjoint = nothing
        for k in reversed(range(0, count, 2)):
            out_ref[k + 1] = adjoint
            adjoint = pair(k, k + 1, adjoint, k)

    @pl.when(jnp.logical_not(low))
    def _():
        state = matrix(0)
        for k in range(1, count - 1, 2):
            out_ref[k] = state
            state = pair(k, k + 1, state, k + 1)
        out_ref[count - 1] = state
        adjoint = matrix(count - 1)
        for k in reversed(range(1, count - 1, 2)):
            out_ref[k + 1] = adjoint
            adjoint = pair(k, k + 1, adjoint, k)
        out_ref[0] = adjoint


def pass_on_kernel(mine_ref, low_ref, high_ref, cum_ref, out_low_ref, out_high_ref):
    step = pl.program_id(0)
    gain = jnp.exp(cum_ref[head_rows(step), :][:, GROUP - 1 :]) * unpaired(step)
    for j in range(STEP):
        sent = of_half(step, low_ref, high_ref, j)
        store_half(step, out_low_ref, out_high_ref, j, sent + gain[j : j + 1] * mine_ref[j])


def inner_kernel(
    g_ref, xt_ref, gt_ref, b_ref, c_ref, cum_ref, skip_ref,
    y_ref, gx_ref, row_ref, skiprow_ref, gb_ref, gc_ref,
    cb_s, acc_s,
):
    step = pl.program_id(0)
    half = GROUP // 2

    @pl.when(step == 0)
    def _():
        cb_s[...] = dot(c_ref[...], b_ref[...], 1, 1)
        acc_s[...] = jnp.zeros_like(acc_s)

    cum = cum_ref[head_rows(step), :]
    cum_t = cum.T
    square = (half, half)
    lower = iota(square, 0) >= iota(square, 1)
    nothing = jnp.zeros((SIZE, GROUP), BF16)
    for j in range(STEP):
        low, high = j * SIZE, (j + 1) * SIZE
        early, late = cum[j : j + 1, :half], cum[j : j + 1, half:]
        start, end = cum_t[:half, j : j + 1], cum_t[half:, j : j + 1]
        e00 = jnp.where(lower, jnp.exp(start - early), 0.0)
        e10 = jnp.exp(end - early)
        e11 = jnp.where(lower, jnp.exp(end - late), 0.0)
        w00 = (cb_s[:half, :half] * e00).astype(BF16)
        w10 = (cb_s[half:, :half] * e10).astype(BF16)
        w11 = (cb_s[half:, half:] * e11).astype(BF16)
        weights = jnp.concatenate(
            [
                jnp.concatenate([w00, jnp.zeros(square, BF16)], axis=1),
                jnp.concatenate([w10, w11], axis=1),
            ],
            axis=0,
        )
        xt = xt_ref[low:high, :]
        gt = gt_ref[low:high, :]
        yt = dot(xt, weights, 1, 1)
        gxt = dot(gt, weights, 1, 0)
        pair = (j // 2) * 2 * SIZE
        two = [xt, nothing] if j % 2 == 0 else [nothing, xt]
        gw = dot(g_ref[:, pair : pair + 2 * SIZE], jnp.concatenate(two, axis=0), 1, 0)
        acc_s[:half, :half] += gw[:half, :half] * e00
        acc_s[half:, :half] += gw[half:, :half] * e10
        acc_s[half:, half:] += gw[half:, half:] * e11
        xf = xt.astype(F32)
        gf = gt.astype(F32)
        row_ref[pl.ds(step * STEP + j, 1), :] = jnp.sum(gf * yt - xf * gxt, axis=0, keepdims=True)
        skiprow_ref[pl.ds(step * STEP + j, 1), :] = jnp.sum(gf * xf, axis=0, keepdims=True)
        skip = skip_ref[step * STEP + j]
        y_ref[low:high, :] = (yt + skip * xf).astype(BF16)
        gx_ref[low:high, :] = (gxt + skip * gf).astype(BF16)

    @pl.when(step == GRID - 1)
    def _():
        acc = acc_s[...].astype(BF16)
        gc_ref[...] = dot(acc, b_ref[...], 1, 0)
        gb_ref[...] = dot(acc, c_ref[...], 0, 0)


def outer_kernel(
    yt_ref, gxt_ref, xt_ref, gt_ref, mine_ref, low_ref, high_ref, b_ref, c_ref, cum_ref, row_ref, skiprow_ref,
    gbi_ref, gci_ref, dt_ref, alog_ref,
    y_ref, gx_ref, gb_ref, gc_ref, gdt_ref, sums_ref,
    row_s, gbt_s, gct_s,
):
    step = pl.program_id(0)

    @pl.when(step == 0)
    def _():
        gbt_s[...] = jnp.zeros_like(gbt_s)
        gct_s[...] = jnp.zeros_like(gct_s)

    cum = cum_ref[head_rows(step), :]
    last = cum[:, GROUP - 1 :]
    to_end = jnp.exp(last - cum)
    from_start = jnp.exp(cum)
    gain = jnp.exp(last)
    mine = jnp.concatenate([mine_ref[j] for j in range(STEP)], axis=0)
    other = jnp.concatenate([of_half(step, low_ref, high_ref, j) for j in range(STEP)], axis=0)
    first = keeps_adjoint(step)
    state_f = jnp.where(first, mine, other)
    adjoint_f = jnp.where(first, other, mine)
    product = state_f * adjoint_f
    product = jnp.concatenate(
        [
            jnp.sum(product[j * SIZE : (j + 1) * SIZE], axis=0, keepdims=True)
            for j in range(STEP)
        ],
        axis=0,
    )
    overlap = jnp.sum(product, axis=1, keepdims=True)
    state = state_f.astype(BF16)
    adjoint = adjoint_f.astype(BF16)
    xf = xt_ref[...].astype(F32)
    gf = gt_ref[...].astype(F32)
    start_w = spread(from_start)
    end_w = spread(to_end)
    carried = dot(state, c_ref[...], 1, 1) * start_w
    gscaled = dot(adjoint, b_ref[...], 1, 1) * end_w
    y_ref[...] = (yt_ref[...].astype(F32) + carried).astype(BF16).T
    gx_ref[...] = (gxt_ref[...].astype(F32) + gscaled).astype(BF16).T
    from_x = per_head(xf * gscaled)
    row = row_ref[head_rows(step), :] + per_head(gf * carried) - from_x
    glast = jnp.sum(from_x, axis=1, keepdims=True) + gain * overlap
    final = iota((STEP, GROUP), 1) == GROUP - 1
    row_s[head_rows(step), :] = row + jnp.where(final, glast, 0.0)
    gct_s[...] += dot(state, (gf * start_w).astype(BF16), 0, 0)
    gbt_s[...] += dot(adjoint, (xf * end_w).astype(BF16), 0, 0)

    @pl.when(step == GRID - 1)
    def _():
        gc_ref[...] = (gci_ref[...] + gct_s[...].T).astype(BF16)
        gb_ref[...] = (gbi_ref[...] + gbt_s[...].T).astype(BF16)
        rate = jnp.exp(column(alog_ref[...]))
        gla = dot(row_s[...], triangle(), 1, 1, EXACT)
        gdt = -rate * gla
        gdt_ref[...] = gdt
        alog = jnp.sum(gdt * dt_ref[...], axis=1, keepdims=True)
        skip = jnp.sum(skiprow_ref[...], axis=1, keepdims=True)
        sums_ref[...] = jnp.concatenate(
            [as_row(alog), as_row(skip), jnp.zeros((1, STATE - 2 * HEADS), F32)], axis=1
        )


def whole(shape):
    return pl.BlockSpec(shape, lambda i: (0,) * len(shape))


def shape_of(shape, dtype=F32):
    return jax.ShapeDtypeStruct(shape, dtype)


WIDE_T = pl.BlockSpec((WIDE, GROUP), lambda i: (i, 0))
WIDE_N = pl.BlockSpec((GROUP, WIDE), lambda i: (0, i))
STEP_SPEC = pl.BlockSpec((STEP, SIZE, STATE), lambda i: (i, 0, 0))
KEEP_SPEC = pl.BlockSpec((STEP, ROWS, STATE), lambda i: (i, 0, 0))
LOW_SPEC = pl.BlockSpec((STEP, SIZE, STATE), lambda i: (jnp.minimum(i, HALF_STEPS - 1), 0, 0))
HIGH_SPEC = pl.BlockSpec((STEP, SIZE, STATE), lambda i: (jnp.maximum(i - HALF_STEPS, 0), 0, 0))


def params(semantics=("arbitrary",)):
    return pltpu.CompilerParams(
        dimension_semantics=semantics, vmem_limit_bytes=VMEM_LIMIT
    )


def swap(low, high):
    count = lax.axis_size("seq")
    low_pairs = [(i, i ^ 1) for i in range(count)]
    high_pairs = [(i, ((i - 1 ^ 1) + 1) % count) for i in range(1, count)] + [(0, count - 1)]
    return lax.ppermute(low, "seq", low_pairs), lax.ppermute(high, "seq", high_pairs)


def shards(x_in, b_in, c_in, dt, a_log, skip, cotangent):
    x, b, c, g, steps = x_in[0], b_in[0], c_in[0], cotangent[0], dt[0]
    alog = a_log[None]
    feat = HEADS * SIZE
    narrow = whole((GROUP, STATE))
    heads = whole((HEADS, GROUP))
    row_spec = whole((1, HEADS))
    half = shape_of((HALF, SIZE, STATE))
    low, high, keep, xt, gt, cum = pl.pallas_call(
        states_kernel,
        grid=(GRID,),
        in_specs=[WIDE_N, WIDE_N, narrow, narrow, heads, row_spec],
        out_specs=[LOW_SPEC, HIGH_SPEC, KEEP_SPEC, WIDE_T, WIDE_T, heads],
        out_shape=[
            half,
            half,
            shape_of((HEADS, ROWS, STATE)),
            shape_of((feat, GROUP), BF16),
            shape_of((feat, GROUP), BF16),
            shape_of((HEADS, GROUP)),
        ],
        compiler_params=params(),
        name="states",
    )(x, g, b, c, steps, alog)
    low_in, high_in = swap(low, high)
    yt, gxt, row, skiprow, gbi, gci = pl.pallas_call(
        inner_kernel,
        grid=(GRID,),
        in_specs=[
            WIDE_N, WIDE_T, WIDE_T, narrow, narrow, heads,
            pl.BlockSpec(memory_space=pltpu.SMEM),
        ],
        out_specs=[WIDE_T, WIDE_T, heads, heads, narrow, narrow],
        out_shape=[
            shape_of((feat, GROUP), BF16),
            shape_of((feat, GROUP), BF16),
            shape_of((HEADS, GROUP)),
            shape_of((HEADS, GROUP)),
            shape_of((GROUP, STATE)),
            shape_of((GROUP, STATE)),
        ],
        scratch_shapes=[pltpu.VMEM((GROUP, GROUP), F32), pltpu.VMEM((GROUP, GROUP), F32)],
        compiler_params=params(),
        cost_estimate=pl.CostEstimate(
            flops=6 * HEADS * GROUP * GROUP * GROUP, bytes_accessed=5 << 20, transcendentals=2 << 20
        ),
        name="inner",
    )(g, xt, gt, b, c, cum, skip)
    joined = pl.pallas_call(
        join_kernel,
        grid=(GRID,),
        in_specs=[KEEP_SPEC, LOW_SPEC, HIGH_SPEC],
        out_specs=KEEP_SPEC,
        out_shape=shape_of((HEADS, ROWS, STATE)),
        compiler_params=params(),
        name="join",
    )(keep, low_in, high_in)
    parts = lax.all_to_all(joined, "seq", 0, 0, tiled=True)
    scanned = pl.pallas_call(
        scan_kernel,
        out_shape=shape_of((HEADS, SIZE, STATE)),
        compiler_params=params(None),
        name="scan",
    )(parts)
    mine = lax.all_to_all(scanned, "seq", 0, 0, tiled=True)
    low_out, high_out = pl.pallas_call(
        pass_on_kernel,
        grid=(GRID,),
        in_specs=[STEP_SPEC, LOW_SPEC, HIGH_SPEC, heads],
        out_specs=[LOW_SPEC, HIGH_SPEC],
        out_shape=[half, half],
        compiler_params=params(),
        name="pass_on",
    )(mine, low, high, cum)
    low_back, high_back = swap(low_out, high_out)
    y, gx, gb, gc, gdt, sums = pl.pallas_call(
        outer_kernel,
        grid=(GRID,),
        in_specs=[
            WIDE_T, WIDE_T, WIDE_T, WIDE_T, STEP_SPEC, LOW_SPEC, HIGH_SPEC,
            narrow, narrow, heads, heads, heads, narrow, narrow, heads, row_spec,
        ],
        out_specs=[WIDE_N, WIDE_N, narrow, narrow, heads, whole((1, STATE))],
        out_shape=[
            shape_of((GROUP, feat), BF16),
            shape_of((GROUP, feat), BF16),
            shape_of((GROUP, STATE), BF16),
            shape_of((GROUP, STATE), BF16),
            shape_of((HEADS, GROUP)),
            shape_of((1, STATE)),
        ],
        scratch_shapes=[
            pltpu.VMEM((HEADS, GROUP), F32),
            pltpu.VMEM((STATE, GROUP), F32),
            pltpu.VMEM((STATE, GROUP), F32),
        ],
        compiler_params=params(),
        name="outer",
    )(yt, gxt, xt, gt, mine, low_back, high_back, b, c, cum, row, skiprow, gbi, gci, steps, alog)
    everyone = lax.axis_size("dp") * lax.axis_size("seq")
    copies = jnp.broadcast_to(sums[None], (everyone, 1, STATE))
    total = jnp.sum(
        lax.all_to_all(copies, ("dp", "seq"), 0, 0, tiled=True), axis=(0, 1)
    )
    return (
        y[None], gx[None], gb[None], gc[None], gdt[None],
        total[:HEADS], total[HEADS : 2 * HEADS],
    )


def solution(mesh):
    placed = (
        P("dp", "seq", None),
        P("dp", "seq", None),
        P("dp", "seq", None),
        P("dp", None, "seq"),
        P(),
        P(),
        P("dp", "seq", None),
    )
    return jax.shard_map(
        shards,
        mesh=mesh,
        in_specs=placed,
        out_specs=(
            P("dp", "seq", None),
            P("dp", "seq", None),
            P("dp", "seq", None),
            P("dp", "seq", None),
            P("dp", None, "seq"),
            P(),
            P(),
        ),
        check_vma=False,
    )
```

```python
import jax
import jax.numpy as jnp
from jax import lax
from jax.experimental import pallas as pl
from jax.experimental.pallas import tpu as pltpu
from jax.sharding import PartitionSpec as P

GROUP = 256
HEADS = 32
SIZE = 64
STATE = 128
STEP = 8
WIDE = STEP * SIZE
GRID = HEADS // STEP
HALF = HEADS // 2
HALF_STEPS = GRID // 2

F32 = jnp.float32
BF16 = jnp.bfloat16
EXACT = lax.Precision.HIGHEST
VMEM_LIMIT = 24 * 1024 * 1024


def dot(a, b, ca, cb, precision=None):
    return lax.dot_general(
        a, b, (((ca,), (cb,)), ((), ())), precision=precision, preferred_element_type=F32
    )


def iota(shape, dim):
    return lax.broadcasted_iota(jnp.int32, shape, dim)


def triangle():
    shape = (GROUP, GROUP)
    return jnp.where(iota(shape, 0) <= iota(shape, 1), 1.0, 0.0).astype(F32)


def column(row):
    shape = (HEADS, HEADS)
    eye = iota(shape, 0) == iota(shape, 1)
    return jnp.sum(jnp.where(eye, jnp.broadcast_to(row, shape), 0.0), axis=1, keepdims=True)


def as_row(col):
    shape = (HEADS, HEADS)
    eye = iota(shape, 0) == iota(shape, 1)
    return jnp.sum(jnp.where(eye, jnp.broadcast_to(col, shape), 0.0), axis=0, keepdims=True)


def spread(rows):
    return jnp.concatenate(
        [jnp.broadcast_to(rows[j : j + 1], (SIZE, GROUP)) for j in range(STEP)], axis=0
    )


def per_head(full):
    return jnp.concatenate(
        [
            jnp.sum(full[j * SIZE : (j + 1) * SIZE], axis=0, keepdims=True)
            for j in range(STEP)
        ],
        axis=0,
    )


def head_rows(step):
    return pl.ds(pl.multiple_of(step * STEP, STEP), STEP)


def keeps_adjoint(step):
    even = lax.rem(lax.axis_index("seq"), 2) == 0
    return even == (step < HALF_STEPS)


def unpaired(step):
    place = lax.axis_index("seq")
    edge = (place == 0) | (place == lax.axis_size("seq") - 1)
    return jnp.where(edge & (step >= HALF_STEPS), 0.0, 1.0).astype(F32)


def states_kernel(
    x_hbm, g_hbm, b_hbm, c_hbm, dt_hbm, alog_hbm,
    low_ref, high_ref, keep_ref, gain_ref, xt_ref, gt_ref, cum_ref,
    x_s, g_s, b_s, c_s, dt_s, alog_s, sems,
):
    def copy(source, target, slot):
        made = pltpu.make_async_copy(source, target, sems.at[slot])
        made.start()
        return made

    alog_copy = copy(alog_hbm, alog_s, 0)
    dt_copy = copy(dt_hbm, dt_s, 1)
    b_copy = copy(b_hbm, b_s, 2)
    c_copy = copy(c_hbm, c_s, 3)
    inputs = []
    for i in range(GRID):
        lanes = pl.ds(i * WIDE, WIDE)
        inputs.append(
            (
                copy(x_hbm.at[:, lanes], x_s.at[i], 4 + 2 * i),
                copy(g_hbm.at[:, lanes], g_s.at[i], 5 + 2 * i),
            )
        )
    alog_copy.wait()
    dt_copy.wait()
    rate = jnp.exp(column(alog_s[...]))
    cum_all = dot(-rate * dt_s[...], triangle(), 1, 0, EXACT)
    cum_ref[...] = cum_all
    b_copy.wait()
    c_copy.wait()
    for i in range(GRID):
        for made in inputs[i]:
            made.wait()
        cum = cum_all[i * STEP : (i + 1) * STEP]
        last = cum[:, GROUP - 1 :]
        to_end = jnp.exp(last - cum)
        from_start = jnp.exp(cum)
        gain = jnp.exp(last)
        xt = x_s[i].T
        gt = g_s[i].T
        rows = pl.ds(i * WIDE, WIDE)
        xt_ref[rows, :] = xt
        gt_ref[rows, :] = gt
        scaled = (xt.astype(F32) * spread(to_end)).astype(BF16)
        raised = (gt.astype(F32) * spread(from_start)).astype(BF16)
        state = dot(scaled, b_s[...], 1, 0)
        adjoint = dot(raised, c_s[...], 1, 0)
        first = keeps_adjoint(i)
        send = jnp.where(first, state, adjoint) * unpaired(i)
        keep = jnp.where(first, adjoint, state)
        send_ref = low_ref if i < HALF_STEPS else high_ref
        base = i % HALF_STEPS * STEP
        for j in range(STEP):
            part = slice(j * SIZE, (j + 1) * SIZE)
            send_ref[base + j] = send[part]
            keep_ref[i * STEP + j] = keep[part]
            gain_ref[i * STEP + j] = jnp.broadcast_to(gain[j : j + 1], (1, STATE))


def join_kernel(keep_ref, low_ref, high_ref, cum_ref, out_ref):
    gain = jnp.exp(cum_ref[:, GROUP - 1 :])
    for h in range(HEADS):
        other = low_ref[h] if h < HALF else high_ref[h - HALF]
        out_ref[h] = keep_ref[h] + gain[h : h + 1] * other


def scan_kernel(part_ref, gain_ref, out_ref):
    count = part_ref.shape[0]
    low = lax.axis_index("seq") < HALF

    def pair(first, second, carried, mine):
        return gain_ref[first] * gain_ref[second] * carried + part_ref[mine]

    nothing = jnp.zeros((SIZE, STATE), F32)

    @pl.when(low)
    def _():
        state = nothing
        for k in range(0, count, 2):
            out_ref[k] = state
            state = pair(k, k + 1, state, k + 1)
        adjoint = nothing
        for k in reversed(range(0, count, 2)):
            out_ref[k + 1] = adjoint
            adjoint = pair(k, k + 1, adjoint, k)

    @pl.when(jnp.logical_not(low))
    def _():
        state = part_ref[0]
        for k in range(1, count - 1, 2):
            out_ref[k] = state
            state = pair(k, k + 1, state, k + 1)
        out_ref[count - 1] = state
        adjoint = part_ref[count - 1]
        for k in reversed(range(1, count - 1, 2)):
            out_ref[k + 1] = adjoint
            adjoint = pair(k, k + 1, adjoint, k)
        out_ref[0] = adjoint


def pass_on_kernel(mine_ref, low_ref, high_ref, cum_ref, out_low_ref, out_high_ref):
    gain = jnp.exp(cum_ref[:, GROUP - 1 :])
    low_gain = gain[:HALF] * unpaired(0)
    high_gain = gain[HALF:] * unpaired(GRID - 1)
    for h in range(HALF):
        out_low_ref[h] = low_ref[h] + low_gain[h : h + 1] * mine_ref[h]
        out_high_ref[h] = high_ref[h] + high_gain[h : h + 1] * mine_ref[HALF + h]


def inner_kernel(
    g_ref, xt_ref, gt_ref, b_ref, c_ref, cum_ref, skip_ref,
    y_ref, gx_ref, row_ref, skiprow_ref, gb_ref, gc_ref,
    cb_s, acc_s,
):
    half = GROUP // 2
    cb_s[...] = dot(c_ref[...], b_ref[...], 1, 1)
    acc_s[...] = jnp.zeros_like(acc_s)
    square = (half, half)
    lower = iota(square, 0) >= iota(square, 1)
    nothing = jnp.zeros((SIZE, GROUP), BF16)

    def some_heads(step, carry):
        cum = cum_ref[head_rows(step), :]
        cum_t = cum.T
        rows = []
        skips = []
        for j in range(STEP):
            early, late = cum[j : j + 1, :half], cum[j : j + 1, half:]
            start, end = cum_t[:half, j : j + 1], cum_t[half:, j : j + 1]
            e00 = jnp.where(lower, jnp.exp(start - early), 0.0)
            e10 = jnp.exp(end - early)
            e11 = jnp.where(lower, jnp.exp(end - late), 0.0)
            w00 = (cb_s[:half, :half] * e00).astype(BF16)
            w10 = (cb_s[half:, :half] * e10).astype(BF16)
            w11 = (cb_s[half:, half:] * e11).astype(BF16)
            weights = jnp.concatenate(
                [
                    jnp.concatenate([w00, jnp.zeros(square, BF16)], axis=1),
                    jnp.concatenate([w10, w11], axis=1),
                ],
                axis=0,
            )
            features = pl.ds(pl.multiple_of(step * WIDE + j * SIZE, SIZE), SIZE)
            xt = xt_ref[features, :]
            gt = gt_ref[features, :]
            yt = dot(xt, weights, 1, 1)
            gxt = dot(gt, weights, 1, 0)
            pair = pl.ds(pl.multiple_of(step * WIDE + j // 2 * 2 * SIZE, 2 * SIZE), 2 * SIZE)
            two = [xt, nothing] if j % 2 == 0 else [nothing, xt]
            gw = dot(g_ref[:, pair], jnp.concatenate(two, axis=0), 1, 0)
            acc_s[:half, :half] += gw[:half, :half] * e00
            acc_s[half:, :half] += gw[half:, :half] * e10
            acc_s[half:, half:] += gw[half:, half:] * e11
            xf = xt.astype(F32)
            gf = gt.astype(F32)
            rows.append(jnp.sum(gf * yt - xf * gxt, axis=0, keepdims=True))
            skips.append(jnp.sum(gf * xf, axis=0, keepdims=True))
            skip = skip_ref[step * STEP + j]
            y_ref[features, :] = (yt + skip * xf).astype(BF16)
            gx_ref[features, :] = (gxt + skip * gf).astype(BF16)
        row_ref[head_rows(step), :] = jnp.concatenate(rows, axis=0)
        skiprow_ref[head_rows(step), :] = jnp.concatenate(skips, axis=0)
        return carry

    lax.fori_loop(0, GRID, some_heads, 0)
    acc = acc_s[...].astype(BF16)
    gc_ref[...] = dot(acc, b_ref[...], 1, 0)
    gb_ref[...] = dot(acc, c_ref[...], 0, 0)


def halves(own):
    even = lax.rem(lax.axis_index("seq"), 2) == 0
    state_low = even == own
    state = jnp.where(state_low, 0, HALF_STEPS)
    return state_low, state, HALF_STEPS - state


def feature_rows(step):
    return pl.ds(pl.multiple_of(step * WIDE, WIDE), WIDE)


def take(ref, step):
    full = ref[pl.ds(pl.multiple_of(step * STEP, STEP), STEP)]
    return full.reshape(WIDE, STATE).astype(BF16)


def take_half(low_ref, high_ref, low, i):
    part = pl.ds(i * STEP, STEP)
    return jnp.where(low, low_ref[part], high_ref[part]).reshape(WIDE, STATE).astype(BF16)


def carried_rows(state, gt_ref, c_ref, cum_ref, step):
    from_start = jnp.exp(cum_ref[head_rows(step), :])
    gf = gt_ref[feature_rows(step), :].astype(F32)
    raw = dot(state, c_ref[...], 1, 1)
    return raw, gf, from_start, per_head(gf * raw) * from_start


def scaled_rows(adjoint, xt_ref, b_ref, cum_ref, step):
    cum = cum_ref[head_rows(step), :]
    to_end = jnp.exp(cum[:, GROUP - 1 :] - cum)
    xf = xt_ref[feature_rows(step), :].astype(F32)
    raw = dot(adjoint, b_ref[...], 1, 1)
    from_x = per_head(xf * raw) * to_end
    final = iota((STEP, GROUP), 1) == GROUP - 1
    total = jnp.sum(from_x, axis=1, keepdims=True)
    return raw, xf, to_end, jnp.where(final, total, 0.0) - from_x


def give_out(
    i, state_step, adjoint_step, state, adjoint, raws,
    yt_ref, gxt_ref, y_hbm, gx_hbm, out_s, sems, gct, gbt,
):
    raw, gf, from_start, back, xf, to_end = raws
    start_w = spread(from_start)
    end_w = spread(to_end)
    y = yt_ref[feature_rows(state_step), :].astype(F32) + raw * start_w
    out_s[2 * i] = y.astype(BF16).T
    gx = gxt_ref[feature_rows(adjoint_step), :].astype(F32) + back * end_w
    out_s[2 * i + 1] = gx.astype(BF16).T
    copies = []
    for slot, step, target in ((2 * i, state_step, y_hbm), (2 * i + 1, adjoint_step, gx_hbm)):
        lanes = pl.ds(pl.multiple_of(step * WIDE, WIDE), WIDE)
        made = pltpu.make_async_copy(out_s.at[slot], target.at[:, lanes], sems.at[slot])
        made.start()
        copies.append(made)
    gct = gct + dot(state, (gf * start_w).astype(BF16), 0, 0)
    gbt = gbt + dot(adjoint, (xf * end_w).astype(BF16), 0, 0)
    return gct, gbt, copies


def own_kernel(
    mine_ref, yt_ref, gxt_ref, xt_ref, gt_ref, b_ref, c_ref, cum_ref,
    y_hbm, gx_hbm, row_ref, gct_ref, gbt_ref,
    out_s, sems,
):
    _, state_first, adjoint_first = halves(True)
    gct = jnp.zeros((STATE, GROUP), F32)
    gbt = jnp.zeros((STATE, GROUP), F32)
    copies = []
    for i in range(HALF_STEPS):
        state_step, adjoint_step = state_first + i, adjoint_first + i
        state = take(mine_ref, state_step)
        adjoint = take(mine_ref, adjoint_step)
        raw, gf, from_start, row = carried_rows(state, gt_ref, c_ref, cum_ref, state_step)
        row_ref[head_rows(state_step), :] = row
        back, xf, to_end, row = scaled_rows(adjoint, xt_ref, b_ref, cum_ref, adjoint_step)
        row_ref[head_rows(adjoint_step), :] = row
        gct, gbt, made = give_out(
            i, state_step, adjoint_step, state, adjoint, (raw, gf, from_start, back, xf, to_end),
            yt_ref, gxt_ref, y_hbm, gx_hbm, out_s, sems, gct, gbt,
        )
        copies += made
    gct_ref[...] = gct
    gbt_ref[...] = gbt
    for made in copies:
        made.wait()


def sums_kernel(
    mine_ref, low_ref, high_ref, xt_ref, gt_ref, b_ref, c_ref, cum_ref, row_ref, own_row_ref,
    skiprow_ref, dt_ref, alog_ref,
    gdt_ref, sums_ref,
    row_s,
):
    state_low, state_first, adjoint_first = halves(False)
    for i in range(HALF_STEPS):
        state = take_half(low_ref, high_ref, state_low, i)
        adjoint = take_half(high_ref, low_ref, state_low, i)
        row_s[head_rows(state_first + i), :] = carried_rows(
            state, gt_ref, c_ref, cum_ref, state_first + i
        )[-1]
        row_s[head_rows(adjoint_first + i), :] = scaled_rows(
            adjoint, xt_ref, b_ref, cum_ref, adjoint_first + i
        )[-1]
    overlap = jnp.concatenate(
        [
            jnp.sum(mine_ref[:HALF] * low_ref[...], axis=1),
            jnp.sum(mine_ref[HALF:] * high_ref[...], axis=1),
        ],
        axis=0,
    )
    overlap = jnp.sum(overlap, axis=1, keepdims=True) * jnp.exp(cum_ref[:, GROUP - 1 :])
    final = iota((HEADS, GROUP), 1) == GROUP - 1
    row = row_ref[...] + own_row_ref[...] + row_s[...] + jnp.where(final, overlap, 0.0)
    gdt = -jnp.exp(column(alog_ref[...])) * dot(row, triangle(), 1, 1, EXACT)
    gdt_ref[...] = gdt
    alog = jnp.sum(gdt * dt_ref[...], axis=1, keepdims=True)
    skip = jnp.sum(skiprow_ref[...], axis=1, keepdims=True)
    sums = jnp.concatenate(
        [as_row(alog), as_row(skip), jnp.zeros((1, STATE - 2 * HEADS), F32)], axis=1
    )
    sums_ref[...] = jnp.broadcast_to(sums[None], sums_ref.shape)


def other_kernel(
    low_ref, high_ref, yt_ref, gxt_ref, xt_ref, gt_ref, b_ref, c_ref, cum_ref,
    gct_ref, gbt_ref, gci_ref, gbi_ref, y_in, gx_in,
    y_hbm, gx_hbm, gc_ref, gb_ref,
    out_s, sems,
):
    state_low, state_first, adjoint_first = halves(False)
    gct = gct_ref[...]
    gbt = gbt_ref[...]
    copies = []
    for i in range(HALF_STEPS):
        state_step, adjoint_step = state_first + i, adjoint_first + i
        state = take_half(low_ref, high_ref, state_low, i)
        adjoint = take_half(high_ref, low_ref, state_low, i)
        raw, gf, from_start, _ = carried_rows(state, gt_ref, c_ref, cum_ref, state_step)
        back, xf, to_end, _ = scaled_rows(adjoint, xt_ref, b_ref, cum_ref, adjoint_step)
        gct, gbt, made = give_out(
            i, state_step, adjoint_step, state, adjoint, (raw, gf, from_start, back, xf, to_end),
            yt_ref, gxt_ref, y_hbm, gx_hbm, out_s, sems, gct, gbt,
        )
        copies += made
    gc_ref[...] = (gci_ref[...] + gct.T).astype(BF16)
    gb_ref[...] = (gbi_ref[...] + gbt.T).astype(BF16)
    for made in copies:
        made.wait()


def shape_of(shape, dtype=F32):
    return jax.ShapeDtypeStruct(shape, dtype)


def call(kernel, name, out_shape, out_specs=None, cost=None, limit=VMEM_LIMIT, **more):
    if out_specs is not None:
        more["out_specs"] = out_specs
    return pl.pallas_call(
        kernel,
        out_shape=out_shape,
        compiler_params=pltpu.CompilerParams(vmem_limit_bytes=limit),
        cost_estimate=cost,
        name=name,
        **more,
    )


def cost(us):
    return pl.CostEstimate(flops=us * 500_000_000, bytes_accessed=us << 21, transcendentals=0)


def swap(low, high):
    count = lax.axis_size("seq")
    low_pairs = [(i, i ^ 1) for i in range(count)]
    high_pairs = [(i, ((i - 1 ^ 1) + 1) % count) for i in range(1, count)] + [(0, count - 1)]
    return lax.ppermute(low, "seq", low_pairs), lax.ppermute(high, "seq", high_pairs)


def shards(x_in, b_in, c_in, dt, a_log, skip, cotangent):
    x, b, c, g, steps = x_in[0], b_in[0], c_in[0], cotangent[0], dt[0]
    alog = a_log[None]
    feat = HEADS * SIZE
    vmem = pl.BlockSpec(memory_space=pltpu.VMEM)
    hbm = pl.BlockSpec(memory_space=pltpu.HBM)
    half = shape_of((HALF, SIZE, STATE))
    all_heads = shape_of((HEADS, SIZE, STATE))
    wide = shape_of((feat, GROUP), BF16)
    tall = shape_of((GROUP, feat), BF16)
    rows = shape_of((HEADS, GROUP))
    low, high, keep, gain, xt, gt, cum = call(
        states_kernel,
        "states",
        [half, half, all_heads, shape_of((HEADS, 1, STATE)), wide, wide, rows],
        in_specs=[hbm] * 6,
        scratch_shapes=[
            pltpu.VMEM((GRID, GROUP, WIDE), BF16),
            pltpu.VMEM((GRID, GROUP, WIDE), BF16),
            pltpu.VMEM((GROUP, STATE), BF16),
            pltpu.VMEM((GROUP, STATE), BF16),
            pltpu.VMEM((HEADS, GROUP), F32),
            pltpu.VMEM((1, HEADS), F32),
            pltpu.SemaphoreType.DMA((4 + 2 * GRID,)),
        ],
        limit=60 * 1024 * 1024,
    )(x, g, b, c, steps, alog)
    low_in, high_in = swap(low, high)
    gains = lax.all_to_all(gain, "seq", 0, 0, tiled=True)
    yt, gxt, row, skiprow, gbi, gci = call(
        inner_kernel,
        "inner",
        [wide, wide, rows, rows, shape_of((GROUP, STATE)), shape_of((GROUP, STATE))],
        in_specs=[vmem] * 6 + [pl.BlockSpec(memory_space=pltpu.SMEM)],
        scratch_shapes=[pltpu.VMEM((GROUP, GROUP), F32), pltpu.VMEM((GROUP, GROUP), F32)],
        cost=cost(6),
    )(g, xt, gt, b, c, cum, skip)
    low_in, high_in, gains, row = lax.optimization_barrier((low_in, high_in, gains, row))
    joined = call(join_kernel, "join", all_heads)(keep, low_in, high_in, cum)
    parts = lax.all_to_all(joined, "seq", 0, 0, tiled=True)
    scanned = call(scan_kernel, "scan", all_heads)(parts, gains)
    mine = lax.all_to_all(scanned, "seq", 0, 0, tiled=True)
    low_out, high_out = call(pass_on_kernel, "pass_on", [half, half])(mine, low, high, cum)
    low_back, high_back = swap(low_out, high_out)
    out_scratch = [
        pltpu.VMEM((2 * HALF_STEPS, GROUP, WIDE), BF16),
        pltpu.SemaphoreType.DMA((2 * HALF_STEPS,)),
    ]
    part = shape_of((STATE, GROUP))
    y, gx, own_row, gct, gbt = call(
        own_kernel,
        "own",
        [tall, tall, rows, part, part],
        [hbm, hbm, vmem, vmem, vmem],
        scratch_shapes=out_scratch,
        cost=cost(4),
    )(mine, yt, gxt, xt, gt, b, c, cum)
    everyone = lax.axis_size("dp") * lax.axis_size("seq")
    gdt, copies = call(
        sums_kernel,
        "sums",
        [rows, shape_of((everyone, 1, STATE))],
        scratch_shapes=[pltpu.VMEM((HEADS, GROUP), F32)],
    )(mine, low_back, high_back, xt, gt, b, c, cum, row, own_row, skiprow, steps, alog)
    sums = lax.all_to_all(copies, ("dp", "seq"), 0, 0, tiled=True)
    y, gx, gc, gb = call(
        other_kernel,
        "other",
        [tall, tall, shape_of((GROUP, STATE), BF16), shape_of((GROUP, STATE), BF16)],
        [hbm, hbm, vmem, vmem],
        in_specs=[vmem] * 13 + [hbm, hbm],
        input_output_aliases={13: 0, 14: 1},
        scratch_shapes=out_scratch,
        cost=cost(4),
    )(low_back, high_back, yt, gxt, xt, gt, b, c, cum, gct, gbt, gci, gbi, y, gx)
    total = jnp.sum(sums, axis=(0, 1))
    return (
        y[None], gx[None], gb[None], gc[None], gdt[None],
        total[:HEADS], total[HEADS : 2 * HEADS],
    )


def solution(mesh):
    placed = (
        P("dp", "seq", None),
        P("dp", "seq", None),
        P("dp", "seq", None),
        P("dp", None, "seq"),
        P(),
        P(),
        P("dp", "seq", None),
    )
    return jax.shard_map(
        shards,
        mesh=mesh,
        in_specs=placed,
        out_specs=(
            P("dp", "seq", None),
            P("dp", "seq", None),
            P("dp", "seq", None),
            P("dp", "seq", None),
            P("dp", None, "seq"),
            P(),
            P(),
        ),
        check_vma=False,
    )
```

```python
import functools

import jax
import jax.numpy as jnp
from jax import lax
from jax.experimental import pallas as pl
from jax.experimental.pallas import tpu as pltpu
from jax.sharding import PartitionSpec as P

GROUP = 256
HEADS = 32
SIZE = 64
STATE = 128
STEP = 8
WIDE = STEP * SIZE
GRID = HEADS // STEP
HALF = HEADS // 2
HALF_STEPS = GRID // 2

F32 = jnp.float32
BF16 = jnp.bfloat16
EXACT = lax.Precision.HIGHEST
VMEM_LIMIT = 24 * 1024 * 1024
LARGE_LIMIT = 60 * 1024 * 1024


def dot(a, b, ca, cb, precision=None):
    return lax.dot_general(
        a, b, (((ca,), (cb,)), ((), ())), precision=precision, preferred_element_type=F32
    )


def iota(shape, dim):
    return lax.broadcasted_iota(jnp.int32, shape, dim)


def triangle():
    shape = (GROUP, GROUP)
    return jnp.where(iota(shape, 0) <= iota(shape, 1), 1.0, 0.0).astype(F32)


def column(row):
    shape = (HEADS, HEADS)
    eye = iota(shape, 0) == iota(shape, 1)
    return jnp.sum(jnp.where(eye, jnp.broadcast_to(row, shape), 0.0), axis=1, keepdims=True)


def as_row(col):
    shape = (HEADS, HEADS)
    eye = iota(shape, 0) == iota(shape, 1)
    return jnp.sum(jnp.where(eye, jnp.broadcast_to(col, shape), 0.0), axis=0, keepdims=True)


def spread(rows):
    return jnp.concatenate(
        [jnp.broadcast_to(rows[j : j + 1], (SIZE, GROUP)) for j in range(STEP)], axis=0
    )


def per_head(full):
    return jnp.concatenate(
        [
            jnp.sum(full[j * SIZE : (j + 1) * SIZE], axis=0, keepdims=True)
            for j in range(STEP)
        ],
        axis=0,
    )


def head_rows(step):
    return pl.ds(pl.multiple_of(step * STEP, STEP), STEP)


def keeps_adjoint(step):
    even = lax.rem(lax.axis_index("seq"), 2) == 0
    return even == (step < HALF_STEPS)


def unpaired(step):
    place = lax.axis_index("seq")
    edge = (place == 0) | (place == lax.axis_size("seq") - 1)
    return jnp.where(edge & (step >= HALF_STEPS), 0.0, 1.0).astype(F32)


def states_kernel(
    x_hbm, g_hbm, b_hbm, c_hbm, dt_hbm, alog_hbm,
    low_ref, high_ref, keep_ref, gain_ref, xt_ref, gt_ref, cum_ref,
    x_s, g_s, b_s, c_s, dt_s, alog_s, sems,
):
    def copy(source, target, slot):
        made = pltpu.make_async_copy(source, target, sems.at[slot])
        made.start()
        return made

    alog_copy = copy(alog_hbm, alog_s, 0)
    dt_copy = copy(dt_hbm, dt_s, 1)
    b_copy = copy(b_hbm, b_s, 2)
    c_copy = copy(c_hbm, c_s, 3)
    inputs = []
    for i in range(GRID):
        lanes = pl.ds(i * WIDE, WIDE)
        inputs.append(
            (
                copy(x_hbm.at[:, lanes], x_s.at[i], 4 + 2 * i),
                copy(g_hbm.at[:, lanes], g_s.at[i], 5 + 2 * i),
            )
        )
    alog_copy.wait()
    dt_copy.wait()
    rate = jnp.exp(column(alog_s[...]))
    cum_all = dot(-rate * dt_s[...], triangle(), 1, 0, EXACT)
    cum_ref[...] = cum_all
    b_copy.wait()
    c_copy.wait()
    for i in range(GRID):
        for made in inputs[i]:
            made.wait()
        cum = cum_all[i * STEP : (i + 1) * STEP]
        last = cum[:, GROUP - 1 :]
        to_end = jnp.exp(last - cum)
        from_start = jnp.exp(cum)
        gain = jnp.exp(last)
        xt = x_s[i].T
        gt = g_s[i].T
        rows = pl.ds(i * WIDE, WIDE)
        xt_ref[rows, :] = xt
        gt_ref[rows, :] = gt
        scaled = (xt.astype(F32) * spread(to_end)).astype(BF16)
        raised = (gt.astype(F32) * spread(from_start)).astype(BF16)
        state = dot(scaled, b_s[...], 1, 0)
        adjoint = dot(raised, c_s[...], 1, 0)
        first = keeps_adjoint(i)
        send = jnp.where(first, state, adjoint) * unpaired(i)
        keep = jnp.where(first, adjoint, state)
        send_ref = low_ref if i < HALF_STEPS else high_ref
        base = i % HALF_STEPS * STEP
        for j in range(STEP):
            part = slice(j * SIZE, (j + 1) * SIZE)
            send_ref[base + j] = send[part]
            keep_ref[i * STEP + j] = keep[part]
            gain_ref[i * STEP + j] = jnp.broadcast_to(gain[j : j + 1], (1, STATE))


def join_kernel(keep_ref, low_ref, high_ref, cum_ref, out_ref):
    gain = jnp.exp(cum_ref[:, GROUP - 1 :])
    for h in range(HEADS):
        other = low_ref[h] if h < HALF else high_ref[h - HALF]
        out_ref[h] = keep_ref[h] + gain[h : h + 1] * other


def scan_kernel(part_ref, gain_ref, out_ref):
    count = part_ref.shape[0]
    low = lax.axis_index("seq") < HALF

    def pair(first, second, carried, mine):
        return gain_ref[first] * gain_ref[second] * carried + part_ref[mine]

    nothing = jnp.zeros((SIZE, STATE), F32)

    @pl.when(low)
    def _():
        state = nothing
        for k in range(0, count, 2):
            out_ref[k] = state
            state = pair(k, k + 1, state, k + 1)
        adjoint = nothing
        for k in reversed(range(0, count, 2)):
            out_ref[k + 1] = adjoint
            adjoint = pair(k, k + 1, adjoint, k)

    @pl.when(jnp.logical_not(low))
    def _():
        state = part_ref[0]
        for k in range(1, count - 1, 2):
            out_ref[k] = state
            state = pair(k, k + 1, state, k + 1)
        out_ref[count - 1] = state
        adjoint = part_ref[count - 1]
        for k in reversed(range(1, count - 1, 2)):
            out_ref[k + 1] = adjoint
            adjoint = pair(k, k + 1, adjoint, k)
        out_ref[0] = adjoint


def pass_on_kernel(mine_ref, low_ref, high_ref, cum_ref, out_low_ref, out_high_ref):
    gain = jnp.exp(cum_ref[:, GROUP - 1 :])
    low_gain = gain[:HALF] * unpaired(0)
    high_gain = gain[HALF:] * unpaired(GRID - 1)
    for h in range(HALF):
        out_low_ref[h] = low_ref[h] + low_gain[h : h + 1] * mine_ref[h]
        out_high_ref[h] = high_ref[h] + high_gain[h : h + 1] * mine_ref[HALF + h]


def inner_kernel(offset, *refs):
    (g_ref, xt_ref, gt_ref, b_ref, c_ref, cum_ref, skip_ref), refs = refs[:7], refs[7:]
    (y_ref, gx_ref, row_ref, skiprow_ref, gb_ref, gc_ref, cb_s, acc_s) = refs[-8:]
    place = pl.program_id(0)
    step = place + offset
    half = GROUP // 2

    @pl.when(place == 0)
    def _():
        cb_s[...] = dot(c_ref[...], b_ref[...], 1, 1)
        acc_s[...] = jnp.zeros_like(acc_s)

    square = (half, half)
    lower = iota(square, 0) >= iota(square, 1)
    nothing = jnp.zeros((SIZE, GROUP), BF16)
    cum = cum_ref[head_rows(step), :]
    cum_t = cum.T
    rows = []
    skips = []
    for j in range(STEP):
        low, high = j * SIZE, (j + 1) * SIZE
        early, late = cum[j : j + 1, :half], cum[j : j + 1, half:]
        start, end = cum_t[:half, j : j + 1], cum_t[half:, j : j + 1]
        e00 = jnp.where(lower, jnp.exp(start - early), 0.0)
        e10 = jnp.exp(end - early)
        e11 = jnp.where(lower, jnp.exp(end - late), 0.0)
        w00 = (cb_s[:half, :half] * e00).astype(BF16)
        w10 = (cb_s[half:, :half] * e10).astype(BF16)
        w11 = (cb_s[half:, half:] * e11).astype(BF16)
        weights = jnp.concatenate(
            [
                jnp.concatenate([w00, jnp.zeros(square, BF16)], axis=1),
                jnp.concatenate([w10, w11], axis=1),
            ],
            axis=0,
        )
        xt = xt_ref[low:high, :]
        gt = gt_ref[low:high, :]
        yt = dot(xt, weights, 1, 1)
        gxt = dot(gt, weights, 1, 0)
        pair = j // 2 * 2 * SIZE
        two = [xt, nothing] if j % 2 == 0 else [nothing, xt]
        gw = dot(g_ref[:, pair : pair + 2 * SIZE], jnp.concatenate(two, axis=0), 1, 0)
        acc_s[:half, :half] += gw[:half, :half] * e00
        acc_s[half:, :half] += gw[half:, :half] * e10
        acc_s[half:, half:] += gw[half:, half:] * e11
        xf = xt.astype(F32)
        gf = gt.astype(F32)
        rows.append(jnp.sum(gf * yt - xf * gxt, axis=0, keepdims=True))
        skips.append(jnp.sum(gf * xf, axis=0, keepdims=True))
        skip = skip_ref[step * STEP + j]
        y_ref[low:high, :] = (yt + skip * xf).astype(BF16)
        gx_ref[low:high, :] = (gxt + skip * gf).astype(BF16)
    here = pl.ds(pl.multiple_of(place * STEP, STEP), STEP)
    row_ref[here, :] = jnp.concatenate(rows, axis=0)
    skiprow_ref[here, :] = jnp.concatenate(skips, axis=0)

    @pl.when(place == HALF_STEPS - 1)
    def _():
        acc = acc_s[...].astype(BF16)
        gc_ref[...] = dot(acc, b_ref[...], 1, 0)
        gb_ref[...] = dot(acc, c_ref[...], 0, 0)


def inner(offset, g, xt, gt, b, c, cum, skip, earlier=()):
    wide_t = pl.BlockSpec((WIDE, GROUP), lambda i: (i + offset, 0))
    wide_n = pl.BlockSpec((GROUP, WIDE), lambda i: (0, i + offset))
    kept = lambda *shape: pl.BlockSpec(shape, lambda i: (0,) * len(shape))
    narrow = kept(GROUP, STATE)
    wide = shape_of((HEADS * SIZE, GROUP), BF16)
    rows = shape_of((HALF, GROUP))
    return call(
        functools.partial(inner_kernel, offset),
        "inner",
        [wide, wide, rows, rows, shape_of((GROUP, STATE)), shape_of((GROUP, STATE))],
        [wide_t, wide_t, kept(HALF, GROUP), kept(HALF, GROUP), narrow, narrow],
        grid=(HALF_STEPS,),
        in_specs=[
            wide_n, wide_t, wide_t, narrow, narrow, kept(HEADS, GROUP),
            pl.BlockSpec(memory_space=pltpu.SMEM),
        ]
        + [pl.BlockSpec(memory_space=pltpu.HBM)] * len(earlier),
        input_output_aliases={7 + i: i for i in range(len(earlier))},
        scratch_shapes=[pltpu.VMEM((GROUP, GROUP), F32), pltpu.VMEM((GROUP, GROUP), F32)],
        cost=cost(4),
        limit=LARGE_LIMIT,
    )(g, xt, gt, b, c, cum, skip, *earlier)


def halves(own):
    even = lax.rem(lax.axis_index("seq"), 2) == 0
    state_low = even == own
    state = jnp.where(state_low, 0, HALF_STEPS)
    return state_low, state, HALF_STEPS - state


def feature_rows(step):
    return pl.ds(pl.multiple_of(step * WIDE, WIDE), WIDE)


def take(ref, step):
    full = ref[pl.ds(pl.multiple_of(step * STEP, STEP), STEP)]
    return full.reshape(WIDE, STATE).astype(BF16)


def take_half(low_ref, high_ref, low, i):
    part = pl.ds(i * STEP, STEP)
    return jnp.where(low, low_ref[part], high_ref[part]).reshape(WIDE, STATE).astype(BF16)


def carried_rows(state, gt_ref, c_ref, cum_ref, step):
    from_start = jnp.exp(cum_ref[head_rows(step), :])
    gf = gt_ref[feature_rows(step), :].astype(F32)
    raw = dot(state, c_ref[...], 1, 1)
    return raw, gf, from_start, per_head(gf * raw) * from_start


def scaled_rows(adjoint, xt_ref, b_ref, cum_ref, step):
    cum = cum_ref[head_rows(step), :]
    to_end = jnp.exp(cum[:, GROUP - 1 :] - cum)
    xf = xt_ref[feature_rows(step), :].astype(F32)
    raw = dot(adjoint, b_ref[...], 1, 1)
    from_x = per_head(xf * raw) * to_end
    final = iota((STEP, GROUP), 1) == GROUP - 1
    total = jnp.sum(from_x, axis=1, keepdims=True)
    return raw, xf, to_end, jnp.where(final, total, 0.0) - from_x


def give_out(
    i, state_step, adjoint_step, state, adjoint, raws,
    yt_ref, gxt_ref, y_hbm, gx_hbm, out_s, sems, gct, gbt,
):
    raw, gf, from_start, back, xf, to_end = raws
    start_w = spread(from_start)
    end_w = spread(to_end)
    y = yt_ref[feature_rows(state_step), :].astype(F32) + raw * start_w
    out_s[2 * i] = y.astype(BF16).T
    gx = gxt_ref[feature_rows(adjoint_step), :].astype(F32) + back * end_w
    out_s[2 * i + 1] = gx.astype(BF16).T
    copies = []
    for slot, step, target in ((2 * i, state_step, y_hbm), (2 * i + 1, adjoint_step, gx_hbm)):
        lanes = pl.ds(pl.multiple_of(step * WIDE, WIDE), WIDE)
        made = pltpu.make_async_copy(out_s.at[slot], target.at[:, lanes], sems.at[slot])
        made.start()
        copies.append(made)
    gct = gct + dot(state, (gf * start_w).astype(BF16), 0, 0)
    gbt = gbt + dot(adjoint, (xf * end_w).astype(BF16), 0, 0)
    return gct, gbt, copies


def own_kernel(
    mine_ref, yt_ref, gxt_ref, xt_ref, gt_ref, b_ref, c_ref, cum_ref,
    y_hbm, gx_hbm, row_ref, gct_ref, gbt_ref,
    out_s, sems,
):
    _, state_first, adjoint_first = halves(True)
    gct = jnp.zeros((STATE, GROUP), F32)
    gbt = jnp.zeros((STATE, GROUP), F32)
    copies = []
    for i in range(HALF_STEPS):
        state_step, adjoint_step = state_first + i, adjoint_first + i
        state = take(mine_ref, state_step)
        adjoint = take(mine_ref, adjoint_step)
        raw, gf, from_start, row = carried_rows(state, gt_ref, c_ref, cum_ref, state_step)
        row_ref[head_rows(state_step), :] = row
        back, xf, to_end, row = scaled_rows(adjoint, xt_ref, b_ref, cum_ref, adjoint_step)
        row_ref[head_rows(adjoint_step), :] = row
        gct, gbt, made = give_out(
            i, state_step, adjoint_step, state, adjoint, (raw, gf, from_start, back, xf, to_end),
            yt_ref, gxt_ref, y_hbm, gx_hbm, out_s, sems, gct, gbt,
        )
        copies += made
    gct_ref[...] = gct
    gbt_ref[...] = gbt
    for made in copies:
        made.wait()


def sums_kernel(
    mine_ref, low_ref, high_ref, xt_ref, gt_ref, b_ref, c_ref, cum_ref, low_row_ref,
    high_row_ref, own_row_ref, low_skiprow_ref, high_skiprow_ref, dt_ref, alog_ref,
    gdt_ref, sums_ref,
    row_s,
):
    state_low, state_first, adjoint_first = halves(False)
    for i in range(HALF_STEPS):
        state = take_half(low_ref, high_ref, state_low, i)
        adjoint = take_half(high_ref, low_ref, state_low, i)
        row_s[head_rows(state_first + i), :] = carried_rows(
            state, gt_ref, c_ref, cum_ref, state_first + i
        )[-1]
        row_s[head_rows(adjoint_first + i), :] = scaled_rows(
            adjoint, xt_ref, b_ref, cum_ref, adjoint_first + i
        )[-1]
    overlap = jnp.concatenate(
        [
            jnp.sum(mine_ref[:HALF] * low_ref[...], axis=1),
            jnp.sum(mine_ref[HALF:] * high_ref[...], axis=1),
        ],
        axis=0,
    )
    overlap = jnp.sum(overlap, axis=1, keepdims=True) * jnp.exp(cum_ref[:, GROUP - 1 :])
    final = iota((HEADS, GROUP), 1) == GROUP - 1
    inner_row = jnp.concatenate([low_row_ref[...], high_row_ref[...]], axis=0)
    row = inner_row + own_row_ref[...] + row_s[...] + jnp.where(final, overlap, 0.0)
    gdt = -jnp.exp(column(alog_ref[...])) * dot(row, triangle(), 1, 1, EXACT)
    gdt_ref[...] = gdt
    alog = jnp.sum(gdt * dt_ref[...], axis=1, keepdims=True)
    skiprow = jnp.concatenate([low_skiprow_ref[...], high_skiprow_ref[...]], axis=0)
    skip = jnp.sum(skiprow, axis=1, keepdims=True)
    sums = jnp.concatenate(
        [as_row(alog), as_row(skip), jnp.zeros((1, STATE - 2 * HEADS), F32)], axis=1
    )
    sums_ref[...] = jnp.broadcast_to(sums[None], sums_ref.shape)


def total_kernel(sums_ref, alog_ref, skip_ref):
    total = jnp.sum(sums_ref[...], axis=0)
    alog_ref[...] = total[:, :HEADS]
    skip_ref[...] = total[:, HEADS : 2 * HEADS]


def other_kernel(
    low_ref, high_ref, yt_ref, gxt_ref, xt_ref, gt_ref, b_ref, c_ref, cum_ref,
    gct_ref, gbt_ref, low_gc_ref, high_gc_ref, low_gb_ref, high_gb_ref, y_in, gx_in,
    y_hbm, gx_hbm, gc_ref, gb_ref,
    out_s, sems,
):
    state_low, state_first, adjoint_first = halves(False)
    gct = gct_ref[...]
    gbt = gbt_ref[...]
    copies = []
    for i in range(HALF_STEPS):
        state_step, adjoint_step = state_first + i, adjoint_first + i
        state = take_half(low_ref, high_ref, state_low, i)
        adjoint = take_half(high_ref, low_ref, state_low, i)
        raw, gf, from_start, _ = carried_rows(state, gt_ref, c_ref, cum_ref, state_step)
        back, xf, to_end, _ = scaled_rows(adjoint, xt_ref, b_ref, cum_ref, adjoint_step)
        gct, gbt, made = give_out(
            i, state_step, adjoint_step, state, adjoint, (raw, gf, from_start, back, xf, to_end),
            yt_ref, gxt_ref, y_hbm, gx_hbm, out_s, sems, gct, gbt,
        )
        copies += made
    gc_ref[...] = (low_gc_ref[...] + high_gc_ref[...] + gct.T).astype(BF16)
    gb_ref[...] = (low_gb_ref[...] + high_gb_ref[...] + gbt.T).astype(BF16)
    for made in copies:
        made.wait()


def shape_of(shape, dtype=F32):
    return jax.ShapeDtypeStruct(shape, dtype)


def call(kernel, name, out_shape, out_specs=None, cost=None, limit=VMEM_LIMIT, **more):
    if out_specs is not None:
        more["out_specs"] = out_specs
    return pl.pallas_call(
        kernel,
        out_shape=out_shape,
        compiler_params=pltpu.CompilerParams(vmem_limit_bytes=limit),
        cost_estimate=cost,
        name=name,
        **more,
    )


def cost(us):
    return pl.CostEstimate(flops=us * 500_000_000, bytes_accessed=us << 21, transcendentals=0)


def swap(low, high):
    count = lax.axis_size("seq")
    low_pairs = [(i, i ^ 1) for i in range(count)]
    high_pairs = [(i, ((i - 1 ^ 1) + 1) % count) for i in range(1, count)] + [(0, count - 1)]
    return lax.ppermute(low, "seq", low_pairs), lax.ppermute(high, "seq", high_pairs)


def shards(x_in, b_in, c_in, dt, a_log, skip, cotangent):
    x, b, c, g, steps = x_in[0], b_in[0], c_in[0], cotangent[0], dt[0]
    alog = a_log[None]
    feat = HEADS * SIZE
    vmem = pl.BlockSpec(memory_space=pltpu.VMEM)
    hbm = pl.BlockSpec(memory_space=pltpu.HBM)
    half = shape_of((HALF, SIZE, STATE))
    all_heads = shape_of((HEADS, SIZE, STATE))
    wide = shape_of((feat, GROUP), BF16)
    tall = shape_of((GROUP, feat), BF16)
    rows = shape_of((HEADS, GROUP))
    low, high, keep, gain, xt, gt, cum = call(
        states_kernel,
        "states",
        [half, half, all_heads, shape_of((HEADS, 1, STATE)), wide, wide, rows],
        in_specs=[hbm] * 6,
        scratch_shapes=[
            pltpu.VMEM((GRID, GROUP, WIDE), BF16),
            pltpu.VMEM((GRID, GROUP, WIDE), BF16),
            pltpu.VMEM((GROUP, STATE), BF16),
            pltpu.VMEM((GROUP, STATE), BF16),
            pltpu.VMEM((HEADS, GROUP), F32),
            pltpu.VMEM((1, HEADS), F32),
            pltpu.SemaphoreType.DMA((4 + 2 * GRID,)),
        ],
        limit=LARGE_LIMIT,
    )(x, g, b, c, steps, alog)
    low_in, high_in = swap(low, high)
    gains = lax.all_to_all(gain, "seq", 0, 0, tiled=True)
    yt, gxt, low_row, low_skiprow, low_gb, low_gc = inner(0, g, xt, gt, b, c, cum, skip)
    low_in, high_in, gains, yt, gxt = lax.optimization_barrier((low_in, high_in, gains, yt, gxt))
    joined = call(join_kernel, "join", all_heads)(keep, low_in, high_in, cum)
    parts = lax.all_to_all(joined, "seq", 0, 0, tiled=True)
    scanned = call(scan_kernel, "scan", all_heads)(parts, gains)
    mine = lax.all_to_all(scanned, "seq", 0, 0, tiled=True)
    low_out, high_out = call(pass_on_kernel, "pass_on", [half, half])(mine, low, high, cum)
    low_back, high_back = swap(low_out, high_out)
    yt, gxt, high_row, high_skiprow, high_gb, high_gc = inner(
        HALF_STEPS, g, xt, gt, b, c, cum, skip, (yt, gxt)
    )
    out_scratch = [
        pltpu.VMEM((2 * HALF_STEPS, GROUP, WIDE), BF16),
        pltpu.SemaphoreType.DMA((2 * HALF_STEPS,)),
    ]
    part = shape_of((STATE, GROUP))
    y, gx, own_row, gct, gbt = call(
        own_kernel,
        "own",
        [tall, tall, rows, part, part],
        [hbm, hbm, vmem, vmem, vmem],
        scratch_shapes=out_scratch,
        cost=cost(4),
    )(mine, yt, gxt, xt, gt, b, c, cum)
    everyone = lax.axis_size("dp") * lax.axis_size("seq")
    gdt, copies = call(
        sums_kernel,
        "sums",
        [rows, shape_of((everyone, 1, STATE))],
        scratch_shapes=[pltpu.VMEM((HEADS, GROUP), F32)],
    )(
        mine, low_back, high_back, xt, gt, b, c, cum, low_row, high_row, own_row,
        low_skiprow, high_skiprow, steps, alog,
    )
    sums = lax.all_to_all(copies, ("dp", "seq"), 0, 0, tiled=True)
    y, gx, gc, gb = call(
        other_kernel,
        "other",
        [tall, tall, shape_of((GROUP, STATE), BF16), shape_of((GROUP, STATE), BF16)],
        [hbm, hbm, vmem, vmem],
        in_specs=[vmem] * 15 + [hbm, hbm],
        input_output_aliases={15: 0, 16: 1},
        scratch_shapes=out_scratch,
        cost=cost(4),
    )(
        low_back, high_back, yt, gxt, xt, gt, b, c, cum, gct, gbt,
        low_gc, high_gc, low_gb, high_gb, y, gx,
    )
    galog, gskip = call(
        total_kernel, "total", [shape_of((1, HEADS)), shape_of((1, HEADS))]
    )(sums)
    return (
        y[None], gx[None], gb[None], gc[None], gdt[None],
        galog[0], gskip[0],
    )


def solution(mesh):
    placed = (
        P("dp", "seq", None),
        P("dp", "seq", None),
        P("dp", "seq", None),
        P("dp", None, "seq"),
        P(),
        P(),
        P("dp", "seq", None),
    )
    return jax.shard_map(
        shards,
        mesh=mesh,
        in_specs=placed,
        out_specs=(
            P("dp", "seq", None),
            P("dp", "seq", None),
            P("dp", "seq", None),
            P("dp", "seq", None),
            P("dp", None, "seq"),
            P(),
            P(),
        ),
        check_vma=False,
    )
```

```python
import functools

import jax
import jax.numpy as jnp
from jax import lax
from jax.experimental import pallas as pl
from jax.experimental.pallas import tpu as pltpu
from jax.sharding import PartitionSpec as P

GROUP = 256
HEADS = 32
SIZE = 64
STATE = 128
STEP = 8
WIDE = STEP * SIZE
GRID = HEADS // STEP
HALF = HEADS // 2
HALF_STEPS = GRID // 2

F32 = jnp.float32
BF16 = jnp.bfloat16
EXACT = lax.Precision.HIGHEST
VMEM_LIMIT = 16 * 1024 * 1024
LARGE_LIMIT = 60 * 1024 * 1024


def dot(a, b, ca, cb, precision=None):
    return lax.dot_general(
        a, b, (((ca,), (cb,)), ((), ())), precision=precision, preferred_element_type=F32
    )


def iota(shape, dim):
    return lax.broadcasted_iota(jnp.int32, shape, dim)


def triangle():
    shape = (GROUP, GROUP)
    return jnp.where(iota(shape, 0) <= iota(shape, 1), 1.0, 0.0).astype(F32)


def column(row):
    shape = (HEADS, HEADS)
    eye = iota(shape, 0) == iota(shape, 1)
    return jnp.sum(jnp.where(eye, jnp.broadcast_to(row, shape), 0.0), axis=1, keepdims=True)


def as_row(col):
    shape = (HEADS, HEADS)
    eye = iota(shape, 0) == iota(shape, 1)
    return jnp.sum(jnp.where(eye, jnp.broadcast_to(col, shape), 0.0), axis=0, keepdims=True)


def spread(rows):
    return jnp.concatenate(
        [jnp.broadcast_to(rows[j : j + 1], (SIZE, GROUP)) for j in range(STEP)], axis=0
    )


def per_head(full):
    return jnp.concatenate(
        [
            jnp.sum(full[j * SIZE : (j + 1) * SIZE], axis=0, keepdims=True)
            for j in range(STEP)
        ],
        axis=0,
    )


def head_rows(step):
    return pl.ds(pl.multiple_of(step * STEP, STEP), STEP)


def keeps_adjoint(step):
    even = lax.rem(lax.axis_index("seq"), 2) == 0
    return even == (step < HALF_STEPS)


def unpaired(step):
    place = lax.axis_index("seq")
    edge = (place == 0) | (place == lax.axis_size("seq") - 1)
    return jnp.where(edge & (step >= HALF_STEPS), 0.0, 1.0).astype(F32)


def states_kernel(
    x_hbm, g_hbm, b_hbm, c_hbm, dt_hbm, alog_hbm,
    low_ref, high_ref, keep_ref, gain_ref, xt_ref, gt_ref, cum_ref,
    x_s, g_s, b_s, c_s, dt_s, alog_s, sems,
):
    def copy(source, target, slot):
        made = pltpu.make_async_copy(source, target, sems.at[slot])
        made.start()
        return made

    alog_copy = copy(alog_hbm, alog_s, 0)
    dt_copy = copy(dt_hbm, dt_s, 1)
    b_copy = copy(b_hbm, b_s, 2)
    c_copy = copy(c_hbm, c_s, 3)
    inputs = []
    for i in range(GRID):
        lanes = pl.ds(i * WIDE, WIDE)
        inputs.append(
            (
                copy(x_hbm.at[:, lanes], x_s.at[i], 4 + 2 * i),
                copy(g_hbm.at[:, lanes], g_s.at[i], 5 + 2 * i),
            )
        )
    alog_copy.wait()
    dt_copy.wait()
    rate = jnp.exp(column(alog_s[...]))
    cum_all = dot(-rate * dt_s[...], triangle(), 1, 0, EXACT)
    cum_ref[...] = cum_all
    b_copy.wait()
    c_copy.wait()
    for i in range(GRID):
        for made in inputs[i]:
            made.wait()
        cum = cum_all[i * STEP : (i + 1) * STEP]
        last = cum[:, GROUP - 1 :]
        to_end = jnp.exp(last - cum)
        from_start = jnp.exp(cum)
        gain = jnp.exp(last)
        xt = x_s[i].T
        gt = g_s[i].T
        rows = pl.ds(i * WIDE, WIDE)
        xt_ref[rows, :] = xt
        gt_ref[rows, :] = gt
        scaled = (xt.astype(F32) * spread(to_end)).astype(BF16)
        raised = (gt.astype(F32) * spread(from_start)).astype(BF16)
        state = dot(scaled, b_s[...], 1, 0)
        adjoint = dot(raised, c_s[...], 1, 0)
        first = keeps_adjoint(i)
        send = jnp.where(first, state, adjoint) * unpaired(i)
        keep = jnp.where(first, adjoint, state)
        send_ref = low_ref if i < HALF_STEPS else high_ref
        base = i % HALF_STEPS * STEP
        for j in range(STEP):
            part = slice(j * SIZE, (j + 1) * SIZE)
            send_ref[base + j] = send[part]
            keep_ref[i * STEP + j] = keep[part]
            gain_ref[i * STEP + j] = jnp.broadcast_to(gain[j : j + 1], (1, STATE))


def join_kernel(keep_ref, low_ref, high_ref, cum_ref, out_ref):
    gain = jnp.exp(cum_ref[:, GROUP - 1 :])
    for h in range(HEADS):
        other = low_ref[h] if h < HALF else high_ref[h - HALF]
        out_ref[h] = keep_ref[h] + gain[h : h + 1] * other


def scan_kernel(part_ref, gain_ref, out_ref):
    count = part_ref.shape[0]
    low = lax.axis_index("seq") < HALF

    def pair(first, second, carried, mine):
        return gain_ref[first] * gain_ref[second] * carried + part_ref[mine]

    nothing = jnp.zeros((SIZE, STATE), F32)

    @pl.when(low)
    def _():
        state = nothing
        for k in range(0, count, 2):
            out_ref[k] = state
            state = pair(k, k + 1, state, k + 1)
        adjoint = nothing
        for k in reversed(range(0, count, 2)):
            out_ref[k + 1] = adjoint
            adjoint = pair(k, k + 1, adjoint, k)

    @pl.when(jnp.logical_not(low))
    def _():
        state = part_ref[0]
        for k in range(1, count - 1, 2):
            out_ref[k] = state
            state = pair(k, k + 1, state, k + 1)
        out_ref[count - 1] = state
        adjoint = part_ref[count - 1]
        for k in reversed(range(1, count - 1, 2)):
            out_ref[k + 1] = adjoint
            adjoint = pair(k, k + 1, adjoint, k)
        out_ref[0] = adjoint


def pass_on_kernel(mine_ref, low_ref, high_ref, cum_ref, out_low_ref, out_high_ref):
    gain = jnp.exp(cum_ref[:, GROUP - 1 :])
    low_gain = gain[:HALF] * unpaired(0)
    high_gain = gain[HALF:] * unpaired(GRID - 1)
    for h in range(HALF):
        out_low_ref[h] = low_ref[h] + low_gain[h : h + 1] * mine_ref[h]
        out_high_ref[h] = high_ref[h] + high_gain[h : h + 1] * mine_ref[HALF + h]


def inner_kernel(offset, *refs):
    (g_ref, xt_ref, gt_ref, b_ref, c_ref, cum_ref, skip_ref), refs = refs[:7], refs[7:]
    (y_ref, gx_ref, row_ref, skiprow_ref, gb_ref, gc_ref, cb_s, acc_s) = refs[-8:]
    place = pl.program_id(0)
    step = place + offset
    half = GROUP // 2

    @pl.when(place == 0)
    def _():
        cb_s[...] = dot(c_ref[...], b_ref[...], 1, 1)
        acc_s[...] = jnp.zeros_like(acc_s)

    square = (half, half)
    lower = iota(square, 0) >= iota(square, 1)
    nothing = jnp.zeros((SIZE, GROUP), BF16)
    cum = cum_ref[head_rows(step), :]
    cum_t = cum.T
    rows = []
    skips = []
    for j in range(STEP):
        low, high = j * SIZE, (j + 1) * SIZE
        early, late = cum[j : j + 1, :half], cum[j : j + 1, half:]
        start, end = cum_t[:half, j : j + 1], cum_t[half:, j : j + 1]
        e00 = jnp.where(lower, jnp.exp(start - early), 0.0)
        e10 = jnp.exp(end - early)
        e11 = jnp.where(lower, jnp.exp(end - late), 0.0)
        w00 = (cb_s[:half, :half] * e00).astype(BF16)
        w10 = (cb_s[half:, :half] * e10).astype(BF16)
        w11 = (cb_s[half:, half:] * e11).astype(BF16)
        weights = jnp.concatenate(
            [
                jnp.concatenate([w00, jnp.zeros(square, BF16)], axis=1),
                jnp.concatenate([w10, w11], axis=1),
            ],
            axis=0,
        )
        xt = xt_ref[low:high, :]
        gt = gt_ref[low:high, :]
        yt = dot(xt, weights, 1, 1)
        gxt = dot(gt, weights, 1, 0)
        pair = j // 2 * 2 * SIZE
        two = [xt, nothing] if j % 2 == 0 else [nothing, xt]
        gw = dot(g_ref[:, pair : pair + 2 * SIZE], jnp.concatenate(two, axis=0), 1, 0)
        acc_s[:half, :half] += gw[:half, :half] * e00
        acc_s[half:, :half] += gw[half:, :half] * e10
        acc_s[half:, half:] += gw[half:, half:] * e11
        xf = xt.astype(F32)
        gf = gt.astype(F32)
        rows.append(jnp.sum(gf * yt - xf * gxt, axis=0, keepdims=True))
        skips.append(jnp.sum(gf * xf, axis=0, keepdims=True))
        skip = skip_ref[step * STEP + j]
        y_ref[low:high, :] = (yt + skip * xf).astype(BF16)
        gx_ref[low:high, :] = (gxt + skip * gf).astype(BF16)
    here = pl.ds(pl.multiple_of(place * STEP, STEP), STEP)
    row_ref[here, :] = jnp.concatenate(rows, axis=0)
    skiprow_ref[here, :] = jnp.concatenate(skips, axis=0)

    @pl.when(place == HALF_STEPS - 1)
    def _():
        acc = acc_s[...].astype(BF16)
        gc_ref[...] = dot(acc, b_ref[...], 1, 0)
        gb_ref[...] = dot(acc, c_ref[...], 0, 0)


def inner(offset, g, xt, gt, b, c, cum, skip, earlier=()):
    wide_t = pl.BlockSpec((WIDE, GROUP), lambda i: (i + offset, 0))
    wide_n = pl.BlockSpec((GROUP, WIDE), lambda i: (0, i + offset))
    kept = lambda *shape: pl.BlockSpec(shape, lambda i: (0,) * len(shape))
    narrow = kept(GROUP, STATE)
    wide = shape_of((HEADS * SIZE, GROUP), BF16)
    rows = shape_of((HALF, GROUP))
    return call(
        functools.partial(inner_kernel, offset),
        "inner",
        [wide, wide, rows, rows, shape_of((GROUP, STATE)), shape_of((GROUP, STATE))],
        [wide_t, wide_t, kept(HALF, GROUP), kept(HALF, GROUP), narrow, narrow],
        grid=(HALF_STEPS,),
        in_specs=[
            wide_n, wide_t, wide_t, narrow, narrow, kept(HEADS, GROUP),
            pl.BlockSpec(memory_space=pltpu.SMEM),
        ]
        + [pl.BlockSpec(memory_space=pltpu.HBM)] * len(earlier),
        input_output_aliases={7 + i: i for i in range(len(earlier))},
        scratch_shapes=[pltpu.VMEM((GROUP, GROUP), F32), pltpu.VMEM((GROUP, GROUP), F32)],
        cost=cost(4),
        limit=VMEM_LIMIT if earlier else LARGE_LIMIT,
    )(g, xt, gt, b, c, cum, skip, *earlier)


def halves(own):
    even = lax.rem(lax.axis_index("seq"), 2) == 0
    state_low = even == own
    state = jnp.where(state_low, 0, HALF_STEPS)
    return state_low, state, HALF_STEPS - state


def feature_rows(step):
    return pl.ds(pl.multiple_of(step * WIDE, WIDE), WIDE)


def take(ref, step):
    full = ref[pl.ds(pl.multiple_of(step * STEP, STEP), STEP)]
    return full.reshape(WIDE, STATE).astype(BF16)


def take_half(low_ref, high_ref, low, i):
    part = pl.ds(i * STEP, STEP)
    return jnp.where(low, low_ref[part], high_ref[part]).reshape(WIDE, STATE).astype(BF16)


def carried_rows(state, gt_ref, c_ref, cum_ref, step):
    from_start = jnp.exp(cum_ref[head_rows(step), :])
    gf = gt_ref[feature_rows(step), :].astype(F32)
    raw = dot(state, c_ref[...], 1, 1)
    return raw, gf, from_start, per_head(gf * raw) * from_start


def scaled_rows(adjoint, xt_ref, b_ref, cum_ref, step):
    cum = cum_ref[head_rows(step), :]
    to_end = jnp.exp(cum[:, GROUP - 1 :] - cum)
    xf = xt_ref[feature_rows(step), :].astype(F32)
    raw = dot(adjoint, b_ref[...], 1, 1)
    from_x = per_head(xf * raw) * to_end
    final = iota((STEP, GROUP), 1) == GROUP - 1
    total = jnp.sum(from_x, axis=1, keepdims=True)
    return raw, xf, to_end, jnp.where(final, total, 0.0) - from_x


def give_out(
    i, state_step, adjoint_step, state, adjoint, raws,
    yt_ref, gxt_ref, y_hbm, gx_hbm, out_s, sems, gct, gbt,
):
    raw, gf, from_start, back, xf, to_end = raws
    start_w = spread(from_start)
    end_w = spread(to_end)
    y = yt_ref[feature_rows(state_step), :].astype(F32) + raw * start_w
    out_s[2 * i] = y.astype(BF16).T
    gx = gxt_ref[feature_rows(adjoint_step), :].astype(F32) + back * end_w
    out_s[2 * i + 1] = gx.astype(BF16).T
    copies = []
    for slot, step, target in ((2 * i, state_step, y_hbm), (2 * i + 1, adjoint_step, gx_hbm)):
        lanes = pl.ds(pl.multiple_of(step * WIDE, WIDE), WIDE)
        made = pltpu.make_async_copy(out_s.at[slot], target.at[:, lanes], sems.at[slot])
        made.start()
        copies.append(made)
    gct = gct + dot(state, (gf * start_w).astype(BF16), 0, 0)
    gbt = gbt + dot(adjoint, (xf * end_w).astype(BF16), 0, 0)
    return gct, gbt, copies


def own_kernel(
    mine_ref, yt_ref, gxt_ref, xt_ref, gt_ref, b_ref, c_ref, cum_ref,
    y_hbm, gx_hbm, row_ref, gct_ref, gbt_ref,
    out_s, sems,
):
    _, state_first, adjoint_first = halves(True)
    gct = jnp.zeros((STATE, GROUP), F32)
    gbt = jnp.zeros((STATE, GROUP), F32)
    copies = []
    for i in range(HALF_STEPS):
        state_step, adjoint_step = state_first + i, adjoint_first + i
        state = take(mine_ref, state_step)
        adjoint = take(mine_ref, adjoint_step)
        raw, gf, from_start, row = carried_rows(state, gt_ref, c_ref, cum_ref, state_step)
        row_ref[head_rows(state_step), :] = row
        back, xf, to_end, row = scaled_rows(adjoint, xt_ref, b_ref, cum_ref, adjoint_step)
        row_ref[head_rows(adjoint_step), :] = row
        gct, gbt, made = give_out(
            i, state_step, adjoint_step, state, adjoint, (raw, gf, from_start, back, xf, to_end),
            yt_ref, gxt_ref, y_hbm, gx_hbm, out_s, sems, gct, gbt,
        )
        copies += made
    gct_ref[...] = gct
    gbt_ref[...] = gbt
    for made in copies:
        made.wait()


def sums_kernel(
    mine_ref, low_ref, high_ref, xt_ref, gt_ref, b_ref, c_ref, cum_ref, low_row_ref,
    high_row_ref, own_row_ref, low_skiprow_ref, high_skiprow_ref, dt_ref, alog_ref,
    gdt_ref, sums_ref,
    row_s,
):
    state_low, state_first, adjoint_first = halves(False)
    for i in range(HALF_STEPS):
        state = take_half(low_ref, high_ref, state_low, i)
        adjoint = take_half(high_ref, low_ref, state_low, i)
        row_s[head_rows(state_first + i), :] = carried_rows(
            state, gt_ref, c_ref, cum_ref, state_first + i
        )[-1]
        row_s[head_rows(adjoint_first + i), :] = scaled_rows(
            adjoint, xt_ref, b_ref, cum_ref, adjoint_first + i
        )[-1]
    overlap = jnp.concatenate(
        [
            jnp.sum(mine_ref[:HALF] * low_ref[...], axis=1),
            jnp.sum(mine_ref[HALF:] * high_ref[...], axis=1),
        ],
        axis=0,
    )
    overlap = jnp.sum(overlap, axis=1, keepdims=True) * jnp.exp(cum_ref[:, GROUP - 1 :])
    final = iota((HEADS, GROUP), 1) == GROUP - 1
    inner_row = jnp.concatenate([low_row_ref[...], high_row_ref[...]], axis=0)
    row = inner_row + own_row_ref[...] + row_s[...] + jnp.where(final, overlap, 0.0)
    gdt = -jnp.exp(column(alog_ref[...])) * dot(row, triangle(), 1, 1, EXACT)
    gdt_ref[...] = gdt
    alog = jnp.sum(gdt * dt_ref[...], axis=1, keepdims=True)
    skiprow = jnp.concatenate([low_skiprow_ref[...], high_skiprow_ref[...]], axis=0)
    skip = jnp.sum(skiprow, axis=1, keepdims=True)
    sums = jnp.concatenate(
        [as_row(alog), as_row(skip), jnp.zeros((1, STATE - 2 * HEADS), F32)], axis=1
    )
    sums_ref[...] = jnp.broadcast_to(sums[None], sums_ref.shape)


def total_kernel(sums_ref, alog_ref, skip_ref):
    total = jnp.sum(sums_ref[...], axis=0)
    alog_ref[...] = total[:, :HEADS]
    skip_ref[...] = total[:, HEADS : 2 * HEADS]


def other_kernel(
    low_ref, high_ref, yt_ref, gxt_ref, xt_ref, gt_ref, b_ref, c_ref, cum_ref,
    gct_ref, gbt_ref, low_gc_ref, high_gc_ref, low_gb_ref, high_gb_ref, y_in, gx_in,
    y_hbm, gx_hbm, gc_ref, gb_ref,
    out_s, sems,
):
    state_low, state_first, adjoint_first = halves(False)
    gct = gct_ref[...]
    gbt = gbt_ref[...]
    copies = []
    for i in range(HALF_STEPS):
        state_step, adjoint_step = state_first + i, adjoint_first + i
        state = take_half(low_ref, high_ref, state_low, i)
        adjoint = take_half(high_ref, low_ref, state_low, i)
        raw, gf, from_start, _ = carried_rows(state, gt_ref, c_ref, cum_ref, state_step)
        back, xf, to_end, _ = scaled_rows(adjoint, xt_ref, b_ref, cum_ref, adjoint_step)
        gct, gbt, made = give_out(
            i, state_step, adjoint_step, state, adjoint, (raw, gf, from_start, back, xf, to_end),
            yt_ref, gxt_ref, y_hbm, gx_hbm, out_s, sems, gct, gbt,
        )
        copies += made
    gc_ref[...] = (low_gc_ref[...] + high_gc_ref[...] + gct.T).astype(BF16)
    gb_ref[...] = (low_gb_ref[...] + high_gb_ref[...] + gbt.T).astype(BF16)
    for made in copies:
        made.wait()


def shape_of(shape, dtype=F32):
    return jax.ShapeDtypeStruct(shape, dtype)


def call(kernel, name, out_shape, out_specs=None, cost=None, limit=VMEM_LIMIT, **more):
    if out_specs is not None:
        more["out_specs"] = out_specs
    return pl.pallas_call(
        kernel,
        out_shape=out_shape,
        compiler_params=pltpu.CompilerParams(vmem_limit_bytes=limit),
        cost_estimate=cost,
        name=name,
        **more,
    )


def cost(us):
    return pl.CostEstimate(flops=us * 500_000_000, bytes_accessed=us << 21, transcendentals=0)


def swap(low, high):
    count = lax.axis_size("seq")
    low_pairs = [(i, i ^ 1) for i in range(count)]
    high_pairs = [(i, ((i - 1 ^ 1) + 1) % count) for i in range(1, count)] + [(0, count - 1)]
    return lax.ppermute(low, "seq", low_pairs), lax.ppermute(high, "seq", high_pairs)


def shards(x_in, b_in, c_in, dt, a_log, skip, cotangent):
    x, b, c, g, steps = x_in[0], b_in[0], c_in[0], cotangent[0], dt[0]
    alog = a_log[None]
    feat = HEADS * SIZE
    vmem = pl.BlockSpec(memory_space=pltpu.VMEM)
    hbm = pl.BlockSpec(memory_space=pltpu.HBM)
    half = shape_of((HALF, SIZE, STATE))
    all_heads = shape_of((HEADS, SIZE, STATE))
    wide = shape_of((feat, GROUP), BF16)
    tall = shape_of((GROUP, feat), BF16)
    rows = shape_of((HEADS, GROUP))
    low, high, keep, gain, xt, gt, cum = call(
        states_kernel,
        "states",
        [half, half, all_heads, shape_of((HEADS, 1, STATE)), wide, wide, rows],
        in_specs=[hbm] * 6,
        scratch_shapes=[
            pltpu.VMEM((GRID, GROUP, WIDE), BF16),
            pltpu.VMEM((GRID, GROUP, WIDE), BF16),
            pltpu.VMEM((GROUP, STATE), BF16),
            pltpu.VMEM((GROUP, STATE), BF16),
            pltpu.VMEM((HEADS, GROUP), F32),
            pltpu.VMEM((1, HEADS), F32),
            pltpu.SemaphoreType.DMA((4 + 2 * GRID,)),
        ],
        limit=LARGE_LIMIT,
    )(x, g, b, c, steps, alog)
    low_in, high_in = swap(low, high)
    gains = lax.all_to_all(gain, "seq", 0, 0, tiled=True)
    yt, gxt, low_row, low_skiprow, low_gb, low_gc = inner(0, g, xt, gt, b, c, cum, skip)
    low_in, high_in, yt, gxt = lax.optimization_barrier((low_in, high_in, yt, gxt))
    joined = call(join_kernel, "join", all_heads)(keep, low_in, high_in, cum)
    parts = lax.all_to_all(joined, "seq", 0, 0, tiled=True)
    scanned = call(scan_kernel, "scan", all_heads)(parts, gains)
    mine = lax.all_to_all(scanned, "seq", 0, 0, tiled=True)
    low_out, high_out = call(pass_on_kernel, "pass_on", [half, half])(mine, low, high, cum)
    low_back, high_back = swap(low_out, high_out)
    yt, gxt, high_row, high_skiprow, high_gb, high_gc = inner(
        HALF_STEPS, g, xt, gt, b, c, cum, skip, (yt, gxt)
    )
    out_scratch = [
        pltpu.VMEM((2 * HALF_STEPS, GROUP, WIDE), BF16),
        pltpu.SemaphoreType.DMA((2 * HALF_STEPS,)),
    ]
    part = shape_of((STATE, GROUP))
    y, gx, own_row, gct, gbt = call(
        own_kernel,
        "own",
        [tall, tall, rows, part, part],
        [hbm, hbm, vmem, vmem, vmem],
        scratch_shapes=out_scratch,
        cost=cost(4),
    )(mine, yt, gxt, xt, gt, b, c, cum)
    everyone = lax.axis_size("dp") * lax.axis_size("seq")
    gdt, copies = call(
        sums_kernel,
        "sums",
        [rows, shape_of((everyone, 1, STATE))],
        scratch_shapes=[pltpu.VMEM((HEADS, GROUP), F32)],
    )(
        mine, low_back, high_back, xt, gt, b, c, cum, low_row, high_row, own_row,
        low_skiprow, high_skiprow, steps, alog,
    )
    sums = lax.all_to_all(copies, ("dp", "seq"), 0, 0, tiled=True)
    y, gx, gc, gb = call(
        other_kernel,
        "other",
        [tall, tall, shape_of((GROUP, STATE), BF16), shape_of((GROUP, STATE), BF16)],
        [hbm, hbm, vmem, vmem],
        in_specs=[vmem] * 15 + [hbm, hbm],
        input_output_aliases={15: 0, 16: 1},
        scratch_shapes=out_scratch,
        cost=cost(4),
        limit=LARGE_LIMIT,
    )(
        low_back, high_back, yt, gxt, xt, gt, b, c, cum, gct, gbt,
        low_gc, high_gc, low_gb, high_gb, y, gx,
    )
    galog, gskip = call(
        total_kernel, "total", [shape_of((1, HEADS)), shape_of((1, HEADS))]
    )(sums)
    return (
        y[None], gx[None], gb[None], gc[None], gdt[None],
        galog[0], gskip[0],
    )


def solution(mesh):
    placed = (
        P("dp", "seq", None),
        P("dp", "seq", None),
        P("dp", "seq", None),
        P("dp", None, "seq"),
        P(),
        P(),
        P("dp", "seq", None),
    )
    return jax.shard_map(
        shards,
        mesh=mesh,
        in_specs=placed,
        out_specs=(
            P("dp", "seq", None),
            P("dp", "seq", None),
            P("dp", "seq", None),
            P("dp", "seq", None),
            P("dp", None, "seq"),
            P(),
            P(),
        ),
        check_vma=False,
    )
```

```python
import jax
import jax.numpy as jnp
from jax import lax
from jax.experimental import pallas as pl
from jax.experimental.pallas import tpu as pltpu
from jax.sharding import PartitionSpec as P

GROUP = 256
HEADS = 32
SIZE = 64
STATE = 128
STEP = 8
WIDE = STEP * SIZE
GRID = HEADS // STEP
HALF = HEADS // 2
HALF_STEPS = GRID // 2
ROWS = SIZE + 1

F32 = jnp.float32
BF16 = jnp.bfloat16
EXACT = lax.Precision.HIGHEST
VMEM_LIMIT = 16 * 1024 * 1024
LARGE_LIMIT = 60 * 1024 * 1024


def dot(a, b, ca, cb, precision=None):
    return lax.dot_general(
        a, b, (((ca,), (cb,)), ((), ())), precision=precision, preferred_element_type=F32
    )


def iota(shape, dim):
    return lax.broadcasted_iota(jnp.int32, shape, dim)


def triangle():
    shape = (GROUP, GROUP)
    return jnp.where(iota(shape, 0) <= iota(shape, 1), 1.0, 0.0).astype(F32)


def column(row):
    shape = (HEADS, HEADS)
    eye = iota(shape, 0) == iota(shape, 1)
    return jnp.sum(jnp.where(eye, jnp.broadcast_to(row, shape), 0.0), axis=1, keepdims=True)


def as_row(col):
    shape = (HEADS, HEADS)
    eye = iota(shape, 0) == iota(shape, 1)
    return jnp.sum(jnp.where(eye, jnp.broadcast_to(col, shape), 0.0), axis=0, keepdims=True)


def spread(rows):
    return jnp.concatenate(
        [jnp.broadcast_to(rows[j : j + 1], (SIZE, GROUP)) for j in range(STEP)], axis=0
    )


def per_head(full):
    return jnp.concatenate(
        [
            jnp.sum(full[j * SIZE : (j + 1) * SIZE], axis=0, keepdims=True)
            for j in range(STEP)
        ],
        axis=0,
    )


def head_rows(step):
    return pl.ds(pl.multiple_of(step * STEP, STEP), STEP)


def keeps_adjoint(step):
    even = lax.rem(lax.axis_index("seq"), 2) == 0
    return even == (step < HALF_STEPS)


def unpaired(step):
    place = lax.axis_index("seq")
    edge = (place == 0) | (place == lax.axis_size("seq") - 1)
    return jnp.where(edge & (step >= HALF_STEPS), 0.0, 1.0).astype(F32)


def states_kernel(
    x_hbm, g_hbm, b_hbm, c_hbm, dt_hbm, alog_hbm,
    low_hbm, high_hbm, keep_hbm, xt_hbm, gt_hbm, cum_ref, rate_ref,
    x_s, g_s, b_s, c_s, dt_s, alog_s, send_s, keep_s, xt_s, gt_s, sems, out_sems,
):
    def copy(source, target, sem):
        made = pltpu.make_async_copy(source, target, sem)
        made.start()
        return made

    alog_copy = copy(alog_hbm, alog_s, sems.at[0])
    dt_copy = copy(dt_hbm, dt_s, sems.at[1])
    b_copy = copy(b_hbm, b_s, sems.at[2])
    c_copy = copy(c_hbm, c_s, sems.at[3])
    inputs = []
    for i in range(GRID):
        lanes = pl.ds(i * WIDE, WIDE)
        inputs.append(
            (
                copy(x_hbm.at[:, lanes], x_s.at[i], sems.at[4 + 2 * i]),
                copy(g_hbm.at[:, lanes], g_s.at[i], sems.at[5 + 2 * i]),
            )
        )
    alog_copy.wait()
    dt_copy.wait()
    rate = jnp.exp(column(alog_s[...]))
    rate_ref[...] = jnp.broadcast_to(rate, (HEADS, STATE))
    cum_all = dot(-rate * dt_s[...], triangle(), 1, 0, EXACT)
    cum_ref[...] = cum_all
    b_copy.wait()
    c_copy.wait()
    outputs = []
    for i in range(GRID):
        for made in inputs[i]:
            made.wait()
        cum = cum_all[i * STEP : (i + 1) * STEP]
        to_end = jnp.exp(cum[:, GROUP - 1 :] - cum)
        from_start = jnp.exp(cum)
        xt = x_s[i].T
        gt = g_s[i].T
        xt_s[i] = xt
        gt_s[i] = gt
        scaled = (xt.astype(F32) * spread(to_end)).astype(BF16)
        raised = (gt.astype(F32) * spread(from_start)).astype(BF16)
        state = dot(scaled, b_s[...], 1, 0)
        adjoint = dot(raised, c_s[...], 1, 0)
        first = keeps_adjoint(i)
        send = jnp.where(first, state, adjoint) * unpaired(i)
        keep = jnp.where(first, adjoint, state)
        send_s[i] = send.reshape(STEP, SIZE, STATE)
        keep_s[i] = keep.reshape(STEP, SIZE, STATE)
        send_hbm = low_hbm if i < HALF_STEPS else high_hbm
        rows = pl.ds(i * WIDE, WIDE)
        for k, (source, target) in enumerate(
            (
                (send_s, send_hbm.at[pl.ds(i % HALF_STEPS * STEP, STEP)]),
                (keep_s, keep_hbm.at[pl.ds(i * STEP, STEP)]),
                (xt_s, xt_hbm.at[rows]),
                (gt_s, gt_hbm.at[rows]),
            )
        ):
            outputs.append(copy(source.at[i], target, out_sems.at[4 * i + k]))
    for made in outputs:
        made.wait()


def head_part(h):
    return slice(h * ROWS, h * ROWS + SIZE), slice(h * ROWS + SIZE, (h + 1) * ROWS)


def join_kernel(keep_ref, low_ref, high_ref, cum_ref, out_ref):
    gain = jnp.exp(cum_ref[:, GROUP - 1 :])
    for h in range(HEADS):
        other = low_ref[h] if h < HALF else high_ref[h - HALF]
        matrix, decay = head_part(h)
        out_ref[matrix, :] = keep_ref[h] + gain[h : h + 1] * other
        out_ref[decay, :] = jnp.broadcast_to(gain[h : h + 1], (1, STATE))


def scan_kernel(part_ref, out_ref):
    count = out_ref.shape[0]
    low = lax.axis_index("seq") < HALF

    def matrix(k):
        return part_ref[head_part(k)[0], :]

    def gain(k):
        return part_ref[head_part(k)[1], :]

    def pair(first, second, carried, mine):
        return gain(first) * gain(second) * carried + matrix(mine)

    nothing = jnp.zeros((SIZE, STATE), F32)

    @pl.when(low)
    def _():
        state = nothing
        for k in range(0, count, 2):
            out_ref[k] = state
            state = pair(k, k + 1, state, k + 1)
        adjoint = nothing
        for k in reversed(range(0, count, 2)):
            out_ref[k + 1] = adjoint
            adjoint = pair(k, k + 1, adjoint, k)

    @pl.when(jnp.logical_not(low))
    def _():
        state = matrix(0)
        for k in range(1, count - 1, 2):
            out_ref[k] = state
            state = pair(k, k + 1, state, k + 1)
        out_ref[count - 1] = state
        adjoint = matrix(count - 1)
        for k in reversed(range(1, count - 1, 2)):
            out_ref[k + 1] = adjoint
            adjoint = pair(k, k + 1, adjoint, k)
        out_ref[0] = adjoint


def pass_on_kernel(mine_ref, low_ref, high_ref, cum_ref, out_low_ref, out_high_ref):
    gain = jnp.exp(cum_ref[:, GROUP - 1 :])
    low_gain = gain[:HALF] * unpaired(0)
    high_gain = gain[HALF:] * unpaired(GRID - 1)
    for h in range(HALF):
        out_low_ref[h] = low_ref[h] + low_gain[h : h + 1] * mine_ref[h]
        out_high_ref[h] = high_ref[h] + high_gain[h : h + 1] * mine_ref[HALF + h]


def inner_kernel(
    g_ref, xt_ref, gt_ref, b_ref, c_ref, cum_ref, skip_ref,
    y_ref, gx_ref, row_ref, skiprow_ref, gb_ref, gc_ref,
    cb_s, acc_s,
):
    step = pl.program_id(0)
    half = GROUP // 2

    @pl.when(step == 0)
    def _():
        cb_s[...] = dot(c_ref[...], b_ref[...], 1, 1)
        acc_s[...] = jnp.zeros_like(acc_s)

    square = (half, half)
    lower = iota(square, 0) >= iota(square, 1)
    nothing = jnp.zeros((SIZE, GROUP), BF16)
    cum = cum_ref[head_rows(step), :]
    cum_t = cum.T
    rows = []
    skips = []
    for j in range(STEP):
        low, high = j * SIZE, (j + 1) * SIZE
        early, late = cum[j : j + 1, :half], cum[j : j + 1, half:]
        start, end = cum_t[:half, j : j + 1], cum_t[half:, j : j + 1]
        e00 = jnp.where(lower, jnp.exp(start - early), 0.0)
        e10 = jnp.exp(end - early)
        e11 = jnp.where(lower, jnp.exp(end - late), 0.0)
        w00 = (cb_s[:half, :half] * e00).astype(BF16)
        w10 = (cb_s[half:, :half] * e10).astype(BF16)
        w11 = (cb_s[half:, half:] * e11).astype(BF16)
        weights = jnp.concatenate(
            [
                jnp.concatenate([w00, jnp.zeros(square, BF16)], axis=1),
                jnp.concatenate([w10, w11], axis=1),
            ],
            axis=0,
        )
        xt = xt_ref[low:high, :]
        gt = gt_ref[low:high, :]
        yt = dot(xt, weights, 1, 1)
        gxt = dot(gt, weights, 1, 0)
        pair = j // 2 * 2 * SIZE
        two = [xt, nothing] if j % 2 == 0 else [nothing, xt]
        gw = dot(g_ref[:, pair : pair + 2 * SIZE], jnp.concatenate(two, axis=0), 1, 0)
        acc_s[:half, :half] += gw[:half, :half] * e00
        acc_s[half:, :half] += gw[half:, :half] * e10
        acc_s[half:, half:] += gw[half:, half:] * e11
        xf = xt.astype(F32)
        gf = gt.astype(F32)
        rows.append(jnp.sum(gf * yt - xf * gxt, axis=0, keepdims=True))
        skips.append(jnp.sum(gf * xf, axis=0, keepdims=True))
        skip = skip_ref[step * STEP + j]
        y_ref[low:high, :] = (yt + skip * xf).astype(BF16)
        gx_ref[low:high, :] = (gxt + skip * gf).astype(BF16)
    row_ref[head_rows(step), :] = jnp.concatenate(rows, axis=0)
    skiprow_ref[head_rows(step), :] = jnp.concatenate(skips, axis=0)

    @pl.when(step == GRID - 1)
    def _():
        acc = acc_s[...].astype(BF16)
        gc_ref[...] = dot(acc, b_ref[...], 1, 0)
        gb_ref[...] = dot(acc, c_ref[...], 0, 0)


def inner(g, xt, gt, b, c, cum, skip):
    wide_t = pl.BlockSpec((WIDE, GROUP), lambda i: (i, 0))
    wide_n = pl.BlockSpec((GROUP, WIDE), lambda i: (0, i))
    narrow = pl.BlockSpec((GROUP, STATE), lambda i: (0, 0))
    heads = pl.BlockSpec((HEADS, GROUP), lambda i: (0, 0))
    wide = shape_of((HEADS * SIZE, GROUP), BF16)
    rows = shape_of((HEADS, GROUP))
    return call(
        inner_kernel,
        "inner",
        [wide, wide, rows, rows, shape_of((GROUP, STATE)), shape_of((GROUP, STATE))],
        [wide_t, wide_t, heads, heads, narrow, narrow],
        grid=(GRID,),
        in_specs=[
            wide_n, wide_t, wide_t, narrow, narrow, heads,
            pl.BlockSpec(memory_space=pltpu.SMEM),
        ],
        scratch_shapes=[pltpu.VMEM((GROUP, GROUP), F32), pltpu.VMEM((GROUP, GROUP), F32)],
        cost=cost(7),
        limit=LARGE_LIMIT,
    )(g, xt, gt, b, c, cum, skip)


def halves(own):
    even = lax.rem(lax.axis_index("seq"), 2) == 0
    state_low = even == own
    state = jnp.where(state_low, 0, HALF_STEPS)
    return state_low, state, HALF_STEPS - state


def feature_rows(step):
    return pl.ds(pl.multiple_of(step * WIDE, WIDE), WIDE)


def take(ref, step):
    full = ref[pl.ds(pl.multiple_of(step * STEP, STEP), STEP)]
    return full.reshape(WIDE, STATE).astype(BF16)


def take_half(low_ref, high_ref, low, i):
    part = pl.ds(i * STEP, STEP)
    return jnp.where(low, low_ref[part], high_ref[part]).reshape(WIDE, STATE).astype(BF16)


def carried_rows(state, gt_ref, c_ref, cum_ref, step):
    from_start = jnp.exp(cum_ref[head_rows(step), :])
    gf = gt_ref[feature_rows(step), :].astype(F32)
    raw = dot(state, c_ref[...], 1, 1)
    return raw, gf, from_start, per_head(gf * raw) * from_start


def scaled_rows(adjoint, xt_ref, b_ref, cum_ref, step):
    cum = cum_ref[head_rows(step), :]
    to_end = jnp.exp(cum[:, GROUP - 1 :] - cum)
    xf = xt_ref[feature_rows(step), :].astype(F32)
    raw = dot(adjoint, b_ref[...], 1, 1)
    from_x = per_head(xf * raw) * to_end
    final = iota((STEP, GROUP), 1) == GROUP - 1
    total = jnp.sum(from_x, axis=1, keepdims=True)
    return raw, xf, to_end, jnp.where(final, total, 0.0) - from_x


def give_out(
    i, state_step, adjoint_step, state, adjoint, raws,
    yt_ref, gxt_ref, y_hbm, gx_hbm, out_s, sems, gct, gbt,
):
    raw, gf, from_start, back, xf, to_end = raws
    start_w = spread(from_start)
    end_w = spread(to_end)
    y = yt_ref[feature_rows(state_step), :].astype(F32) + raw * start_w
    out_s[2 * i] = y.astype(BF16).T
    gx = gxt_ref[feature_rows(adjoint_step), :].astype(F32) + back * end_w
    out_s[2 * i + 1] = gx.astype(BF16).T
    copies = []
    for slot, step, target in ((2 * i, state_step, y_hbm), (2 * i + 1, adjoint_step, gx_hbm)):
        lanes = pl.ds(pl.multiple_of(step * WIDE, WIDE), WIDE)
        made = pltpu.make_async_copy(out_s.at[slot], target.at[:, lanes], sems.at[slot])
        made.start()
        copies.append(made)
    gct = gct + dot(state, (gf * start_w).astype(BF16), 0, 0)
    gbt = gbt + dot(adjoint, (xf * end_w).astype(BF16), 0, 0)
    return gct, gbt, copies


def own_kernel(
    mine_ref, yt_ref, gxt_ref, xt_ref, gt_ref, b_ref, c_ref, cum_ref,
    y_hbm, gx_hbm, row_ref, gct_ref, gbt_ref,
    out_s, sems,
):
    _, state_first, adjoint_first = halves(True)
    gct = jnp.zeros((STATE, GROUP), F32)
    gbt = jnp.zeros((STATE, GROUP), F32)
    copies = []
    for i in range(HALF_STEPS):
        state_step, adjoint_step = state_first + i, adjoint_first + i
        state = take(mine_ref, state_step)
        adjoint = take(mine_ref, adjoint_step)
        raw, gf, from_start, row = carried_rows(state, gt_ref, c_ref, cum_ref, state_step)
        row_ref[head_rows(state_step), :] = row
        back, xf, to_end, row = scaled_rows(adjoint, xt_ref, b_ref, cum_ref, adjoint_step)
        row_ref[head_rows(adjoint_step), :] = row
        gct, gbt, made = give_out(
            i, state_step, adjoint_step, state, adjoint, (raw, gf, from_start, back, xf, to_end),
            yt_ref, gxt_ref, y_hbm, gx_hbm, out_s, sems, gct, gbt,
        )
        copies += made
    gct_ref[...] = gct
    gbt_ref[...] = gbt
    for made in copies:
        made.wait()


def sums_kernel(
    mine_ref, low_ref, high_ref, xt_ref, gt_ref, b_ref, c_ref, cum_ref, inner_row_ref,
    own_row_ref, skiprow_ref, dt_ref, rate_ref,
    gdt_ref, sums_ref,
    row_s,
):
    state_low, state_first, adjoint_first = halves(False)
    for i in range(HALF_STEPS):
        state = take_half(low_ref, high_ref, state_low, i)
        adjoint = take_half(high_ref, low_ref, state_low, i)
        row_s[head_rows(state_first + i), :] = carried_rows(
            state, gt_ref, c_ref, cum_ref, state_first + i
        )[-1]
        row_s[head_rows(adjoint_first + i), :] = scaled_rows(
            adjoint, xt_ref, b_ref, cum_ref, adjoint_first + i
        )[-1]
    overlap = jnp.concatenate(
        [
            jnp.sum(mine_ref[:HALF] * low_ref[...], axis=1),
            jnp.sum(mine_ref[HALF:] * high_ref[...], axis=1),
        ],
        axis=0,
    )
    overlap = jnp.sum(overlap, axis=1, keepdims=True) * jnp.exp(cum_ref[:, GROUP - 1 :])
    final = iota((HEADS, GROUP), 1) == GROUP - 1
    row = inner_row_ref[...] + own_row_ref[...] + row_s[...] + jnp.where(final, overlap, 0.0)
    gdt = -rate_ref[:, :1] * dot(row, triangle(), 1, 1, EXACT)
    gdt_ref[...] = gdt
    alog = jnp.sum(gdt * dt_ref[...], axis=1, keepdims=True)
    skip = jnp.sum(skiprow_ref[...], axis=1, keepdims=True)
    sums = jnp.concatenate(
        [as_row(alog), as_row(skip), jnp.zeros((1, STATE - 2 * HEADS), F32)], axis=1
    )
    sums_ref[...] = jnp.broadcast_to(sums[None], sums_ref.shape)


def total_kernel(sums_ref, alog_ref, skip_ref):
    total = jnp.sum(sums_ref[...], axis=0)
    alog_ref[...] = total[:, :HEADS]
    skip_ref[...] = total[:, HEADS : 2 * HEADS]


def other_kernel(
    low_ref, high_ref, yt_ref, gxt_ref, xt_ref, gt_ref, b_ref, c_ref, cum_ref,
    gct_ref, gbt_ref, gci_ref, gbi_ref, y_in, gx_in,
    y_hbm, gx_hbm, gc_ref, gb_ref,
    out_s, sems,
):
    state_low, state_first, adjoint_first = halves(False)
    gct = gct_ref[...]
    gbt = gbt_ref[...]
    copies = []
    for i in range(HALF_STEPS):
        state_step, adjoint_step = state_first + i, adjoint_first + i
        state = take_half(low_ref, high_ref, state_low, i)
        adjoint = take_half(high_ref, low_ref, state_low, i)
        raw, gf, from_start, _ = carried_rows(state, gt_ref, c_ref, cum_ref, state_step)
        back, xf, to_end, _ = scaled_rows(adjoint, xt_ref, b_ref, cum_ref, adjoint_step)
        gct, gbt, made = give_out(
            i, state_step, adjoint_step, state, adjoint, (raw, gf, from_start, back, xf, to_end),
            yt_ref, gxt_ref, y_hbm, gx_hbm, out_s, sems, gct, gbt,
        )
        copies += made
    gc_ref[...] = (gci_ref[...] + gct.T).astype(BF16)
    gb_ref[...] = (gbi_ref[...] + gbt.T).astype(BF16)
    for made in copies:
        made.wait()


def shape_of(shape, dtype=F32):
    return jax.ShapeDtypeStruct(shape, dtype)


def call(kernel, name, out_shape, out_specs=None, cost=None, limit=VMEM_LIMIT, **more):
    if out_specs is not None:
        more["out_specs"] = out_specs
    return pl.pallas_call(
        kernel,
        out_shape=out_shape,
        compiler_params=pltpu.CompilerParams(vmem_limit_bytes=limit),
        cost_estimate=cost,
        name=name,
        **more,
    )


def cost(us):
    return pl.CostEstimate(flops=us * 500_000_000, bytes_accessed=us << 21, transcendentals=0)


def swap(low, high):
    count = lax.axis_size("seq")
    low_pairs = [(i, i ^ 1) for i in range(count)]
    high_pairs = [(i, ((i - 1 ^ 1) + 1) % count) for i in range(1, count)] + [(0, count - 1)]
    return lax.ppermute(low, "seq", low_pairs), lax.ppermute(high, "seq", high_pairs)


def shards(x_in, b_in, c_in, dt, a_log, skip, cotangent):
    x, b, c, g, steps = x_in[0], b_in[0], c_in[0], cotangent[0], dt[0]
    alog = a_log[None]
    feat = HEADS * SIZE
    vmem = pl.BlockSpec(memory_space=pltpu.VMEM)
    hbm = pl.BlockSpec(memory_space=pltpu.HBM)
    half = shape_of((HALF, SIZE, STATE))
    all_heads = shape_of((HEADS, SIZE, STATE))
    wide = shape_of((feat, GROUP), BF16)
    tall = shape_of((GROUP, feat), BF16)
    rows = shape_of((HEADS, GROUP))
    vector = shape_of((HEADS, STATE))
    low, high, keep, xt, gt, cum, rate = call(
        states_kernel,
        "states",
        [half, half, all_heads, wide, wide, rows, vector],
        [hbm] * 5 + [vmem] * 2,
        in_specs=[hbm] * 6,
        scratch_shapes=[
            pltpu.VMEM((GRID, GROUP, WIDE), BF16),
            pltpu.VMEM((GRID, GROUP, WIDE), BF16),
            pltpu.VMEM((GROUP, STATE), BF16),
            pltpu.VMEM((GROUP, STATE), BF16),
            pltpu.VMEM((HEADS, GROUP), F32),
            pltpu.VMEM((1, HEADS), F32),
            pltpu.VMEM((GRID, STEP, SIZE, STATE), F32),
            pltpu.VMEM((GRID, STEP, SIZE, STATE), F32),
            pltpu.VMEM((GRID, WIDE, GROUP), BF16),
            pltpu.VMEM((GRID, WIDE, GROUP), BF16),
            pltpu.SemaphoreType.DMA((4 + 2 * GRID,)),
            pltpu.SemaphoreType.DMA((4 * GRID,)),
        ],
        limit=LARGE_LIMIT,
    )(x, g, b, c, steps, alog)
    low_in, high_in = swap(low, high)
    yt, gxt, row, skiprow, gbi, gci = inner(g, xt, gt, b, c, cum, skip)
    low_in, high_in, yt, gxt = lax.optimization_barrier((low_in, high_in, yt, gxt))
    joined = call(join_kernel, "join", shape_of((HEADS * ROWS, STATE)))(keep, low_in, high_in, cum)
    parts = lax.all_to_all(joined.reshape(HEADS, ROWS, 1, STATE), "seq", 0, 0, tiled=True)
    scanned = call(scan_kernel, "scan", all_heads)(parts.reshape(HEADS * ROWS, STATE))
    mine = lax.all_to_all(scanned, "seq", 0, 0, tiled=True)
    low_out, high_out = call(pass_on_kernel, "pass_on", [half, half])(mine, low, high, cum)
    low_back, high_back = swap(low_out, high_out)
    out_scratch = [
        pltpu.VMEM((2 * HALF_STEPS, GROUP, WIDE), BF16),
        pltpu.SemaphoreType.DMA((2 * HALF_STEPS,)),
    ]
    part = shape_of((STATE, GROUP))
    y, gx, own_row, gct, gbt = call(
        own_kernel,
        "own",
        [tall, tall, rows, part, part],
        [hbm, hbm, vmem, vmem, vmem],
        scratch_shapes=out_scratch,
        cost=cost(4),
    )(mine, yt, gxt, xt, gt, b, c, cum)
    everyone = lax.axis_size("dp") * lax.axis_size("seq")
    gdt, copies = call(
        sums_kernel,
        "sums",
        [rows, shape_of((everyone, 1, STATE))],
        scratch_shapes=[pltpu.VMEM((HEADS, GROUP), F32)],
    )(
        mine, low_back, high_back, xt, gt, b, c, cum, row, own_row, skiprow, steps, rate,
    )
    sums = lax.all_to_all(copies, ("dp", "seq"), 0, 0, tiled=True)
    y, gx, gc, gb = call(
        other_kernel,
        "other",
        [tall, tall, shape_of((GROUP, STATE), BF16), shape_of((GROUP, STATE), BF16)],
        [hbm, hbm, vmem, vmem],
        in_specs=[vmem] * 13 + [hbm, hbm],
        input_output_aliases={13: 0, 14: 1},
        scratch_shapes=out_scratch,
        cost=cost(4),
        limit=LARGE_LIMIT,
    )(
        low_back, high_back, yt, gxt, xt, gt, b, c, cum, gct, gbt,
        gci, gbi, y, gx,
    )
    galog, gskip = call(
        total_kernel, "total", [shape_of((1, HEADS)), shape_of((1, HEADS))]
    )(sums)
    return (
        y[None], gx[None], gb[None], gc[None], gdt[None],
        galog[0], gskip[0],
    )


def solution(mesh):
    placed = (
        P("dp", "seq", None),
        P("dp", "seq", None),
        P("dp", "seq", None),
        P("dp", None, "seq"),
        P(),
        P(),
        P("dp", "seq", None),
    )
    return jax.shard_map(
        shards,
        mesh=mesh,
        in_specs=placed,
        out_specs=(
            P("dp", "seq", None),
            P("dp", "seq", None),
            P("dp", "seq", None),
            P("dp", "seq", None),
            P("dp", None, "seq"),
            P(),
            P(),
        ),
        check_vma=False,
    )
```

```python
import jax
import jax.numpy as jnp
from jax import lax
from jax.experimental import pallas as pl
from jax.experimental.pallas import tpu as pltpu
from jax.sharding import PartitionSpec as P

GROUP = 256
HEADS = 32
SIZE = 64
STATE = 128
STEP = 8
WIDE = STEP * SIZE
GRID = HEADS // STEP
HALF = HEADS // 2
HALF_STEPS = GRID // 2
ROWS = SIZE + 1

F32 = jnp.float32
BF16 = jnp.bfloat16
EXACT = lax.Precision.HIGHEST
VMEM_LIMIT = 16 * 1024 * 1024
LARGE_LIMIT = 60 * 1024 * 1024


def dot(a, b, ca, cb, precision=None):
    return lax.dot_general(
        a, b, (((ca,), (cb,)), ((), ())), precision=precision, preferred_element_type=F32
    )


def iota(shape, dim):
    return lax.broadcasted_iota(jnp.int32, shape, dim)


def triangle():
    shape = (GROUP, GROUP)
    return jnp.where(iota(shape, 0) <= iota(shape, 1), 1.0, 0.0).astype(F32)


def column(row):
    shape = (HEADS, HEADS)
    eye = iota(shape, 0) == iota(shape, 1)
    return jnp.sum(jnp.where(eye, jnp.broadcast_to(row, shape), 0.0), axis=1, keepdims=True)


def as_row(col):
    shape = (HEADS, HEADS)
    eye = iota(shape, 0) == iota(shape, 1)
    return jnp.sum(jnp.where(eye, jnp.broadcast_to(col, shape), 0.0), axis=0, keepdims=True)


def spread(rows):
    return jnp.concatenate(
        [jnp.broadcast_to(rows[j : j + 1], (SIZE, GROUP)) for j in range(STEP)], axis=0
    )


def per_head(full):
    return jnp.concatenate(
        [
            jnp.sum(full[j * SIZE : (j + 1) * SIZE], axis=0, keepdims=True)
            for j in range(STEP)
        ],
        axis=0,
    )


def head_rows(step):
    return pl.ds(pl.multiple_of(step * STEP, STEP), STEP)


def keeps_adjoint(step):
    even = lax.rem(lax.axis_index("seq"), 2) == 0
    return even == (step < HALF_STEPS)


def unpaired(step):
    place = lax.axis_index("seq")
    edge = (place == 0) | (place == lax.axis_size("seq") - 1)
    return jnp.where(edge & (step >= HALF_STEPS), 0.0, 1.0).astype(F32)


def start_copy(source, target, sem):
    made = pltpu.make_async_copy(source, target, sem)
    made.start()
    return made


def start_either(first, one, other, sem):
    @pl.when(first)
    def _():
        start_copy(*one, sem)

    @pl.when(jnp.logical_not(first))
    def _():
        start_copy(*other, sem)

    return pltpu.make_async_copy(*one, sem)


def fetch_chunks(x_hbm, g_hbm, in_s, sems, sending):
    chunks = []
    for i in range(GRID):
        is_state = keeps_adjoint(i) == sending
        lanes = pl.ds(i * WIDE, WIDE)
        target = in_s.at[i]
        made = start_either(
            is_state, (x_hbm.at[:, lanes], target), (g_hbm.at[:, lanes], target), sems.at[i]
        )
        chunks.append((is_state, made))
    return chunks


def chunk_matrix(i, is_state, cum_all, in_s, t_s, b_ref, c_ref):
    cum = cum_all[i * STEP : (i + 1) * STEP]
    weights = jnp.exp(jnp.where(is_state, cum[:, GROUP - 1 :] - cum, cum))
    turned = in_s[i].T
    t_s[i] = turned
    scaled = (turned.astype(F32) * spread(weights)).astype(BF16)
    matrix = dot(scaled, jnp.where(is_state, b_ref[...], c_ref[...]), 1, 0)
    return matrix.reshape(STEP, SIZE, STATE)


def send_kernel(
    x_hbm, g_hbm, b_hbm, c_hbm, dt_hbm, alog_hbm,
    low_hbm, high_hbm, xt_hbm, gt_hbm, cum_ref, rate_ref,
    in_s, b_s, c_s, dt_s, alog_s, send_s, t_s, sems, out_sems,
):
    alog_copy = start_copy(alog_hbm, alog_s, sems.at[GRID])
    dt_copy = start_copy(dt_hbm, dt_s, sems.at[GRID + 1])
    b_copy = start_copy(b_hbm, b_s, sems.at[GRID + 2])
    c_copy = start_copy(c_hbm, c_s, sems.at[GRID + 3])
    chunks = fetch_chunks(x_hbm, g_hbm, in_s, sems, True)
    alog_copy.wait()
    dt_copy.wait()
    rate = jnp.exp(column(alog_s[...]))
    rate_ref[...] = jnp.broadcast_to(rate, (HEADS, STATE))
    cum_all = dot(-rate * dt_s[...], triangle(), 1, 0, EXACT)
    cum_ref[...] = cum_all
    b_copy.wait()
    c_copy.wait()
    outputs = []
    for i, (is_state, made) in enumerate(chunks):
        made.wait()
        send_s[i] = chunk_matrix(i, is_state, cum_all, in_s, t_s, b_s, c_s) * unpaired(i)
        send_hbm = low_hbm if i < HALF_STEPS else high_hbm
        rows = pl.ds(i * WIDE, WIDE)
        outputs.append(
            start_copy(
                send_s.at[i], send_hbm.at[pl.ds(i % HALF_STEPS * STEP, STEP)], out_sems.at[2 * i]
            )
        )
        outputs.append(
            start_either(
                is_state, (t_s.at[i], xt_hbm.at[rows]), (t_s.at[i], gt_hbm.at[rows]),
                out_sems.at[2 * i + 1],
            )
        )
    for made in outputs:
        made.wait()


def keep_kernel(
    x_hbm, g_hbm, b_ref, c_ref, cum_ref, xt_in, gt_in,
    keep_hbm, xt_hbm, gt_hbm,
    in_s, keep_s, t_s, sems, out_sems,
):
    cum_all = cum_ref[...]
    outputs = []
    for i, (is_state, made) in enumerate(fetch_chunks(x_hbm, g_hbm, in_s, sems, False)):
        made.wait()
        keep_s[i] = chunk_matrix(i, is_state, cum_all, in_s, t_s, b_ref, c_ref)
        rows = pl.ds(i * WIDE, WIDE)
        outputs.append(
            start_copy(keep_s.at[i], keep_hbm.at[pl.ds(i * STEP, STEP)], out_sems.at[2 * i])
        )
        outputs.append(
            start_either(
                is_state, (t_s.at[i], xt_hbm.at[rows]), (t_s.at[i], gt_hbm.at[rows]),
                out_sems.at[2 * i + 1],
            )
        )
    for made in outputs:
        made.wait()


def head_part(h):
    return slice(h * ROWS, h * ROWS + SIZE), slice(h * ROWS + SIZE, (h + 1) * ROWS)


def join_kernel(keep_ref, low_ref, high_ref, cum_ref, out_ref):
    gain = jnp.exp(cum_ref[:, GROUP - 1 :])
    for h in range(HEADS):
        other = low_ref[h] if h < HALF else high_ref[h - HALF]
        matrix, decay = head_part(h)
        out_ref[matrix, :] = keep_ref[h] + gain[h : h + 1] * other
        out_ref[decay, :] = jnp.broadcast_to(gain[h : h + 1], (1, STATE))


def scan_kernel(part_ref, out_ref):
    count = out_ref.shape[0]
    low = lax.axis_index("seq") < HALF

    def matrix(k):
        return part_ref[head_part(k)[0], :]

    def gain(k):
        return part_ref[head_part(k)[1], :]

    def pair(first, second, carried, mine):
        return gain(first) * gain(second) * carried + matrix(mine)

    nothing = jnp.zeros((SIZE, STATE), F32)

    @pl.when(low)
    def _():
        state = nothing
        for k in range(0, count, 2):
            out_ref[k] = state
            state = pair(k, k + 1, state, k + 1)
        adjoint = nothing
        for k in reversed(range(0, count, 2)):
            out_ref[k + 1] = adjoint
            adjoint = pair(k, k + 1, adjoint, k)

    @pl.when(jnp.logical_not(low))
    def _():
        state = matrix(0)
        for k in range(1, count - 1, 2):
            out_ref[k] = state
            state = pair(k, k + 1, state, k + 1)
        out_ref[count - 1] = state
        adjoint = matrix(count - 1)
        for k in reversed(range(1, count - 1, 2)):
            out_ref[k + 1] = adjoint
            adjoint = pair(k, k + 1, adjoint, k)
        out_ref[0] = adjoint


def pass_on_kernel(mine_ref, low_ref, high_ref, cum_ref, out_low_ref, out_high_ref):
    gain = jnp.exp(cum_ref[:, GROUP - 1 :])
    low_gain = gain[:HALF] * unpaired(0)
    high_gain = gain[HALF:] * unpaired(GRID - 1)
    for h in range(HALF):
        out_low_ref[h] = low_ref[h] + low_gain[h : h + 1] * mine_ref[h]
        out_high_ref[h] = high_ref[h] + high_gain[h : h + 1] * mine_ref[HALF + h]


def inner_kernel(
    g_ref, xt_ref, gt_ref, b_ref, c_ref, cum_ref, skip_ref,
    y_ref, gx_ref, row_ref, skiprow_ref, gb_ref, gc_ref,
    cb_s, acc_s,
):
    step = pl.program_id(0)
    half = GROUP // 2

    @pl.when(step == 0)
    def _():
        cb_s[...] = dot(c_ref[...], b_ref[...], 1, 1)
        acc_s[...] = jnp.zeros_like(acc_s)

    square = (half, half)
    lower = iota(square, 0) >= iota(square, 1)
    nothing = jnp.zeros((SIZE, GROUP), BF16)
    cum = cum_ref[head_rows(step), :]
    cum_t = cum.T
    rows = []
    skips = []
    for j in range(STEP):
        low, high = j * SIZE, (j + 1) * SIZE
        early, late = cum[j : j + 1, :half], cum[j : j + 1, half:]
        start, end = cum_t[:half, j : j + 1], cum_t[half:, j : j + 1]
        e00 = jnp.where(lower, jnp.exp(start - early), 0.0)
        e10 = jnp.exp(end - early)
        e11 = jnp.where(lower, jnp.exp(end - late), 0.0)
        w00 = (cb_s[:half, :half] * e00).astype(BF16)
        w10 = (cb_s[half:, :half] * e10).astype(BF16)
        w11 = (cb_s[half:, half:] * e11).astype(BF16)
        weights = jnp.concatenate(
            [
                jnp.concatenate([w00, jnp.zeros(square, BF16)], axis=1),
                jnp.concatenate([w10, w11], axis=1),
            ],
            axis=0,
        )
        xt = xt_ref[low:high, :]
        gt = gt_ref[low:high, :]
        yt = dot(xt, weights, 1, 1)
        gxt = dot(gt, weights, 1, 0)
        pair = j // 2 * 2 * SIZE
        two = [xt, nothing] if j % 2 == 0 else [nothing, xt]
        gw = dot(g_ref[:, pair : pair + 2 * SIZE], jnp.concatenate(two, axis=0), 1, 0)
        acc_s[:half, :half] += gw[:half, :half] * e00
        acc_s[half:, :half] += gw[half:, :half] * e10
        acc_s[half:, half:] += gw[half:, half:] * e11
        xf = xt.astype(F32)
        gf = gt.astype(F32)
        rows.append(jnp.sum(gf * yt - xf * gxt, axis=0, keepdims=True))
        skips.append(jnp.sum(gf * xf, axis=0, keepdims=True))
        skip = skip_ref[step * STEP + j]
        y_ref[low:high, :] = (yt + skip * xf).astype(BF16)
        gx_ref[low:high, :] = (gxt + skip * gf).astype(BF16)
    row_ref[head_rows(step), :] = jnp.concatenate(rows, axis=0)
    skiprow_ref[head_rows(step), :] = jnp.concatenate(skips, axis=0)

    @pl.when(step == GRID - 1)
    def _():
        acc = acc_s[...].astype(BF16)
        gc_ref[...] = dot(acc, b_ref[...], 1, 0)
        gb_ref[...] = dot(acc, c_ref[...], 0, 0)


def inner(g, xt, gt, b, c, cum, skip):
    wide_t = pl.BlockSpec((WIDE, GROUP), lambda i: (i, 0))
    wide_n = pl.BlockSpec((GROUP, WIDE), lambda i: (0, i))
    narrow = pl.BlockSpec((GROUP, STATE), lambda i: (0, 0))
    heads = pl.BlockSpec((HEADS, GROUP), lambda i: (0, 0))
    wide = shape_of((HEADS * SIZE, GROUP), BF16)
    rows = shape_of((HEADS, GROUP))
    return call(
        inner_kernel,
        "inner",
        [wide, wide, rows, rows, shape_of((GROUP, STATE)), shape_of((GROUP, STATE))],
        [wide_t, wide_t, heads, heads, narrow, narrow],
        grid=(GRID,),
        in_specs=[
            wide_n, wide_t, wide_t, narrow, narrow, heads,
            pl.BlockSpec(memory_space=pltpu.SMEM),
        ],
        scratch_shapes=[pltpu.VMEM((GROUP, GROUP), F32), pltpu.VMEM((GROUP, GROUP), F32)],
        cost=cost(7),
        limit=LARGE_LIMIT,
    )(g, xt, gt, b, c, cum, skip)


def halves(own):
    even = lax.rem(lax.axis_index("seq"), 2) == 0
    state_low = even == own
    state = jnp.where(state_low, 0, HALF_STEPS)
    return state_low, state, HALF_STEPS - state


def feature_rows(step):
    return pl.ds(pl.multiple_of(step * WIDE, WIDE), WIDE)


def take(ref, step):
    full = ref[pl.ds(pl.multiple_of(step * STEP, STEP), STEP)]
    return full.reshape(WIDE, STATE).astype(BF16)


def take_half(low_ref, high_ref, low, i):
    part = pl.ds(i * STEP, STEP)
    return jnp.where(low, low_ref[part], high_ref[part]).reshape(WIDE, STATE).astype(BF16)


def carried_rows(state, gt_ref, c_ref, cum_ref, step):
    from_start = jnp.exp(cum_ref[head_rows(step), :])
    gf = gt_ref[feature_rows(step), :].astype(F32)
    raw = dot(state, c_ref[...], 1, 1)
    return raw, gf, from_start, per_head(gf * raw) * from_start


def scaled_rows(adjoint, xt_ref, b_ref, cum_ref, step):
    cum = cum_ref[head_rows(step), :]
    to_end = jnp.exp(cum[:, GROUP - 1 :] - cum)
    xf = xt_ref[feature_rows(step), :].astype(F32)
    raw = dot(adjoint, b_ref[...], 1, 1)
    from_x = per_head(xf * raw) * to_end
    final = iota((STEP, GROUP), 1) == GROUP - 1
    total = jnp.sum(from_x, axis=1, keepdims=True)
    return raw, xf, to_end, jnp.where(final, total, 0.0) - from_x


def give_out(
    i, state_step, adjoint_step, state, adjoint, raws,
    yt_ref, gxt_ref, y_hbm, gx_hbm, out_s, sems, gct, gbt,
):
    raw, gf, from_start, back, xf, to_end = raws
    start_w = spread(from_start)
    end_w = spread(to_end)
    y = yt_ref[feature_rows(state_step), :].astype(F32) + raw * start_w
    out_s[2 * i] = y.astype(BF16).T
    gx = gxt_ref[feature_rows(adjoint_step), :].astype(F32) + back * end_w
    out_s[2 * i + 1] = gx.astype(BF16).T
    copies = []
    for slot, step, target in ((2 * i, state_step, y_hbm), (2 * i + 1, adjoint_step, gx_hbm)):
        lanes = pl.ds(pl.multiple_of(step * WIDE, WIDE), WIDE)
        made = pltpu.make_async_copy(out_s.at[slot], target.at[:, lanes], sems.at[slot])
        made.start()
        copies.append(made)
    gct = gct + dot(state, (gf * start_w).astype(BF16), 0, 0)
    gbt = gbt + dot(adjoint, (xf * end_w).astype(BF16), 0, 0)
    return gct, gbt, copies


def partner_weights(mine_ref, xt_ref, gt_ref, b_ref, c_ref, cum_ref, out_ref):
    _, state_first, adjoint_first = halves(False)
    for i in range(HALF_STEPS):
        for step, data_ref, rhs_ref, is_state in (
            (state_first + i, gt_ref, c_ref, True),
            (adjoint_first + i, xt_ref, b_ref, False),
        ):
            cum = cum_ref[head_rows(step), :]
            last = cum[:, GROUP - 1 :]
            lag = cum if is_state else last - cum
            data = data_ref[feature_rows(step), :].astype(F32) * spread(lag * jnp.exp(lag))
            made = dot(data.astype(BF16), rhs_ref[...], 1, 0).reshape(STEP, SIZE, STATE)
            gain = last * jnp.exp(last)
            here = pl.multiple_of(step * STEP, STEP)
            for j in range(STEP):
                out_ref[here + j] = made[j] + gain[j : j + 1] * mine_ref[here + j]


def own_kernel(
    mine_ref, yt_ref, gxt_ref, xt_ref, gt_ref, b_ref, c_ref, cum_ref, inner_row_ref, skiprow_ref,
    y_hbm, gx_hbm, row_ref, gct_ref, gbt_ref, weights_ref, base_ref,
    out_s, sems,
):
    _, state_first, adjoint_first = halves(True)
    gct = jnp.zeros((STATE, GROUP), F32)
    gbt = jnp.zeros((STATE, GROUP), F32)
    copies = []
    for i in range(HALF_STEPS):
        state_step, adjoint_step = state_first + i, adjoint_first + i
        state = take(mine_ref, state_step)
        adjoint = take(mine_ref, adjoint_step)
        raw, gf, from_start, row = carried_rows(state, gt_ref, c_ref, cum_ref, state_step)
        row_ref[head_rows(state_step), :] = row
        back, xf, to_end, row = scaled_rows(adjoint, xt_ref, b_ref, cum_ref, adjoint_step)
        row_ref[head_rows(adjoint_step), :] = row
        gct, gbt, made = give_out(
            i, state_step, adjoint_step, state, adjoint, (raw, gf, from_start, back, xf, to_end),
            yt_ref, gxt_ref, y_hbm, gx_hbm, out_s, sems, gct, gbt,
        )
        copies += made
    gct_ref[...] = gct
    gbt_ref[...] = gbt
    partner_weights(mine_ref, xt_ref, gt_ref, b_ref, c_ref, cum_ref, weights_ref)
    alog = (inner_row_ref[...] + row_ref[...]) * cum_ref[...]
    alog = jnp.sum(alog, axis=1, keepdims=True)
    skip = jnp.sum(skiprow_ref[...], axis=1, keepdims=True)
    lane = iota((HEADS, STATE), 1)
    base_ref[...] = jnp.where(lane == 0, alog, jnp.where(lane == 1, skip, 0.0))
    for made in copies:
        made.wait()


def sums_kernel(weights_ref, low_ref, high_ref, base_ref, sums_ref):
    product = jnp.concatenate(
        [
            jnp.sum(weights_ref[:HALF] * low_ref[...], axis=1),
            jnp.sum(weights_ref[HALF:] * high_ref[...], axis=1),
        ],
        axis=0,
    )
    alog = base_ref[:, :1] + jnp.sum(product, axis=1, keepdims=True)
    skip = base_ref[:, 1:2]
    sums = jnp.concatenate(
        [as_row(alog), as_row(skip), jnp.zeros((1, STATE - 2 * HEADS), F32)], axis=1
    )
    sums_ref[...] = jnp.broadcast_to(sums[None], sums_ref.shape)


def total_kernel(sums_ref, alog_ref, skip_ref):
    total = jnp.sum(sums_ref[...], axis=0)
    alog_ref[...] = total[:, :HEADS]
    skip_ref[...] = total[:, HEADS : 2 * HEADS]


def other_kernel(
    low_ref, high_ref, yt_ref, gxt_ref, xt_ref, gt_ref, b_ref, c_ref, cum_ref,
    gct_ref, gbt_ref, gci_ref, gbi_ref, mine_ref, inner_row_ref, own_row_ref, rate_ref, y_in, gx_in,
    y_hbm, gx_hbm, gc_ref, gb_ref, gdt_ref,
    out_s, row_s, sems,
):
    state_low, state_first, adjoint_first = halves(False)
    gct = gct_ref[...]
    gbt = gbt_ref[...]
    copies = []
    for i in range(HALF_STEPS):
        state_step, adjoint_step = state_first + i, adjoint_first + i
        state = take_half(low_ref, high_ref, state_low, i)
        adjoint = take_half(high_ref, low_ref, state_low, i)
        raw, gf, from_start, row = carried_rows(state, gt_ref, c_ref, cum_ref, state_step)
        row_s[head_rows(state_step), :] = row
        back, xf, to_end, row = scaled_rows(adjoint, xt_ref, b_ref, cum_ref, adjoint_step)
        row_s[head_rows(adjoint_step), :] = row
        gct, gbt, made = give_out(
            i, state_step, adjoint_step, state, adjoint, (raw, gf, from_start, back, xf, to_end),
            yt_ref, gxt_ref, y_hbm, gx_hbm, out_s, sems, gct, gbt,
        )
        copies += made
    gc_ref[...] = (gci_ref[...] + gct.T).astype(BF16)
    gb_ref[...] = (gbi_ref[...] + gbt.T).astype(BF16)
    overlap = jnp.concatenate(
        [
            jnp.sum(mine_ref[:HALF] * low_ref[...], axis=1),
            jnp.sum(mine_ref[HALF:] * high_ref[...], axis=1),
        ],
        axis=0,
    )
    overlap = jnp.sum(overlap, axis=1, keepdims=True) * jnp.exp(cum_ref[:, GROUP - 1 :])
    final = iota((HEADS, GROUP), 1) == GROUP - 1
    row = inner_row_ref[...] + own_row_ref[...] + row_s[...] + jnp.where(final, overlap, 0.0)
    gdt_ref[...] = -rate_ref[:, :1] * dot(row, triangle(), 1, 1, EXACT)
    for made in copies:
        made.wait()


def shape_of(shape, dtype=F32):
    return jax.ShapeDtypeStruct(shape, dtype)


def call(kernel, name, out_shape, out_specs=None, cost=None, limit=VMEM_LIMIT, **more):
    if out_specs is not None:
        more["out_specs"] = out_specs
    return pl.pallas_call(
        kernel,
        out_shape=out_shape,
        compiler_params=pltpu.CompilerParams(vmem_limit_bytes=limit),
        cost_estimate=cost,
        name=name,
        **more,
    )


def cost(us):
    return pl.CostEstimate(flops=us * 500_000_000, bytes_accessed=us << 21, transcendentals=0)


def swap(low, high):
    count = lax.axis_size("seq")
    low_pairs = [(i, i ^ 1) for i in range(count)]
    high_pairs = [(i, ((i - 1 ^ 1) + 1) % count) for i in range(1, count)] + [(0, count - 1)]
    return lax.ppermute(low, "seq", low_pairs), lax.ppermute(high, "seq", high_pairs)


def shards(x_in, b_in, c_in, dt, a_log, skip, cotangent):
    x, b, c, g, steps = x_in[0], b_in[0], c_in[0], cotangent[0], dt[0]
    alog = a_log[None]
    feat = HEADS * SIZE
    vmem = pl.BlockSpec(memory_space=pltpu.VMEM)
    hbm = pl.BlockSpec(memory_space=pltpu.HBM)
    half = shape_of((HALF, SIZE, STATE))
    all_heads = shape_of((HEADS, SIZE, STATE))
    wide = shape_of((feat, GROUP), BF16)
    tall = shape_of((GROUP, feat), BF16)
    rows = shape_of((HEADS, GROUP))
    vector = shape_of((HEADS, STATE))
    chunk = pltpu.VMEM((GRID, GROUP, WIDE), BF16)
    turned = pltpu.VMEM((GRID, WIDE, GROUP), BF16)
    matrices = pltpu.VMEM((GRID, STEP, SIZE, STATE), F32)
    low, high, xt, gt, cum, rate = call(
        send_kernel,
        "send",
        [half, half, wide, wide, rows, vector],
        [hbm] * 4 + [vmem] * 2,
        in_specs=[hbm] * 6,
        scratch_shapes=[
            chunk,
            pltpu.VMEM((GROUP, STATE), BF16),
            pltpu.VMEM((GROUP, STATE), BF16),
            pltpu.VMEM((HEADS, GROUP), F32),
            pltpu.VMEM((1, HEADS), F32),
            matrices,
            turned,
            pltpu.SemaphoreType.DMA((GRID + 4,)),
            pltpu.SemaphoreType.DMA((2 * GRID,)),
        ],
        limit=LARGE_LIMIT,
    )(x, g, b, c, steps, alog)
    low_in, high_in = swap(low, high)
    keep, xt, gt = call(
        keep_kernel,
        "keep",
        [all_heads, wide, wide],
        [hbm] * 3,
        in_specs=[hbm, hbm, vmem, vmem, vmem, hbm, hbm],
        input_output_aliases={5: 1, 6: 2},
        scratch_shapes=[
            chunk,
            matrices,
            turned,
            pltpu.SemaphoreType.DMA((GRID,)),
            pltpu.SemaphoreType.DMA((2 * GRID,)),
        ],
        cost=cost(3),
        limit=LARGE_LIMIT,
    )(x, g, b, c, cum, xt, gt)
    yt, gxt, row, skiprow, gbi, gci = inner(g, xt, gt, b, c, cum, skip)
    low_in, high_in, yt, gxt = lax.optimization_barrier((low_in, high_in, yt, gxt))
    joined = call(join_kernel, "join", shape_of((HEADS * ROWS, STATE)))(keep, low_in, high_in, cum)
    parts = lax.all_to_all(joined.reshape(HEADS, ROWS, 1, STATE), "seq", 0, 0, tiled=True)
    scanned = call(scan_kernel, "scan", all_heads)(parts.reshape(HEADS * ROWS, STATE))
    mine = lax.all_to_all(scanned, "seq", 0, 0, tiled=True)
    low_out, high_out = call(pass_on_kernel, "pass_on", [half, half])(mine, low, high, cum)
    low_back, high_back = swap(low_out, high_out)
    out_scratch = pltpu.VMEM((2 * HALF_STEPS, GROUP, WIDE), BF16)
    part = shape_of((STATE, GROUP))
    y, gx, own_row, gct, gbt, weights, base = call(
        own_kernel,
        "own",
        [tall, tall, rows, part, part, all_heads, vector],
        [hbm, hbm] + [vmem] * 5,
        scratch_shapes=[out_scratch, pltpu.SemaphoreType.DMA((2 * HALF_STEPS,))],
        cost=cost(4),
    )(mine, yt, gxt, xt, gt, b, c, cum, row, skiprow)
    everyone = lax.axis_size("dp") * lax.axis_size("seq")
    copies = call(sums_kernel, "sums", shape_of((everyone, 1, STATE)))(
        weights, low_back, high_back, base
    )
    sums = lax.all_to_all(copies, ("dp", "seq"), 0, 0, tiled=True)
    y, gx, gc, gb, gdt = call(
        other_kernel,
        "other",
        [tall, tall, shape_of((GROUP, STATE), BF16), shape_of((GROUP, STATE), BF16), rows],
        [hbm, hbm, vmem, vmem, vmem],
        in_specs=[vmem] * 17 + [hbm, hbm],
        input_output_aliases={17: 0, 18: 1},
        scratch_shapes=[
            out_scratch,
            pltpu.VMEM((HEADS, GROUP), F32),
            pltpu.SemaphoreType.DMA((2 * HALF_STEPS,)),
        ],
        cost=cost(4),
        limit=LARGE_LIMIT,
    )(
        low_back, high_back, yt, gxt, xt, gt, b, c, cum, gct, gbt,
        gci, gbi, mine, row, own_row, rate, y, gx,
    )
    galog, gskip = call(
        total_kernel, "total", [shape_of((1, HEADS)), shape_of((1, HEADS))]
    )(sums)
    return (
        y[None], gx[None], gb[None], gc[None], gdt[None],
        galog[0], gskip[0],
    )


def solution(mesh):
    placed = (
        P("dp", "seq", None),
        P("dp", "seq", None),
        P("dp", "seq", None),
        P("dp", None, "seq"),
        P(),
        P(),
        P("dp", "seq", None),
    )
    return jax.shard_map(
        shards,
        mesh=mesh,
        in_specs=placed,
        out_specs=(
            P("dp", "seq", None),
            P("dp", "seq", None),
            P("dp", "seq", None),
            P("dp", "seq", None),
            P("dp", None, "seq"),
            P(),
            P(),
        ),
        check_vma=False,
    )
```

```python
import functools

import jax
import jax.numpy as jnp
from jax import lax
from jax.experimental import pallas as pl
from jax.experimental.pallas import tpu as pltpu
from jax.sharding import PartitionSpec as P

GROUP = 256
HEADS = 32
SIZE = 64
STATE = 128
STEP = 8
WIDE = STEP * SIZE
GRID = HEADS // STEP
HALF = HEADS // 2
HALF_STEPS = GRID // 2

F32 = jnp.float32
BF16 = jnp.bfloat16
EXACT = lax.Precision.HIGHEST
VMEM_LIMIT = 16 * 1024 * 1024
LARGE_LIMIT = 60 * 1024 * 1024


def dot(a, b, ca, cb, precision=None):
    return lax.dot_general(
        a, b, (((ca,), (cb,)), ((), ())), precision=precision, preferred_element_type=F32
    )


def iota(shape, dim):
    return lax.broadcasted_iota(jnp.int32, shape, dim)


def triangle():
    shape = (GROUP, GROUP)
    return jnp.where(iota(shape, 0) <= iota(shape, 1), 1.0, 0.0).astype(F32)


def column(row):
    shape = (HEADS, HEADS)
    eye = iota(shape, 0) == iota(shape, 1)
    return jnp.sum(jnp.where(eye, jnp.broadcast_to(row, shape), 0.0), axis=1, keepdims=True)


def as_row(col):
    shape = (HEADS, HEADS)
    eye = iota(shape, 0) == iota(shape, 1)
    return jnp.sum(jnp.where(eye, jnp.broadcast_to(col, shape), 0.0), axis=0, keepdims=True)


def spread(rows):
    return jnp.concatenate(
        [jnp.broadcast_to(rows[j : j + 1], (SIZE, GROUP)) for j in range(STEP)], axis=0
    )


def per_head(full):
    return jnp.concatenate(
        [
            jnp.sum(full[j * SIZE : (j + 1) * SIZE], axis=0, keepdims=True)
            for j in range(STEP)
        ],
        axis=0,
    )


def head_rows(step):
    return pl.ds(pl.multiple_of(step * STEP, STEP), STEP)


def keeps_adjoint(step):
    even = lax.rem(lax.axis_index("seq"), 2) == 0
    return even == (step < HALF_STEPS)


def unpaired(step):
    place = lax.axis_index("seq")
    edge = (place == 0) | (place == lax.axis_size("seq") - 1)
    return jnp.where(edge & (step >= HALF_STEPS), 0.0, 1.0).astype(F32)


def states_kernel(
    x_hbm, g_hbm, b_hbm, c_hbm, dt_hbm, alog_hbm,
    low_ref, high_ref, keep_ref, gain_ref, xt_ref, gt_ref, cum_ref,
    x_s, g_s, b_s, c_s, dt_s, alog_s, sems,
):
    def copy(source, target, slot):
        made = pltpu.make_async_copy(source, target, sems.at[slot])
        made.start()
        return made

    alog_copy = copy(alog_hbm, alog_s, 0)
    dt_copy = copy(dt_hbm, dt_s, 1)
    b_copy = copy(b_hbm, b_s, 2)
    c_copy = copy(c_hbm, c_s, 3)
    inputs = []
    for i in range(GRID):
        lanes = pl.ds(i * WIDE, WIDE)
        inputs.append(
            (
                copy(x_hbm.at[:, lanes], x_s.at[i], 4 + 2 * i),
                copy(g_hbm.at[:, lanes], g_s.at[i], 5 + 2 * i),
            )
        )
    alog_copy.wait()
    dt_copy.wait()
    rate = jnp.exp(column(alog_s[...]))
    cum_all = dot(-rate * dt_s[...], triangle(), 1, 0, EXACT)
    cum_ref[...] = cum_all
    b_copy.wait()
    c_copy.wait()
    for i in range(GRID):
        for made in inputs[i]:
            made.wait()
        cum = cum_all[i * STEP : (i + 1) * STEP]
        last = cum[:, GROUP - 1 :]
        to_end = jnp.exp(last - cum)
        from_start = jnp.exp(cum)
        gain = jnp.exp(last)
        xt = x_s[i].T
        gt = g_s[i].T
        rows = pl.ds(i * WIDE, WIDE)
        xt_ref[rows, :] = xt
        gt_ref[rows, :] = gt
        scaled = (xt.astype(F32) * spread(to_end)).astype(BF16)
        raised = (gt.astype(F32) * spread(from_start)).astype(BF16)
        state = dot(scaled, b_s[...], 1, 0)
        adjoint = dot(raised, c_s[...], 1, 0)
        first = keeps_adjoint(i)
        send = jnp.where(first, state, adjoint) * unpaired(i)
        keep = jnp.where(first, adjoint, state)
        send_ref = low_ref if i < HALF_STEPS else high_ref
        base = i % HALF_STEPS * STEP
        for j in range(STEP):
            part = slice(j * SIZE, (j + 1) * SIZE)
            send_ref[base + j] = send[part]
            keep_ref[i * STEP + j] = keep[part]
            gain_ref[i * STEP + j] = jnp.broadcast_to(gain[j : j + 1], (1, STATE))


def join_kernel(keep_ref, low_ref, high_ref, cum_ref, out_ref):
    gain = jnp.exp(cum_ref[:, GROUP - 1 :])
    for h in range(HEADS):
        other = low_ref[h] if h < HALF else high_ref[h - HALF]
        out_ref[h] = keep_ref[h] + gain[h : h + 1] * other


def scan_kernel(part_ref, gain_ref, out_ref):
    count = part_ref.shape[0]
    low = lax.axis_index("seq") < HALF

    def pair(first, second, carried, mine):
        return gain_ref[first] * gain_ref[second] * carried + part_ref[mine]

    nothing = jnp.zeros((SIZE, STATE), F32)

    @pl.when(low)
    def _():
        state = nothing
        for k in range(0, count, 2):
            out_ref[k] = state
            state = pair(k, k + 1, state, k + 1)
        adjoint = nothing
        for k in reversed(range(0, count, 2)):
            out_ref[k + 1] = adjoint
            adjoint = pair(k, k + 1, adjoint, k)

    @pl.when(jnp.logical_not(low))
    def _():
        state = part_ref[0]
        for k in range(1, count - 1, 2):
            out_ref[k] = state
            state = pair(k, k + 1, state, k + 1)
        out_ref[count - 1] = state
        adjoint = part_ref[count - 1]
        for k in reversed(range(1, count - 1, 2)):
            out_ref[k + 1] = adjoint
            adjoint = pair(k, k + 1, adjoint, k)
        out_ref[0] = adjoint


def pass_on_kernel(mine_ref, low_ref, high_ref, cum_ref, out_low_ref, out_high_ref):
    gain = jnp.exp(cum_ref[:, GROUP - 1 :])
    low_gain = gain[:HALF] * unpaired(0)
    high_gain = gain[HALF:] * unpaired(GRID - 1)
    for h in range(HALF):
        out_low_ref[h] = low_ref[h] + low_gain[h : h + 1] * mine_ref[h]
        out_high_ref[h] = high_ref[h] + high_gain[h : h + 1] * mine_ref[HALF + h]


def inner_kernel(offset, *refs):
    (g_ref, xt_ref, gt_ref, b_ref, c_ref, cum_ref, skip_ref), refs = refs[:7], refs[7:]
    (y_ref, gx_ref, row_ref, skiprow_ref, gb_ref, gc_ref, cb_s, acc_s) = refs[-8:]
    place = pl.program_id(0)
    step = place + offset
    half = GROUP // 2

    @pl.when(place == 0)
    def _():
        cb_s[...] = dot(c_ref[...], b_ref[...], 1, 1)
        acc_s[...] = jnp.zeros_like(acc_s)

    square = (half, half)
    lower = iota(square, 0) >= iota(square, 1)
    nothing = jnp.zeros((SIZE, GROUP), BF16)
    cum = cum_ref[head_rows(step), :]
    cum_t = cum.T
    rows = []
    skips = []
    for j in range(STEP):
        low, high = j * SIZE, (j + 1) * SIZE
        early, late = cum[j : j + 1, :half], cum[j : j + 1, half:]
        start, end = cum_t[:half, j : j + 1], cum_t[half:, j : j + 1]
        e00 = jnp.where(lower, jnp.exp(start - early), 0.0)
        e10 = jnp.exp(end - early)
        e11 = jnp.where(lower, jnp.exp(end - late), 0.0)
        w00 = (cb_s[:half, :half] * e00).astype(BF16)
        w10 = (cb_s[half:, :half] * e10).astype(BF16)
        w11 = (cb_s[half:, half:] * e11).astype(BF16)
        weights = jnp.concatenate(
            [
                jnp.concatenate([w00, jnp.zeros(square, BF16)], axis=1),
                jnp.concatenate([w10, w11], axis=1),
            ],
            axis=0,
        )
        xt = xt_ref[low:high, :]
        gt = gt_ref[low:high, :]
        yt = dot(xt, weights, 1, 1)
        gxt = dot(gt, weights, 1, 0)
        pair = j // 2 * 2 * SIZE
        two = [xt, nothing] if j % 2 == 0 else [nothing, xt]
        gw = dot(g_ref[:, pair : pair + 2 * SIZE], jnp.concatenate(two, axis=0), 1, 0)
        acc_s[:half, :half] += gw[:half, :half] * e00
        acc_s[half:, :half] += gw[half:, :half] * e10
        acc_s[half:, half:] += gw[half:, half:] * e11
        xf = xt.astype(F32)
        gf = gt.astype(F32)
        rows.append(jnp.sum(gf * yt - xf * gxt, axis=0, keepdims=True))
        skips.append(jnp.sum(gf * xf, axis=0, keepdims=True))
        skip = skip_ref[step * STEP + j]
        y_ref[low:high, :] = (yt + skip * xf).astype(BF16)
        gx_ref[low:high, :] = (gxt + skip * gf).astype(BF16)
    here = pl.ds(pl.multiple_of(place * STEP, STEP), STEP)
    row_ref[here, :] = jnp.concatenate(rows, axis=0)
    skiprow_ref[here, :] = jnp.concatenate(skips, axis=0)

    @pl.when(place == HALF_STEPS - 1)
    def _():
        acc = acc_s[...].astype(BF16)
        gc_ref[...] = dot(acc, b_ref[...], 1, 0)
        gb_ref[...] = dot(acc, c_ref[...], 0, 0)


def inner(offset, g, xt, gt, b, c, cum, skip, earlier=()):
    wide_t = pl.BlockSpec((WIDE, GROUP), lambda i: (i + offset, 0))
    wide_n = pl.BlockSpec((GROUP, WIDE), lambda i: (0, i + offset))
    kept = lambda *shape: pl.BlockSpec(shape, lambda i: (0,) * len(shape))
    narrow = kept(GROUP, STATE)
    wide = shape_of((HEADS * SIZE, GROUP), BF16)
    rows = shape_of((HALF, GROUP))
    return call(
        functools.partial(inner_kernel, offset),
        "inner",
        [wide, wide, rows, rows, shape_of((GROUP, STATE)), shape_of((GROUP, STATE))],
        [wide_t, wide_t, kept(HALF, GROUP), kept(HALF, GROUP), narrow, narrow],
        grid=(HALF_STEPS,),
        in_specs=[
            wide_n, wide_t, wide_t, narrow, narrow, kept(HEADS, GROUP),
            pl.BlockSpec(memory_space=pltpu.SMEM),
        ]
        + [pl.BlockSpec(memory_space=pltpu.HBM)] * len(earlier),
        input_output_aliases={7 + i: i for i in range(len(earlier))},
        scratch_shapes=[pltpu.VMEM((GROUP, GROUP), F32), pltpu.VMEM((GROUP, GROUP), F32)],
        cost=cost(4),
        limit=VMEM_LIMIT if earlier else LARGE_LIMIT,
    )(g, xt, gt, b, c, cum, skip, *earlier)


def halves(own):
    even = lax.rem(lax.axis_index("seq"), 2) == 0
    state_low = even == own
    state = jnp.where(state_low, 0, HALF_STEPS)
    return state_low, state, HALF_STEPS - state


def feature_rows(step):
    return pl.ds(pl.multiple_of(step * WIDE, WIDE), WIDE)


def take(ref, step):
    full = ref[pl.ds(pl.multiple_of(step * STEP, STEP), STEP)]
    return full.reshape(WIDE, STATE).astype(BF16)


def take_half(low_ref, high_ref, low, i):
    part = pl.ds(i * STEP, STEP)
    return jnp.where(low, low_ref[part], high_ref[part]).reshape(WIDE, STATE).astype(BF16)


def carried_rows(state, gt_ref, c_ref, cum_ref, step):
    from_start = jnp.exp(cum_ref[head_rows(step), :])
    gf = gt_ref[feature_rows(step), :].astype(F32)
    raw = dot(state, c_ref[...], 1, 1)
    return raw, gf, from_start, per_head(gf * raw) * from_start


def scaled_rows(adjoint, xt_ref, b_ref, cum_ref, step):
    cum = cum_ref[head_rows(step), :]
    to_end = jnp.exp(cum[:, GROUP - 1 :] - cum)
    xf = xt_ref[feature_rows(step), :].astype(F32)
    raw = dot(adjoint, b_ref[...], 1, 1)
    from_x = per_head(xf * raw) * to_end
    final = iota((STEP, GROUP), 1) == GROUP - 1
    total = jnp.sum(from_x, axis=1, keepdims=True)
    return raw, xf, to_end, jnp.where(final, total, 0.0) - from_x


def give_out(
    i, state_step, adjoint_step, state, adjoint, raws,
    yt_ref, gxt_ref, y_hbm, gx_hbm, out_s, sems, gct, gbt,
):
    raw, gf, from_start, back, xf, to_end = raws
    start_w = spread(from_start)
    end_w = spread(to_end)
    y = yt_ref[feature_rows(state_step), :].astype(F32) + raw * start_w
    out_s[2 * i] = y.astype(BF16).T
    gx = gxt_ref[feature_rows(adjoint_step), :].astype(F32) + back * end_w
    out_s[2 * i + 1] = gx.astype(BF16).T
    copies = []
    for slot, step, target in ((2 * i, state_step, y_hbm), (2 * i + 1, adjoint_step, gx_hbm)):
        lanes = pl.ds(pl.multiple_of(step * WIDE, WIDE), WIDE)
        made = pltpu.make_async_copy(out_s.at[slot], target.at[:, lanes], sems.at[slot])
        made.start()
        copies.append(made)
    gct = gct + dot(state, (gf * start_w).astype(BF16), 0, 0)
    gbt = gbt + dot(adjoint, (xf * end_w).astype(BF16), 0, 0)
    return gct, gbt, copies


def partner_weights(mine_ref, xt_ref, gt_ref, b_ref, c_ref, cum_ref, out_ref):
    _, state_first, adjoint_first = halves(False)
    for i in range(HALF_STEPS):
        for step, data_ref, rhs_ref, is_state in (
            (state_first + i, gt_ref, c_ref, True),
            (adjoint_first + i, xt_ref, b_ref, False),
        ):
            cum = cum_ref[head_rows(step), :]
            last = cum[:, GROUP - 1 :]
            lag = cum if is_state else last - cum
            data = data_ref[feature_rows(step), :].astype(F32) * spread(lag * jnp.exp(lag))
            made = dot(data.astype(BF16), rhs_ref[...], 1, 0).reshape(STEP, SIZE, STATE)
            gain = last * jnp.exp(last)
            here = pl.multiple_of(step * STEP, STEP)
            for j in range(STEP):
                out_ref[here + j] = made[j] + gain[j : j + 1] * mine_ref[here + j]


def own_kernel(
    mine_ref, yt_ref, gxt_ref, xt_ref, gt_ref, b_ref, c_ref, cum_ref,
    low_row_ref, high_row_ref, low_skiprow_ref, high_skiprow_ref,
    y_hbm, gx_hbm, row_ref, gct_ref, gbt_ref, weights_ref, base_ref,
    out_s, sems,
):
    _, state_first, adjoint_first = halves(True)
    gct = jnp.zeros((STATE, GROUP), F32)
    gbt = jnp.zeros((STATE, GROUP), F32)
    copies = []
    for i in range(HALF_STEPS):
        state_step, adjoint_step = state_first + i, adjoint_first + i
        state = take(mine_ref, state_step)
        adjoint = take(mine_ref, adjoint_step)
        raw, gf, from_start, row = carried_rows(state, gt_ref, c_ref, cum_ref, state_step)
        row_ref[head_rows(state_step), :] = row
        back, xf, to_end, row = scaled_rows(adjoint, xt_ref, b_ref, cum_ref, adjoint_step)
        row_ref[head_rows(adjoint_step), :] = row
        gct, gbt, made = give_out(
            i, state_step, adjoint_step, state, adjoint, (raw, gf, from_start, back, xf, to_end),
            yt_ref, gxt_ref, y_hbm, gx_hbm, out_s, sems, gct, gbt,
        )
        copies += made
    gct_ref[...] = gct
    gbt_ref[...] = gbt
    partner_weights(mine_ref, xt_ref, gt_ref, b_ref, c_ref, cum_ref, weights_ref)
    row = row_ref[...] + jnp.concatenate([low_row_ref[...], high_row_ref[...]], axis=0)
    alog = jnp.sum(row * cum_ref[...], axis=1, keepdims=True)
    skiprow = jnp.concatenate([low_skiprow_ref[...], high_skiprow_ref[...]], axis=0)
    skip = jnp.sum(skiprow, axis=1, keepdims=True)
    lane = iota((HEADS, STATE), 1)
    base_ref[...] = jnp.where(lane == 0, alog, jnp.where(lane == 1, skip, 0.0))
    row_ref[...] = row
    for made in copies:
        made.wait()


def sums_kernel(weights_ref, low_ref, high_ref, base_ref, sums_ref):
    product = jnp.concatenate(
        [
            jnp.sum(weights_ref[:HALF] * low_ref[...], axis=1),
            jnp.sum(weights_ref[HALF:] * high_ref[...], axis=1),
        ],
        axis=0,
    )
    alog = base_ref[:, :1] + jnp.sum(product, axis=1, keepdims=True)
    skip = base_ref[:, 1:2]
    sums = jnp.concatenate(
        [as_row(alog), as_row(skip), jnp.zeros((1, STATE - 2 * HEADS), F32)], axis=1
    )
    sums_ref[...] = jnp.broadcast_to(sums[None], sums_ref.shape)


def total_kernel(sums_ref, alog_ref, skip_ref):
    total = jnp.sum(sums_ref[...], axis=0)
    alog_ref[...] = total[:, :HEADS]
    skip_ref[...] = total[:, HEADS : 2 * HEADS]


def other_kernel(
    low_ref, high_ref, yt_ref, gxt_ref, xt_ref, gt_ref, b_ref, c_ref, cum_ref,
    gct_ref, gbt_ref, low_gc_ref, high_gc_ref, low_gb_ref, high_gb_ref,
    mine_ref, row_ref, alog_ref, y_in, gx_in,
    y_hbm, gx_hbm, gc_ref, gb_ref, gdt_ref,
    out_s, row_s, sems,
):
    state_low, state_first, adjoint_first = halves(False)
    gct = gct_ref[...]
    gbt = gbt_ref[...]
    copies = []
    for i in range(HALF_STEPS):
        state_step, adjoint_step = state_first + i, adjoint_first + i
        state = take_half(low_ref, high_ref, state_low, i)
        adjoint = take_half(high_ref, low_ref, state_low, i)
        raw, gf, from_start, row = carried_rows(state, gt_ref, c_ref, cum_ref, state_step)
        row_s[head_rows(state_step), :] = row
        back, xf, to_end, row = scaled_rows(adjoint, xt_ref, b_ref, cum_ref, adjoint_step)
        row_s[head_rows(adjoint_step), :] = row
        gct, gbt, made = give_out(
            i, state_step, adjoint_step, state, adjoint, (raw, gf, from_start, back, xf, to_end),
            yt_ref, gxt_ref, y_hbm, gx_hbm, out_s, sems, gct, gbt,
        )
        copies += made
    gc_ref[...] = (low_gc_ref[...] + high_gc_ref[...] + gct.T).astype(BF16)
    gb_ref[...] = (low_gb_ref[...] + high_gb_ref[...] + gbt.T).astype(BF16)
    overlap = jnp.concatenate(
        [
            jnp.sum(mine_ref[:HALF] * low_ref[...], axis=1),
            jnp.sum(mine_ref[HALF:] * high_ref[...], axis=1),
        ],
        axis=0,
    )
    overlap = jnp.sum(overlap, axis=1, keepdims=True) * jnp.exp(cum_ref[:, GROUP - 1 :])
    final = iota((HEADS, GROUP), 1) == GROUP - 1
    row = row_ref[...] + row_s[...] + jnp.where(final, overlap, 0.0)
    gdt_ref[...] = -jnp.exp(column(alog_ref[...])) * dot(row, triangle(), 1, 1, EXACT)
    for made in copies:
        made.wait()


def shape_of(shape, dtype=F32):
    return jax.ShapeDtypeStruct(shape, dtype)


def call(kernel, name, out_shape, out_specs=None, cost=None, limit=VMEM_LIMIT, **more):
    if out_specs is not None:
        more["out_specs"] = out_specs
    return pl.pallas_call(
        kernel,
        out_shape=out_shape,
        compiler_params=pltpu.CompilerParams(vmem_limit_bytes=limit),
        cost_estimate=cost,
        name=name,
        **more,
    )


def cost(us):
    return pl.CostEstimate(flops=us * 500_000_000, bytes_accessed=us << 21, transcendentals=0)


def swap(low, high):
    count = lax.axis_size("seq")
    low_pairs = [(i, i ^ 1) for i in range(count)]
    high_pairs = [(i, ((i - 1 ^ 1) + 1) % count) for i in range(1, count)] + [(0, count - 1)]
    return lax.ppermute(low, "seq", low_pairs), lax.ppermute(high, "seq", high_pairs)


def shards(x_in, b_in, c_in, dt, a_log, skip, cotangent):
    x, b, c, g, steps = x_in[0], b_in[0], c_in[0], cotangent[0], dt[0]
    alog = a_log[None]
    feat = HEADS * SIZE
    vmem = pl.BlockSpec(memory_space=pltpu.VMEM)
    hbm = pl.BlockSpec(memory_space=pltpu.HBM)
    half = shape_of((HALF, SIZE, STATE))
    all_heads = shape_of((HEADS, SIZE, STATE))
    wide = shape_of((feat, GROUP), BF16)
    tall = shape_of((GROUP, feat), BF16)
    rows = shape_of((HEADS, GROUP))
    low, high, keep, gain, xt, gt, cum = call(
        states_kernel,
        "states",
        [half, half, all_heads, shape_of((HEADS, 1, STATE)), wide, wide, rows],
        in_specs=[hbm] * 6,
        scratch_shapes=[
            pltpu.VMEM((GRID, GROUP, WIDE), BF16),
            pltpu.VMEM((GRID, GROUP, WIDE), BF16),
            pltpu.VMEM((GROUP, STATE), BF16),
            pltpu.VMEM((GROUP, STATE), BF16),
            pltpu.VMEM((HEADS, GROUP), F32),
            pltpu.VMEM((1, HEADS), F32),
            pltpu.SemaphoreType.DMA((4 + 2 * GRID,)),
        ],
        limit=LARGE_LIMIT,
    )(x, g, b, c, steps, alog)
    low_in, high_in = swap(low, high)
    gains = lax.all_to_all(gain, "seq", 0, 0, tiled=True)
    yt, gxt, low_row, low_skiprow, low_gb, low_gc = inner(0, g, xt, gt, b, c, cum, skip)
    low_in, high_in, yt, gxt = lax.optimization_barrier((low_in, high_in, yt, gxt))
    joined = call(join_kernel, "join", all_heads)(keep, low_in, high_in, cum)
    parts = lax.all_to_all(joined, "seq", 0, 0, tiled=True)
    scanned = call(scan_kernel, "scan", all_heads)(parts, gains)
    mine = lax.all_to_all(scanned, "seq", 0, 0, tiled=True)
    low_out, high_out = call(pass_on_kernel, "pass_on", [half, half])(mine, low, high, cum)
    low_back, high_back = swap(low_out, high_out)
    yt, gxt, high_row, high_skiprow, high_gb, high_gc = inner(
        HALF_STEPS, g, xt, gt, b, c, cum, skip, (yt, gxt)
    )
    out_scratch = [
        pltpu.VMEM((2 * HALF_STEPS, GROUP, WIDE), BF16),
        pltpu.SemaphoreType.DMA((2 * HALF_STEPS,)),
    ]
    part = shape_of((STATE, GROUP))
    y, gx, row, gct, gbt, weights, base = call(
        own_kernel,
        "own",
        [tall, tall, rows, part, part, all_heads, shape_of((HEADS, STATE))],
        [hbm, hbm] + [vmem] * 5,
        scratch_shapes=out_scratch,
        cost=cost(4),
    )(mine, yt, gxt, xt, gt, b, c, cum, low_row, high_row, low_skiprow, high_skiprow)
    everyone = lax.axis_size("dp") * lax.axis_size("seq")
    copies = call(sums_kernel, "sums", shape_of((everyone, 1, STATE)))(
        weights, low_back, high_back, base
    )
    sums = lax.all_to_all(copies, ("dp", "seq"), 0, 0, tiled=True)
    y, gx, gc, gb, gdt = call(
        other_kernel,
        "other",
        [tall, tall, shape_of((GROUP, STATE), BF16), shape_of((GROUP, STATE), BF16), rows],
        [hbm, hbm, vmem, vmem, vmem],
        in_specs=[vmem] * 18 + [hbm, hbm],
        input_output_aliases={18: 0, 19: 1},
        scratch_shapes=[out_scratch[0], pltpu.VMEM((HEADS, GROUP), F32), out_scratch[1]],
        cost=cost(4),
        limit=LARGE_LIMIT,
    )(
        low_back, high_back, yt, gxt, xt, gt, b, c, cum, gct, gbt,
        low_gc, high_gc, low_gb, high_gb, mine, row, alog, y, gx,
    )
    galog, gskip = call(
        total_kernel, "total", [shape_of((1, HEADS)), shape_of((1, HEADS))]
    )(sums)
    return (
        y[None], gx[None], gb[None], gc[None], gdt[None],
        galog[0], gskip[0],
    )


def solution(mesh):
    placed = (
        P("dp", "seq", None),
        P("dp", "seq", None),
        P("dp", "seq", None),
        P("dp", None, "seq"),
        P(),
        P(),
        P("dp", "seq", None),
    )
    return jax.shard_map(
        shards,
        mesh=mesh,
        in_specs=placed,
        out_specs=(
            P("dp", "seq", None),
            P("dp", "seq", None),
            P("dp", "seq", None),
            P("dp", "seq", None),
            P("dp", None, "seq"),
            P(),
            P(),
        ),
        check_vma=False,
    )
```

```python
import functools

import jax
import jax.numpy as jnp
from jax import lax
from jax.experimental import pallas as pl
from jax.experimental.pallas import tpu as pltpu
from jax.sharding import PartitionSpec as P

GROUP = 256
HEADS = 32
SIZE = 64
STATE = 128
STEP = 8
WIDE = STEP * SIZE
GRID = HEADS // STEP
HALF = HEADS // 2
HALF_STEPS = GRID // 2

F32 = jnp.float32
BF16 = jnp.bfloat16
EXACT = lax.Precision.HIGHEST
VMEM_LIMIT = 16 * 1024 * 1024
LARGE_LIMIT = 60 * 1024 * 1024


def dot(a, b, ca, cb, precision=None):
    return lax.dot_general(
        a, b, (((ca,), (cb,)), ((), ())), precision=precision, preferred_element_type=F32
    )


def iota(shape, dim):
    return lax.broadcasted_iota(jnp.int32, shape, dim)


def triangle():
    shape = (GROUP, GROUP)
    return jnp.where(iota(shape, 0) <= iota(shape, 1), 1.0, 0.0).astype(F32)


def column(row):
    shape = (HEADS, HEADS)
    eye = iota(shape, 0) == iota(shape, 1)
    return jnp.sum(jnp.where(eye, jnp.broadcast_to(row, shape), 0.0), axis=1, keepdims=True)


def as_row(col):
    shape = (HEADS, HEADS)
    eye = iota(shape, 0) == iota(shape, 1)
    return jnp.sum(jnp.where(eye, jnp.broadcast_to(col, shape), 0.0), axis=0, keepdims=True)


def spread(rows):
    return jnp.concatenate(
        [jnp.broadcast_to(rows[j : j + 1], (SIZE, GROUP)) for j in range(STEP)], axis=0
    )


def per_head(full):
    return jnp.concatenate(
        [
            jnp.sum(full[j * SIZE : (j + 1) * SIZE], axis=0, keepdims=True)
            for j in range(STEP)
        ],
        axis=0,
    )


def head_rows(step):
    return pl.ds(pl.multiple_of(step * STEP, STEP), STEP)


def keeps_adjoint(step):
    even = lax.rem(lax.axis_index("seq"), 2) == 0
    return even == (step < HALF_STEPS)


def unpaired(step):
    place = lax.axis_index("seq")
    edge = (place == 0) | (place == lax.axis_size("seq") - 1)
    return jnp.where(edge & (step >= HALF_STEPS), 0.0, 1.0).astype(F32)


def states_kernel(
    x_hbm, g_hbm, b_hbm, c_hbm, dt_hbm, alog_hbm,
    high_ref, low_ref, keep_ref, gain_ref, xt_ref, gt_ref, cum_ref,
    x_s, g_s, b_s, c_s, dt_s, alog_s, sems,
):
    def copy(source, target, slot):
        made = pltpu.make_async_copy(source, target, sems.at[slot])
        made.start()
        return made

    alog_copy = copy(alog_hbm, alog_s, 0)
    dt_copy = copy(dt_hbm, dt_s, 1)
    b_copy = copy(b_hbm, b_s, 2)
    c_copy = copy(c_hbm, c_s, 3)
    inputs = []
    for i in range(GRID):
        lanes = pl.ds(i * WIDE, WIDE)
        inputs.append(
            (
                copy(x_hbm.at[:, lanes], x_s.at[i], 4 + 2 * i),
                copy(g_hbm.at[:, lanes], g_s.at[i], 5 + 2 * i),
            )
        )
    alog_copy.wait()
    dt_copy.wait()
    rate = jnp.exp(column(alog_s[...]))
    cum_all = dot(-rate * dt_s[...], triangle(), 1, 0, EXACT)
    cum_ref[...] = cum_all
    b_copy.wait()
    c_copy.wait()
    for i in range(GRID):
        for made in inputs[i]:
            made.wait()
        cum = cum_all[i * STEP : (i + 1) * STEP]
        last = cum[:, GROUP - 1 :]
        to_end = jnp.exp(last - cum)
        from_start = jnp.exp(cum)
        gain = jnp.exp(last)
        xt = x_s[i].T
        gt = g_s[i].T
        rows = pl.ds(i * WIDE, WIDE)
        xt_ref[rows, :] = xt
        gt_ref[rows, :] = gt
        scaled = (xt.astype(F32) * spread(to_end)).astype(BF16)
        raised = (gt.astype(F32) * spread(from_start)).astype(BF16)
        state = dot(scaled, b_s[...], 1, 0)
        adjoint = dot(raised, c_s[...], 1, 0)
        first = keeps_adjoint(i)
        send = jnp.where(first, state, adjoint) * unpaired(i)
        keep = jnp.where(first, adjoint, state)
        send_ref = low_ref if i < HALF_STEPS else high_ref
        base = i % HALF_STEPS * STEP
        for j in range(STEP):
            part = slice(j * SIZE, (j + 1) * SIZE)
            send_ref[base + j] = send[part]
            keep_ref[i * STEP + j] = keep[part]
            gain_ref[i * STEP + j] = jnp.broadcast_to(gain[j : j + 1], (1, STATE))


def join_kernel(keep_ref, high_ref, low_ref, cum_ref, out_ref):
    gain = jnp.exp(cum_ref[:, GROUP - 1 :])
    for h in range(HEADS):
        other = low_ref[h] if h < HALF else high_ref[h - HALF]
        out_ref[h] = keep_ref[h] + gain[h : h + 1] * other


def scan_kernel(part_ref, gain_ref, out_ref):
    count = part_ref.shape[0]
    low = lax.axis_index("seq") < HALF

    def pair(first, second, carried, mine):
        return gain_ref[first] * gain_ref[second] * carried + part_ref[mine]

    nothing = jnp.zeros((SIZE, STATE), F32)

    @pl.when(low)
    def _():
        state = nothing
        for k in range(0, count, 2):
            out_ref[k] = state
            state = pair(k, k + 1, state, k + 1)
        adjoint = nothing
        for k in reversed(range(0, count, 2)):
            out_ref[k + 1] = adjoint
            adjoint = pair(k, k + 1, adjoint, k)

    @pl.when(jnp.logical_not(low))
    def _():
        state = part_ref[0]
        for k in range(1, count - 1, 2):
            out_ref[k] = state
            state = pair(k, k + 1, state, k + 1)
        out_ref[count - 1] = state
        adjoint = part_ref[count - 1]
        for k in reversed(range(1, count - 1, 2)):
            out_ref[k + 1] = adjoint
            adjoint = pair(k, k + 1, adjoint, k)
        out_ref[0] = adjoint


def pass_on_kernel(mine_ref, high_ref, low_ref, cum_ref, out_high_ref, out_low_ref):
    gain = jnp.exp(cum_ref[:, GROUP - 1 :])
    low_gain = gain[:HALF] * unpaired(0)
    high_gain = gain[HALF:] * unpaired(GRID - 1)
    for h in range(HALF):
        out_low_ref[h] = low_ref[h] + low_gain[h : h + 1] * mine_ref[h]
        out_high_ref[h] = high_ref[h] + high_gain[h : h + 1] * mine_ref[HALF + h]


def inner_kernel(offset, *refs):
    (g_ref, xt_ref, gt_ref, b_ref, c_ref, cum_ref, skip_ref), refs = refs[:7], refs[7:]
    (y_ref, gx_ref, row_ref, skiprow_ref, gb_ref, gc_ref, cb_s, acc_s) = refs[-8:]
    place = pl.program_id(0)
    step = place + offset
    half = GROUP // 2

    @pl.when(place == 0)
    def _():
        cb_s[...] = dot(c_ref[...], b_ref[...], 1, 1)
        acc_s[...] = jnp.zeros_like(acc_s)

    square = (half, half)
    lower = iota(square, 0) >= iota(square, 1)
    nothing = jnp.zeros((SIZE, GROUP), BF16)
    cum = cum_ref[head_rows(step), :]
    cum_t = cum.T
    rows = []
    skips = []
    for j in range(STEP):
        low, high = j * SIZE, (j + 1) * SIZE
        early, late = cum[j : j + 1, :half], cum[j : j + 1, half:]
        start, end = cum_t[:half, j : j + 1], cum_t[half:, j : j + 1]
        e00 = jnp.where(lower, jnp.exp(start - early), 0.0)
        e10 = jnp.exp(end - early)
        e11 = jnp.where(lower, jnp.exp(end - late), 0.0)
        w00 = (cb_s[:half, :half] * e00).astype(BF16)
        w10 = (cb_s[half:, :half] * e10).astype(BF16)
        w11 = (cb_s[half:, half:] * e11).astype(BF16)
        weights = jnp.concatenate(
            [
                jnp.concatenate([w00, jnp.zeros(square, BF16)], axis=1),
                jnp.concatenate([w10, w11], axis=1),
            ],
            axis=0,
        )
        xt = xt_ref[low:high, :]
        gt = gt_ref[low:high, :]
        yt = dot(xt, weights, 1, 1)
        gxt = dot(gt, weights, 1, 0)
        pair = j // 2 * 2 * SIZE
        two = [xt, nothing] if j % 2 == 0 else [nothing, xt]
        gw = dot(g_ref[:, pair : pair + 2 * SIZE], jnp.concatenate(two, axis=0), 1, 0)
        acc_s[:half, :half] += gw[:half, :half] * e00
        acc_s[half:, :half] += gw[half:, :half] * e10
        acc_s[half:, half:] += gw[half:, half:] * e11
        xf = xt.astype(F32)
        gf = gt.astype(F32)
        rows.append(jnp.sum(gf * yt - xf * gxt, axis=0, keepdims=True))
        skips.append(jnp.sum(gf * xf, axis=0, keepdims=True))
        skip = skip_ref[step * STEP + j]
        y_ref[low:high, :] = (yt + skip * xf).astype(BF16)
        gx_ref[low:high, :] = (gxt + skip * gf).astype(BF16)
    here = pl.ds(pl.multiple_of(place * STEP, STEP), STEP)
    row_ref[here, :] = jnp.concatenate(rows, axis=0)
    skiprow_ref[here, :] = jnp.concatenate(skips, axis=0)

    @pl.when(place == HALF_STEPS - 1)
    def _():
        acc = acc_s[...].astype(BF16)
        gc_ref[...] = dot(acc, b_ref[...], 1, 0)
        gb_ref[...] = dot(acc, c_ref[...], 0, 0)


def inner(offset, g, xt, gt, b, c, cum, skip, earlier=()):
    wide_t = pl.BlockSpec((WIDE, GROUP), lambda i: (i + offset, 0))
    wide_n = pl.BlockSpec((GROUP, WIDE), lambda i: (0, i + offset))
    kept = lambda *shape: pl.BlockSpec(shape, lambda i: (0,) * len(shape))
    narrow = kept(GROUP, STATE)
    wide = shape_of((HEADS * SIZE, GROUP), BF16)
    rows = shape_of((HALF, GROUP))
    return call(
        functools.partial(inner_kernel, offset),
        "inner",
        [wide, wide, rows, rows, shape_of((GROUP, STATE)), shape_of((GROUP, STATE))],
        [wide_t, wide_t, kept(HALF, GROUP), kept(HALF, GROUP), narrow, narrow],
        grid=(HALF_STEPS,),
        in_specs=[
            wide_n, wide_t, wide_t, narrow, narrow, kept(HEADS, GROUP),
            pl.BlockSpec(memory_space=pltpu.SMEM),
        ]
        + [pl.BlockSpec(memory_space=pltpu.HBM)] * len(earlier),
        input_output_aliases={7 + i: i for i in range(len(earlier))},
        scratch_shapes=[pltpu.VMEM((GROUP, GROUP), F32), pltpu.VMEM((GROUP, GROUP), F32)],
        cost=cost(4),
        limit=VMEM_LIMIT if earlier else LARGE_LIMIT,
    )(g, xt, gt, b, c, cum, skip, *earlier)


def halves(own):
    even = lax.rem(lax.axis_index("seq"), 2) == 0
    state_low = even == own
    state = jnp.where(state_low, 0, HALF_STEPS)
    return state_low, state, HALF_STEPS - state


def feature_rows(step):
    return pl.ds(pl.multiple_of(step * WIDE, WIDE), WIDE)


def take(ref, step):
    full = ref[pl.ds(pl.multiple_of(step * STEP, STEP), STEP)]
    return full.reshape(WIDE, STATE).astype(BF16)


def take_half(low_ref, high_ref, low, i):
    part = pl.ds(i * STEP, STEP)
    return jnp.where(low, low_ref[part], high_ref[part]).reshape(WIDE, STATE).astype(BF16)


def carried_rows(state, gt_ref, c_ref, cum_ref, step):
    from_start = jnp.exp(cum_ref[head_rows(step), :])
    gf = gt_ref[feature_rows(step), :].astype(F32)
    raw = dot(state, c_ref[...], 1, 1)
    return raw, gf, from_start, per_head(gf * raw) * from_start


def scaled_rows(adjoint, xt_ref, b_ref, cum_ref, step):
    cum = cum_ref[head_rows(step), :]
    to_end = jnp.exp(cum[:, GROUP - 1 :] - cum)
    xf = xt_ref[feature_rows(step), :].astype(F32)
    raw = dot(adjoint, b_ref[...], 1, 1)
    from_x = per_head(xf * raw) * to_end
    final = iota((STEP, GROUP), 1) == GROUP - 1
    total = jnp.sum(from_x, axis=1, keepdims=True)
    return raw, xf, to_end, jnp.where(final, total, 0.0) - from_x


def give_out(
    i, state_step, adjoint_step, state, adjoint, raws,
    yt_ref, gxt_ref, y_hbm, gx_hbm, out_s, sems, gct, gbt,
):
    raw, gf, from_start, back, xf, to_end = raws
    start_w = spread(from_start)
    end_w = spread(to_end)
    y = yt_ref[feature_rows(state_step), :].astype(F32) + raw * start_w
    out_s[2 * i] = y.astype(BF16).T
    gx = gxt_ref[feature_rows(adjoint_step), :].astype(F32) + back * end_w
    out_s[2 * i + 1] = gx.astype(BF16).T
    copies = []
    for slot, step, target in ((2 * i, state_step, y_hbm), (2 * i + 1, adjoint_step, gx_hbm)):
        lanes = pl.ds(pl.multiple_of(step * WIDE, WIDE), WIDE)
        made = pltpu.make_async_copy(out_s.at[slot], target.at[:, lanes], sems.at[slot])
        made.start()
        copies.append(made)
    gct = gct + dot(state, (gf * start_w).astype(BF16), 0, 0)
    gbt = gbt + dot(adjoint, (xf * end_w).astype(BF16), 0, 0)
    return gct, gbt, copies


def partner_weights(mine_ref, xt_ref, gt_ref, b_ref, c_ref, cum_ref, out_ref):
    _, state_first, adjoint_first = halves(False)
    for i in range(HALF_STEPS):
        for step, data_ref, rhs_ref, is_state in (
            (state_first + i, gt_ref, c_ref, True),
            (adjoint_first + i, xt_ref, b_ref, False),
        ):
            cum = cum_ref[head_rows(step), :]
            last = cum[:, GROUP - 1 :]
            lag = cum if is_state else last - cum
            data = data_ref[feature_rows(step), :].astype(F32) * spread(lag * jnp.exp(lag))
            made = dot(data.astype(BF16), rhs_ref[...], 1, 0).reshape(STEP, SIZE, STATE)
            gain = last * jnp.exp(last)
            here = pl.multiple_of(step * STEP, STEP)
            for j in range(STEP):
                out_ref[here + j] = made[j] + gain[j : j + 1] * mine_ref[here + j]


def own_kernel(
    mine_ref, yt_ref, gxt_ref, xt_ref, gt_ref, b_ref, c_ref, cum_ref,
    low_row_ref, high_row_ref, low_skiprow_ref, high_skiprow_ref,
    y_hbm, gx_hbm, row_ref, gct_ref, gbt_ref, weights_ref, base_ref,
    out_s, sems,
):
    _, state_first, adjoint_first = halves(True)
    gct = jnp.zeros((STATE, GROUP), F32)
    gbt = jnp.zeros((STATE, GROUP), F32)
    copies = []
    for i in range(HALF_STEPS):
        state_step, adjoint_step = state_first + i, adjoint_first + i
        state = take(mine_ref, state_step)
        adjoint = take(mine_ref, adjoint_step)
        raw, gf, from_start, row = carried_rows(state, gt_ref, c_ref, cum_ref, state_step)
        row_ref[head_rows(state_step), :] = row
        back, xf, to_end, row = scaled_rows(adjoint, xt_ref, b_ref, cum_ref, adjoint_step)
        row_ref[head_rows(adjoint_step), :] = row
        gct, gbt, made = give_out(
            i, state_step, adjoint_step, state, adjoint, (raw, gf, from_start, back, xf, to_end),
            yt_ref, gxt_ref, y_hbm, gx_hbm, out_s, sems, gct, gbt,
        )
        copies += made
    gct_ref[...] = gct
    gbt_ref[...] = gbt
    partner_weights(mine_ref, xt_ref, gt_ref, b_ref, c_ref, cum_ref, weights_ref)
    row = row_ref[...] + jnp.concatenate([low_row_ref[...], high_row_ref[...]], axis=0)
    alog = jnp.sum(row * cum_ref[...], axis=1, keepdims=True)
    skiprow = jnp.concatenate([low_skiprow_ref[...], high_skiprow_ref[...]], axis=0)
    skip = jnp.sum(skiprow, axis=1, keepdims=True)
    lane = iota((HEADS, STATE), 1)
    base_ref[...] = jnp.where(lane == 0, alog, jnp.where(lane == 1, skip, 0.0))
    row_ref[...] = row
    for made in copies:
        made.wait()


def sums_kernel(weights_ref, high_ref, low_ref, base_ref, sums_ref):
    product = jnp.concatenate(
        [
            jnp.sum(weights_ref[:HALF] * low_ref[...], axis=1),
            jnp.sum(weights_ref[HALF:] * high_ref[...], axis=1),
        ],
        axis=0,
    )
    alog = base_ref[:, :1] + jnp.sum(product, axis=1, keepdims=True)
    skip = base_ref[:, 1:2]
    sums = jnp.concatenate(
        [as_row(alog), as_row(skip), jnp.zeros((1, STATE - 2 * HEADS), F32)], axis=1
    )
    sums_ref[...] = jnp.broadcast_to(sums[None], sums_ref.shape)


def total_kernel(sums_ref, alog_ref, skip_ref):
    total = jnp.sum(sums_ref[...], axis=0)
    alog_ref[...] = total[:, :HEADS]
    skip_ref[...] = total[:, HEADS : 2 * HEADS]


def other_kernel(
    high_ref, low_ref, yt_ref, gxt_ref, xt_ref, gt_ref, b_ref, c_ref, cum_ref,
    gct_ref, gbt_ref, low_gc_ref, high_gc_ref, low_gb_ref, high_gb_ref,
    mine_ref, row_ref, alog_ref, y_in, gx_in,
    y_hbm, gx_hbm, gc_ref, gb_ref, gdt_ref,
    out_s, row_s, sems,
):
    state_low, state_first, adjoint_first = halves(False)
    gct = gct_ref[...]
    gbt = gbt_ref[...]
    copies = []
    for i in range(HALF_STEPS):
        state_step, adjoint_step = state_first + i, adjoint_first + i
        state = take_half(low_ref, high_ref, state_low, i)
        adjoint = take_half(high_ref, low_ref, state_low, i)
        raw, gf, from_start, row = carried_rows(state, gt_ref, c_ref, cum_ref, state_step)
        row_s[head_rows(state_step), :] = row
        back, xf, to_end, row = scaled_rows(adjoint, xt_ref, b_ref, cum_ref, adjoint_step)
        row_s[head_rows(adjoint_step), :] = row
        gct, gbt, made = give_out(
            i, state_step, adjoint_step, state, adjoint, (raw, gf, from_start, back, xf, to_end),
            yt_ref, gxt_ref, y_hbm, gx_hbm, out_s, sems, gct, gbt,
        )
        copies += made
    gc_ref[...] = (low_gc_ref[...] + high_gc_ref[...] + gct.T).astype(BF16)
    gb_ref[...] = (low_gb_ref[...] + high_gb_ref[...] + gbt.T).astype(BF16)
    overlap = jnp.concatenate(
        [
            jnp.sum(mine_ref[:HALF] * low_ref[...], axis=1),
            jnp.sum(mine_ref[HALF:] * high_ref[...], axis=1),
        ],
        axis=0,
    )
    overlap = jnp.sum(overlap, axis=1, keepdims=True) * jnp.exp(cum_ref[:, GROUP - 1 :])
    final = iota((HEADS, GROUP), 1) == GROUP - 1
    row = row_ref[...] + row_s[...] + jnp.where(final, overlap, 0.0)
    gdt_ref[...] = -jnp.exp(column(alog_ref[...])) * dot(row, triangle(), 1, 1, EXACT)
    for made in copies:
        made.wait()


def shape_of(shape, dtype=F32):
    return jax.ShapeDtypeStruct(shape, dtype)


def call(kernel, name, out_shape, out_specs=None, cost=None, limit=VMEM_LIMIT, **more):
    if out_specs is not None:
        more["out_specs"] = out_specs
    return pl.pallas_call(
        kernel,
        out_shape=out_shape,
        compiler_params=pltpu.CompilerParams(vmem_limit_bytes=limit),
        cost_estimate=cost,
        name=name,
        **more,
    )


def cost(us):
    return pl.CostEstimate(flops=us * 500_000_000, bytes_accessed=us << 21, transcendentals=0)


def swap(low, high):
    count = lax.axis_size("seq")
    low_pairs = [(i, i ^ 1) for i in range(count)]
    high_pairs = [(i, ((i - 1 ^ 1) + 1) % count) for i in range(1, count)] + [(0, count - 1)]
    high = lax.ppermute(high, "seq", high_pairs)
    return lax.ppermute(low, "seq", low_pairs), high


def shards(x_in, b_in, c_in, dt, a_log, skip, cotangent):
    x, b, c, g, steps = x_in[0], b_in[0], c_in[0], cotangent[0], dt[0]
    alog = a_log[None]
    feat = HEADS * SIZE
    vmem = pl.BlockSpec(memory_space=pltpu.VMEM)
    hbm = pl.BlockSpec(memory_space=pltpu.HBM)
    half = shape_of((HALF, SIZE, STATE))
    all_heads = shape_of((HEADS, SIZE, STATE))
    wide = shape_of((feat, GROUP), BF16)
    tall = shape_of((GROUP, feat), BF16)
    rows = shape_of((HEADS, GROUP))
    high, low, keep, gain, xt, gt, cum = call(
        states_kernel,
        "states",
        [half, half, all_heads, shape_of((HEADS, 1, STATE)), wide, wide, rows],
        in_specs=[hbm] * 6,
        scratch_shapes=[
            pltpu.VMEM((GRID, GROUP, WIDE), BF16),
            pltpu.VMEM((GRID, GROUP, WIDE), BF16),
            pltpu.VMEM((GROUP, STATE), BF16),
            pltpu.VMEM((GROUP, STATE), BF16),
            pltpu.VMEM((HEADS, GROUP), F32),
            pltpu.VMEM((1, HEADS), F32),
            pltpu.SemaphoreType.DMA((4 + 2 * GRID,)),
        ],
        limit=LARGE_LIMIT,
    )(x, g, b, c, steps, alog)
    low_in, high_in = swap(low, high)
    gains = lax.all_to_all(gain, "seq", 0, 0, tiled=True)
    yt, gxt, low_row, low_skiprow, low_gb, low_gc = inner(0, g, xt, gt, b, c, cum, skip)
    high_in, low_in, yt, gxt = lax.optimization_barrier((high_in, low_in, yt, gxt))
    joined = call(join_kernel, "join", all_heads)(keep, high_in, low_in, cum)
    parts = lax.all_to_all(joined, "seq", 0, 0, tiled=True)
    scanned = call(scan_kernel, "scan", all_heads)(parts, gains)
    mine = lax.all_to_all(scanned, "seq", 0, 0, tiled=True)
    high_out, low_out = call(pass_on_kernel, "pass_on", [half, half])(mine, high, low, cum)
    low_back, high_back = swap(low_out, high_out)
    yt, gxt, high_row, high_skiprow, high_gb, high_gc = inner(
        HALF_STEPS, g, xt, gt, b, c, cum, skip, (yt, gxt)
    )
    out_scratch = [
        pltpu.VMEM((2 * HALF_STEPS, GROUP, WIDE), BF16),
        pltpu.SemaphoreType.DMA((2 * HALF_STEPS,)),
    ]
    part = shape_of((STATE, GROUP))
    y, gx, row, gct, gbt, weights, base = call(
        own_kernel,
        "own",
        [tall, tall, rows, part, part, all_heads, shape_of((HEADS, STATE))],
        [hbm, hbm] + [vmem] * 5,
        scratch_shapes=out_scratch,
        cost=cost(4),
    )(mine, yt, gxt, xt, gt, b, c, cum, low_row, high_row, low_skiprow, high_skiprow)
    everyone = lax.axis_size("dp") * lax.axis_size("seq")
    copies = call(sums_kernel, "sums", shape_of((everyone, 1, STATE)))(
        weights, high_back, low_back, base
    )
    sums = lax.all_to_all(copies, ("dp", "seq"), 0, 0, tiled=True)
    y, gx, gc, gb, gdt = call(
        other_kernel,
        "other",
        [tall, tall, shape_of((GROUP, STATE), BF16), shape_of((GROUP, STATE), BF16), rows],
        [hbm, hbm, vmem, vmem, vmem],
        in_specs=[vmem] * 18 + [hbm, hbm],
        input_output_aliases={18: 0, 19: 1},
        scratch_shapes=[out_scratch[0], pltpu.VMEM((HEADS, GROUP), F32), out_scratch[1]],
        cost=cost(4),
        limit=LARGE_LIMIT,
    )(
        high_back, low_back, yt, gxt, xt, gt, b, c, cum, gct, gbt,
        low_gc, high_gc, low_gb, high_gb, mine, row, alog, y, gx,
    )
    galog, gskip = call(
        total_kernel, "total", [shape_of((1, HEADS)), shape_of((1, HEADS))]
    )(sums)
    return (
        y[None], gx[None], gb[None], gc[None], gdt[None],
        galog[0], gskip[0],
    )


def solution(mesh):
    placed = (
        P("dp", "seq", None),
        P("dp", "seq", None),
        P("dp", "seq", None),
        P("dp", None, "seq"),
        P(),
        P(),
        P("dp", "seq", None),
    )
    return jax.shard_map(
        shards,
        mesh=mesh,
        in_specs=placed,
        out_specs=(
            P("dp", "seq", None),
            P("dp", "seq", None),
            P("dp", "seq", None),
            P("dp", "seq", None),
            P("dp", None, "seq"),
            P(),
            P(),
        ),
        check_vma=False,
    )
```

```python
import functools

import jax
import jax.numpy as jnp
from jax import lax
from jax.experimental import pallas as pl
from jax.experimental.pallas import tpu as pltpu
from jax.sharding import PartitionSpec as P

GROUP = 256
HEADS = 32
SIZE = 64
STATE = 128
STEP = 8
WIDE = STEP * SIZE
GRID = HEADS // STEP
HALF = HEADS // 2
HALF_STEPS = GRID // 2

F32 = jnp.float32
BF16 = jnp.bfloat16
EXACT = lax.Precision.HIGHEST
VMEM_LIMIT = 16 * 1024 * 1024
LARGE_LIMIT = 60 * 1024 * 1024


def dot(a, b, ca, cb, precision=None):
    return lax.dot_general(
        a, b, (((ca,), (cb,)), ((), ())), precision=precision, preferred_element_type=F32
    )


def iota(shape, dim):
    return lax.broadcasted_iota(jnp.int32, shape, dim)


def triangle():
    shape = (GROUP, GROUP)
    return jnp.where(iota(shape, 0) <= iota(shape, 1), 1.0, 0.0).astype(F32)


def column(row):
    shape = (HEADS, HEADS)
    eye = iota(shape, 0) == iota(shape, 1)
    return jnp.sum(jnp.where(eye, jnp.broadcast_to(row, shape), 0.0), axis=1, keepdims=True)


def as_row(col):
    shape = (HEADS, HEADS)
    eye = iota(shape, 0) == iota(shape, 1)
    return jnp.sum(jnp.where(eye, jnp.broadcast_to(col, shape), 0.0), axis=0, keepdims=True)


def spread(rows):
    return jnp.concatenate(
        [jnp.broadcast_to(rows[j : j + 1], (SIZE, GROUP)) for j in range(STEP)], axis=0
    )


def per_head(full):
    return jnp.concatenate(
        [
            jnp.sum(full[j * SIZE : (j + 1) * SIZE], axis=0, keepdims=True)
            for j in range(STEP)
        ],
        axis=0,
    )


def head_rows(step):
    return pl.ds(pl.multiple_of(step * STEP, STEP), STEP)


def keeps_adjoint(step):
    even = lax.rem(lax.axis_index("seq"), 2) == 0
    return even == (step < HALF_STEPS)


def unpaired(step):
    place = lax.axis_index("seq")
    edge = (place == 0) | (place == lax.axis_size("seq") - 1)
    return jnp.where(edge & (step >= HALF_STEPS), 0.0, 1.0).astype(F32)


def states_kernel(
    x_hbm, g_hbm, b_hbm, c_hbm, dt_hbm, alog_hbm,
    high_ref, low_ref, keep_ref, gain_ref, xt_ref, gt_ref, cum_ref,
    x_s, g_s, b_s, c_s, dt_s, alog_s, sems,
):
    def copy(source, target, slot):
        made = pltpu.make_async_copy(source, target, sems.at[slot])
        made.start()
        return made

    alog_copy = copy(alog_hbm, alog_s, 0)
    dt_copy = copy(dt_hbm, dt_s, 1)
    b_copy = copy(b_hbm, b_s, 2)
    c_copy = copy(c_hbm, c_s, 3)
    inputs = []
    for i in range(GRID):
        lanes = pl.ds(i * WIDE, WIDE)
        inputs.append(
            (
                copy(x_hbm.at[:, lanes], x_s.at[i], 4 + 2 * i),
                copy(g_hbm.at[:, lanes], g_s.at[i], 5 + 2 * i),
            )
        )
    alog_copy.wait()
    dt_copy.wait()
    rate = jnp.exp(column(alog_s[...]))
    cum_all = dot(-rate * dt_s[...], triangle(), 1, 0, EXACT)
    cum_ref[...] = cum_all
    b_copy.wait()
    c_copy.wait()
    for i in range(GRID):
        for made in inputs[i]:
            made.wait()
        cum = cum_all[i * STEP : (i + 1) * STEP]
        last = cum[:, GROUP - 1 :]
        to_end = jnp.exp(last - cum)
        from_start = jnp.exp(cum)
        gain = jnp.exp(last)
        xt = x_s[i].T
        gt = g_s[i].T
        rows = pl.ds(i * WIDE, WIDE)
        xt_ref[rows, :] = xt
        gt_ref[rows, :] = gt
        scaled = (xt.astype(F32) * spread(to_end)).astype(BF16)
        raised = (gt.astype(F32) * spread(from_start)).astype(BF16)
        state = dot(scaled, b_s[...], 1, 0)
        adjoint = dot(raised, c_s[...], 1, 0)
        first = keeps_adjoint(i)
        send = jnp.where(first, state, adjoint) * unpaired(i)
        keep = jnp.where(first, adjoint, state)
        send_ref = low_ref if i < HALF_STEPS else high_ref
        base = i % HALF_STEPS * STEP
        for j in range(STEP):
            part = slice(j * SIZE, (j + 1) * SIZE)
            send_ref[base + j] = send[part]
            keep_ref[i * STEP + j] = keep[part]
            gain_ref[i * STEP + j] = jnp.broadcast_to(gain[j : j + 1], (1, STATE))


def join_kernel(keep_ref, high_ref, low_ref, cum_ref, out_ref):
    gain = jnp.exp(cum_ref[:, GROUP - 1 :])
    for h in range(HEADS):
        other = low_ref[h] if h < HALF else high_ref[h - HALF]
        out_ref[h] = keep_ref[h] + gain[h : h + 1] * other


def scan_kernel(part_ref, gain_ref, out_ref):
    count = part_ref.shape[0]
    low = lax.axis_index("seq") < HALF

    def pair(first, second, carried, mine):
        return gain_ref[first] * gain_ref[second] * carried + part_ref[mine]

    nothing = jnp.zeros((SIZE, STATE), F32)

    @pl.when(low)
    def _():
        state = nothing
        for k in range(0, count, 2):
            out_ref[k] = state
            state = pair(k, k + 1, state, k + 1)
        adjoint = nothing
        for k in reversed(range(0, count, 2)):
            out_ref[k + 1] = adjoint
            adjoint = pair(k, k + 1, adjoint, k)

    @pl.when(jnp.logical_not(low))
    def _():
        state = part_ref[0]
        for k in range(1, count - 1, 2):
            out_ref[k] = state
            state = pair(k, k + 1, state, k + 1)
        out_ref[count - 1] = state
        adjoint = part_ref[count - 1]
        for k in reversed(range(1, count - 1, 2)):
            out_ref[k + 1] = adjoint
            adjoint = pair(k, k + 1, adjoint, k)
        out_ref[0] = adjoint


def pass_on_kernel(mine_ref, high_ref, low_ref, cum_ref, out_high_ref, out_low_ref):
    gain = jnp.exp(cum_ref[:, GROUP - 1 :])
    low_gain = gain[:HALF] * unpaired(0)
    high_gain = gain[HALF:] * unpaired(GRID - 1)
    for h in range(HALF):
        out_low_ref[h] = low_ref[h] + low_gain[h : h + 1] * mine_ref[h]
        out_high_ref[h] = high_ref[h] + high_gain[h : h + 1] * mine_ref[HALF + h]


def inner_kernel(offset, *refs):
    (g_ref, xt_ref, gt_ref, b_ref, c_ref, cum_ref, skip_ref), refs = refs[:7], refs[7:]
    (y_ref, gx_ref, row_ref, skiprow_ref, gb_ref, gc_ref, cb_s, acc_s) = refs[-8:]
    place = pl.program_id(0)
    step = place + offset
    half = GROUP // 2

    @pl.when(place == 0)
    def _():
        cb_s[...] = dot(c_ref[...], b_ref[...], 1, 1)
        acc_s[...] = jnp.zeros_like(acc_s)

    square = (half, half)
    lower = iota(square, 0) >= iota(square, 1)
    nothing = jnp.zeros((SIZE, GROUP), BF16)
    cum = cum_ref[head_rows(step), :]
    cum_t = cum.T
    rows = []
    skips = []
    for j in range(STEP):
        low, high = j * SIZE, (j + 1) * SIZE
        early, late = cum[j : j + 1, :half], cum[j : j + 1, half:]
        start, end = cum_t[:half, j : j + 1], cum_t[half:, j : j + 1]
        e00 = jnp.where(lower, jnp.exp(start - early), 0.0)
        e10 = jnp.exp(end - early)
        e11 = jnp.where(lower, jnp.exp(end - late), 0.0)
        w00 = (cb_s[:half, :half] * e00).astype(BF16)
        w10 = (cb_s[half:, :half] * e10).astype(BF16)
        w11 = (cb_s[half:, half:] * e11).astype(BF16)
        weights = jnp.concatenate(
            [
                jnp.concatenate([w00, jnp.zeros(square, BF16)], axis=1),
                jnp.concatenate([w10, w11], axis=1),
            ],
            axis=0,
        )
        xt = xt_ref[low:high, :]
        gt = gt_ref[low:high, :]
        yt = dot(xt, weights, 1, 1)
        gxt = dot(gt, weights, 1, 0)
        pair = j // 2 * 2 * SIZE
        two = [xt, nothing] if j % 2 == 0 else [nothing, xt]
        gw = dot(g_ref[:, pair : pair + 2 * SIZE], jnp.concatenate(two, axis=0), 1, 0)
        acc_s[:half, :half] += gw[:half, :half] * e00
        acc_s[half:, :half] += gw[half:, :half] * e10
        acc_s[half:, half:] += gw[half:, half:] * e11
        xf = xt.astype(F32)
        gf = gt.astype(F32)
        rows.append(jnp.sum(gf * yt - xf * gxt, axis=0, keepdims=True))
        skips.append(jnp.sum(gf * xf, axis=0, keepdims=True))
        skip = skip_ref[step * STEP + j]
        y_ref[low:high, :] = (yt + skip * xf).astype(BF16)
        gx_ref[low:high, :] = (gxt + skip * gf).astype(BF16)
    here = pl.ds(pl.multiple_of(place * STEP, STEP), STEP)
    row_ref[here, :] = jnp.concatenate(rows, axis=0)
    skiprow_ref[here, :] = jnp.concatenate(skips, axis=0)

    @pl.when(place == HALF_STEPS - 1)
    def _():
        acc = acc_s[...].astype(BF16)
        gc_ref[...] = dot(acc, b_ref[...], 1, 0)
        gb_ref[...] = dot(acc, c_ref[...], 0, 0)


def inner(offset, g, xt, gt, b, c, cum, skip, earlier=()):
    wide_t = pl.BlockSpec((WIDE, GROUP), lambda i: (i + offset, 0))
    wide_n = pl.BlockSpec((GROUP, WIDE), lambda i: (0, i + offset))
    kept = lambda *shape: pl.BlockSpec(shape, lambda i: (0,) * len(shape))
    narrow = kept(GROUP, STATE)
    wide = shape_of((HEADS * SIZE, GROUP), BF16)
    rows = shape_of((HALF, GROUP))
    return call(
        functools.partial(inner_kernel, offset),
        "inner",
        [wide, wide, rows, rows, shape_of((GROUP, STATE)), shape_of((GROUP, STATE))],
        [wide_t, wide_t, kept(HALF, GROUP), kept(HALF, GROUP), narrow, narrow],
        grid=(HALF_STEPS,),
        in_specs=[
            wide_n, wide_t, wide_t, narrow, narrow, kept(HEADS, GROUP),
            pl.BlockSpec(memory_space=pltpu.SMEM),
        ]
        + [pl.BlockSpec(memory_space=pltpu.HBM)] * len(earlier),
        input_output_aliases={7 + i: i for i in range(len(earlier))},
        scratch_shapes=[pltpu.VMEM((GROUP, GROUP), F32), pltpu.VMEM((GROUP, GROUP), F32)],
        cost=cost(4),
        limit=VMEM_LIMIT if earlier else LARGE_LIMIT,
    )(g, xt, gt, b, c, cum, skip, *earlier)


def halves(own):
    even = lax.rem(lax.axis_index("seq"), 2) == 0
    state_low = even == own
    state = jnp.where(state_low, 0, HALF_STEPS)
    return state_low, state, HALF_STEPS - state


def feature_rows(step):
    return pl.ds(pl.multiple_of(step * WIDE, WIDE), WIDE)


def take(ref, step):
    full = ref[pl.ds(pl.multiple_of(step * STEP, STEP), STEP)]
    return full.reshape(WIDE, STATE).astype(BF16)


def take_half(low_ref, high_ref, low, i):
    part = pl.ds(i * STEP, STEP)
    return jnp.where(low, low_ref[part], high_ref[part]).reshape(WIDE, STATE).astype(BF16)


def carried_rows(state, gt_ref, c_ref, cum_ref, step):
    from_start = jnp.exp(cum_ref[head_rows(step), :])
    gf = gt_ref[feature_rows(step), :].astype(F32)
    raw = dot(state, c_ref[...], 1, 1)
    return raw, gf, from_start, per_head(gf * raw) * from_start


def scaled_rows(adjoint, xt_ref, b_ref, cum_ref, step):
    cum = cum_ref[head_rows(step), :]
    to_end = jnp.exp(cum[:, GROUP - 1 :] - cum)
    xf = xt_ref[feature_rows(step), :].astype(F32)
    raw = dot(adjoint, b_ref[...], 1, 1)
    from_x = per_head(xf * raw) * to_end
    final = iota((STEP, GROUP), 1) == GROUP - 1
    total = jnp.sum(from_x, axis=1, keepdims=True)
    return raw, xf, to_end, jnp.where(final, total, 0.0) - from_x


def give_out(
    i, state_step, adjoint_step, state, adjoint, raws,
    yt_ref, gxt_ref, y_hbm, gx_hbm, out_s, sems, gct, gbt,
):
    raw, gf, from_start, back, xf, to_end = raws
    start_w = spread(from_start)
    end_w = spread(to_end)
    y = yt_ref[feature_rows(state_step), :].astype(F32) + raw * start_w
    out_s[2 * i] = y.astype(BF16).T
    gx = gxt_ref[feature_rows(adjoint_step), :].astype(F32) + back * end_w
    out_s[2 * i + 1] = gx.astype(BF16).T
    copies = []
    for slot, step, target in ((2 * i, state_step, y_hbm), (2 * i + 1, adjoint_step, gx_hbm)):
        lanes = pl.ds(pl.multiple_of(step * WIDE, WIDE), WIDE)
        made = pltpu.make_async_copy(out_s.at[slot], target.at[:, lanes], sems.at[slot])
        made.start()
        copies.append(made)
    gct = gct + dot(state, (gf * start_w).astype(BF16), 0, 0)
    gbt = gbt + dot(adjoint, (xf * end_w).astype(BF16), 0, 0)
    return gct, gbt, copies


def partner_weights(mine_ref, xt_ref, gt_ref, b_ref, c_ref, cum_ref, out_ref):
    _, state_first, adjoint_first = halves(False)
    for i in range(HALF_STEPS):
        for step, data_ref, rhs_ref, is_state in (
            (state_first + i, gt_ref, c_ref, True),
            (adjoint_first + i, xt_ref, b_ref, False),
        ):
            cum = cum_ref[head_rows(step), :]
            last = cum[:, GROUP - 1 :]
            lag = cum if is_state else last - cum
            data = data_ref[feature_rows(step), :].astype(F32) * spread(lag * jnp.exp(lag))
            made = dot(data.astype(BF16), rhs_ref[...], 1, 0).reshape(STEP, SIZE, STATE)
            gain = last * jnp.exp(last)
            here = pl.multiple_of(step * STEP, STEP)
            for j in range(STEP):
                out_ref[here + j] = made[j] + gain[j : j + 1] * mine_ref[here + j]


def own_kernel(
    mine_ref, yt_ref, gxt_ref, xt_ref, gt_ref, b_ref, c_ref, cum_ref,
    low_row_ref, high_row_ref, low_skiprow_ref, high_skiprow_ref,
    y_hbm, gx_hbm, row_ref, gct_ref, gbt_ref, weights_ref, base_ref,
    out_s, sems,
):
    _, state_first, adjoint_first = halves(True)
    gct = jnp.zeros((STATE, GROUP), F32)
    gbt = jnp.zeros((STATE, GROUP), F32)
    copies = []
    for i in range(HALF_STEPS):
        state_step, adjoint_step = state_first + i, adjoint_first + i
        state = take(mine_ref, state_step)
        adjoint = take(mine_ref, adjoint_step)
        raw, gf, from_start, row = carried_rows(state, gt_ref, c_ref, cum_ref, state_step)
        row_ref[head_rows(state_step), :] = row
        back, xf, to_end, row = scaled_rows(adjoint, xt_ref, b_ref, cum_ref, adjoint_step)
        row_ref[head_rows(adjoint_step), :] = row
        gct, gbt, made = give_out(
            i, state_step, adjoint_step, state, adjoint, (raw, gf, from_start, back, xf, to_end),
            yt_ref, gxt_ref, y_hbm, gx_hbm, out_s, sems, gct, gbt,
        )
        copies += made
    gct_ref[...] = gct
    gbt_ref[...] = gbt
    partner_weights(mine_ref, xt_ref, gt_ref, b_ref, c_ref, cum_ref, weights_ref)
    row = row_ref[...] + jnp.concatenate([low_row_ref[...], high_row_ref[...]], axis=0)
    alog = jnp.sum(row * cum_ref[...], axis=1, keepdims=True)
    skiprow = jnp.concatenate([low_skiprow_ref[...], high_skiprow_ref[...]], axis=0)
    skip = jnp.sum(skiprow, axis=1, keepdims=True)
    lane = iota((HEADS, STATE), 1)
    base_ref[...] = jnp.where(lane == 0, alog, jnp.where(lane == 1, skip, 0.0))
    row_ref[...] = row
    for made in copies:
        made.wait()


def sums_kernel(weights_ref, high_ref, low_ref, base_ref, sums_ref):
    product = jnp.concatenate(
        [
            jnp.sum(weights_ref[:HALF] * low_ref[...], axis=1),
            jnp.sum(weights_ref[HALF:] * high_ref[...], axis=1),
        ],
        axis=0,
    )
    alog = base_ref[:, :1] + jnp.sum(product, axis=1, keepdims=True)
    skip = base_ref[:, 1:2]
    sums = jnp.concatenate(
        [as_row(alog), as_row(skip), jnp.zeros((1, STATE - 2 * HEADS), F32)], axis=1
    )
    sums_ref[...] = jnp.broadcast_to(sums[None], sums_ref.shape)


def total_kernel(sums_ref, alog_ref, skip_ref):
    total = jnp.sum(sums_ref[...], axis=0)
    alog_ref[...] = total[:, :HEADS]
    skip_ref[...] = total[:, HEADS : 2 * HEADS]


def other_kernel(
    high_ref, low_ref, yt_ref, gxt_ref, xt_ref, gt_ref, b_ref, c_ref, cum_ref,
    gct_ref, gbt_ref, low_gc_ref, high_gc_ref, low_gb_ref, high_gb_ref,
    mine_ref, row_ref, alog_ref, y_in, gx_in,
    y_hbm, gx_hbm, gc_ref, gb_ref, gdt_ref,
    out_s, row_s, sems,
):
    state_low, state_first, adjoint_first = halves(False)
    gct = gct_ref[...]
    gbt = gbt_ref[...]
    copies = []
    for i in range(HALF_STEPS):
        state_step, adjoint_step = state_first + i, adjoint_first + i
        state = take_half(low_ref, high_ref, state_low, i)
        adjoint = take_half(high_ref, low_ref, state_low, i)
        raw, gf, from_start, row = carried_rows(state, gt_ref, c_ref, cum_ref, state_step)
        row_s[head_rows(state_step), :] = row
        back, xf, to_end, row = scaled_rows(adjoint, xt_ref, b_ref, cum_ref, adjoint_step)
        row_s[head_rows(adjoint_step), :] = row
        gct, gbt, made = give_out(
            i, state_step, adjoint_step, state, adjoint, (raw, gf, from_start, back, xf, to_end),
            yt_ref, gxt_ref, y_hbm, gx_hbm, out_s, sems, gct, gbt,
        )
        copies += made
    gc_ref[...] = (low_gc_ref[...] + high_gc_ref[...] + gct.T).astype(BF16)
    gb_ref[...] = (low_gb_ref[...] + high_gb_ref[...] + gbt.T).astype(BF16)
    overlap = jnp.concatenate(
        [
            jnp.sum(mine_ref[:HALF] * low_ref[...], axis=1),
            jnp.sum(mine_ref[HALF:] * high_ref[...], axis=1),
        ],
        axis=0,
    )
    overlap = jnp.sum(overlap, axis=1, keepdims=True) * jnp.exp(cum_ref[:, GROUP - 1 :])
    final = iota((HEADS, GROUP), 1) == GROUP - 1
    row = row_ref[...] + row_s[...] + jnp.where(final, overlap, 0.0)
    gdt_ref[...] = -jnp.exp(column(alog_ref[...])) * dot(row, triangle(), 1, 1, EXACT)
    for made in copies:
        made.wait()


def shape_of(shape, dtype=F32):
    return jax.ShapeDtypeStruct(shape, dtype)


def call(kernel, name, out_shape, out_specs=None, cost=None, limit=VMEM_LIMIT, **more):
    if out_specs is not None:
        more["out_specs"] = out_specs
    return pl.pallas_call(
        kernel,
        out_shape=out_shape,
        compiler_params=pltpu.CompilerParams(vmem_limit_bytes=limit),
        cost_estimate=cost,
        name=name,
        **more,
    )


def cost(us):
    return pl.CostEstimate(flops=us * 500_000_000, bytes_accessed=us << 21, transcendentals=0)


def swap(low, high):
    count = lax.axis_size("seq")
    low_pairs = [(i, i ^ 1) for i in range(count)]
    high_pairs = [(i, ((i - 1 ^ 1) + 1) % count) for i in range(1, count)] + [(0, count - 1)]
    high = lax.ppermute(high, "seq", high_pairs)
    return lax.ppermute(low, "seq", low_pairs), high


def shards(x_in, b_in, c_in, dt, a_log, skip, cotangent):
    x, b, c, g, steps = x_in[0], b_in[0], c_in[0], cotangent[0], dt[0]
    alog = a_log[None]
    feat = HEADS * SIZE
    vmem = pl.BlockSpec(memory_space=pltpu.VMEM)
    hbm = pl.BlockSpec(memory_space=pltpu.HBM)
    half = shape_of((HALF, SIZE, STATE))
    all_heads = shape_of((HEADS, SIZE, STATE))
    wide = shape_of((feat, GROUP), BF16)
    tall = shape_of((GROUP, feat), BF16)
    rows = shape_of((HEADS, GROUP))
    high, low, keep, gain, xt, gt, cum = call(
        states_kernel,
        "states",
        [half, half, all_heads, shape_of((HEADS, 1, STATE)), wide, wide, rows],
        in_specs=[hbm] * 6,
        scratch_shapes=[
            pltpu.VMEM((GRID, GROUP, WIDE), BF16),
            pltpu.VMEM((GRID, GROUP, WIDE), BF16),
            pltpu.VMEM((GROUP, STATE), BF16),
            pltpu.VMEM((GROUP, STATE), BF16),
            pltpu.VMEM((HEADS, GROUP), F32),
            pltpu.VMEM((1, HEADS), F32),
            pltpu.SemaphoreType.DMA((4 + 2 * GRID,)),
        ],
        limit=LARGE_LIMIT,
    )(x, g, b, c, steps, alog)
    low_in, high_in = swap(low, high)
    gains = lax.all_to_all(gain, "seq", 0, 0, tiled=True)
    yt, gxt, low_row, low_skiprow, low_gb, low_gc = inner(0, g, xt, gt, b, c, cum, skip)
    high_in, low_in, yt, gxt = lax.optimization_barrier((high_in, low_in, yt, gxt))
    joined = call(join_kernel, "join", all_heads)(keep, high_in, low_in, cum)
    parts = lax.all_to_all(joined, "seq", 0, 0, tiled=True)
    scanned = call(scan_kernel, "scan", all_heads)(parts, gains)
    mine = lax.all_to_all(scanned, "seq", 0, 0, tiled=True)
    high_out, low_out = call(pass_on_kernel, "pass_on", [half, half])(mine, high, low, cum)
    low_back, high_back = swap(low_out, high_out)
    yt, gxt, high_row, high_skiprow, high_gb, high_gc = inner(
        HALF_STEPS, g, xt, gt, b, c, cum, skip, (yt, gxt)
    )
    out_scratch = [
        pltpu.VMEM((2 * HALF_STEPS, GROUP, WIDE), BF16),
        pltpu.SemaphoreType.DMA((2 * HALF_STEPS,)),
    ]
    part = shape_of((STATE, GROUP))
    y, gx, row, gct, gbt, weights, base = call(
        own_kernel,
        "own",
        [tall, tall, rows, part, part, all_heads, shape_of((HEADS, STATE))],
        [hbm, hbm] + [vmem] * 5,
        scratch_shapes=out_scratch,
        cost=cost(4),
    )(mine, yt, gxt, xt, gt, b, c, cum, low_row, high_row, low_skiprow, high_skiprow)
    everyone = lax.axis_size("dp") * lax.axis_size("seq")
    copies = call(sums_kernel, "sums", shape_of((everyone, 1, STATE)))(
        weights, high_back, low_back, base
    )
    sums = lax.all_to_all(copies, ("dp", "seq"), 0, 0, tiled=True)
    y, gx, gc, gb, gdt = call(
        other_kernel,
        "other",
        [tall, tall, shape_of((GROUP, STATE), BF16), shape_of((GROUP, STATE), BF16), rows],
        [hbm, hbm, vmem, vmem, vmem],
        in_specs=[vmem] * 18 + [hbm, hbm],
        input_output_aliases={18: 0, 19: 1},
        scratch_shapes=[out_scratch[0], pltpu.VMEM((HEADS, GROUP), F32), out_scratch[1]],
        cost=cost(4),
        limit=52 * 1024 * 1024,
    )(
        high_back, low_back, yt, gxt, xt, gt, b, c, cum, gct, gbt,
        low_gc, high_gc, low_gb, high_gb, mine, row, alog, y, gx,
    )
    galog, gskip = call(
        total_kernel, "total", [shape_of((1, HEADS)), shape_of((1, HEADS))]
    )(sums)
    return (
        y[None], gx[None], gb[None], gc[None], gdt[None],
        galog[0], gskip[0],
    )


def solution(mesh):
    placed = (
        P("dp", "seq", None),
        P("dp", "seq", None),
        P("dp", "seq", None),
        P("dp", None, "seq"),
        P(),
        P(),
        P("dp", "seq", None),
    )
    return jax.shard_map(
        shards,
        mesh=mesh,
        in_specs=placed,
        out_specs=(
            P("dp", "seq", None),
            P("dp", "seq", None),
            P("dp", "seq", None),
            P("dp", "seq", None),
            P("dp", None, "seq"),
            P(),
            P(),
        ),
        check_vma=False,
    )
```
